512 devices in a mesh: tm: 8 (over x, z_hi), space: 64 (over y, z_lo, core).
Axes of the slice: x: 4, y: 4, z: 16 (z_hi: 2, z_lo: 8; z = z_hi * 8 + z_lo), core: 2. Of those that a mesh axis runs over, the one named last changes fastest.
Arguments:
- initial: float32 [128, 64, 128], P('space'), may hold values from -1.5 to 1.5
- coeff: float32 [128, 64, 128], P('space'), may hold values from 0.5 to 4
- guess: float32 [8, 128, 64, 128], P('tm', 'space'), may hold values from -1.5 to 1.5
Outputs:
- fine_nodes: float32 [8, 2, 128, 64, 128], P('tm', None, 'space')
- coarse_end: float32 [8, 64, 32, 64], P('tm', 'space')
The draws below stay inside these ranges and needn't reach their ends.
All inputs are finite; a program needn't handle non-finite values.
Results may differ from the reference program's by a relative error of at most 0.0001.
Values sent between devices are 32-bit elements; how exact they have to be, the bound alone decides.
No kernel may reach another device: no remote copies, remote signals or barrier semaphores. Data moves between devices by JAX's collectives and lax.ppermute only.
A program may use at most 128 MiB of HBM per device.

```python
import math
import jax
import jax.numpy as jnp
from jax import lax

NY = 64
NZ = 128
ITERS = 2
SECTIONS = 8
NX = 128


def shard_levels(rng, dims, shards, low, high):
    factor_of, own = 1.0, jax.random.fold_in(rng, 6)
    for axis_at, blocks in shards:
        draws = jnp.exp(jax.random.uniform(jax.random.fold_in(own, axis_at), (blocks,), jnp.float32, low / len(shards), high / len(shards)))
        factor_of = factor_of * jnp.repeat(draws, dims[axis_at] // blocks).reshape([-1 if axis == axis_at else 1 for axis in range(len(dims))])
    return factor_of


def setup_inputs(seed: int = 0) -> dict:
    key_of = jax.random.split(jax.random.key(seed), 4)
    return {
        "initial": jnp.clip(jax.random.uniform(key_of[0], (NX, NY, NZ), jnp.float32, -1.5, 1.5) * shard_levels(key_of[0], (NX, NY, NZ), ((0, 64),), -0.4, 0.0), -1.5, 1.5),
        "coeff": jnp.clip(jnp.exp(math.log(4.0) - 2.0794415 * jax.random.uniform(key_of[1], (NX, NY, NZ), jnp.float32) ** shard_levels(key_of[1], (NX, NY, NZ), ((0, 64),), -0.2, 0.2)), 0.5, 4.0),
        "guess": jnp.clip(jax.random.uniform(key_of[2], (SECTIONS, NX, NY, NZ), jnp.float32, -1.5, 1.5) * shard_levels(key_of[2], (SECTIONS, NX, NY, NZ), ((0, 8), (1, 64)), -0.4, 0.0), -1.5, 1.5),
    }


STEP = 0.06
QUAD = ((0.0, 0.0, 0.0), (5.0 / 24.0, 1.0 / 3.0, -1.0 / 24.0), (1.0 / 6.0, 2.0 / 3.0, 1.0 / 6.0))


def laplace(field):
    total = -6.0 * field
    for axis_number in (-3, -2, -1):
        total = total + jnp.roll(field, 1, axis_number) + jnp.roll(field, -1, axis_number)
    return total


def fine_rhs(field, coeff):
    return laplace(field) + coeff * (field - field * field * field)


def coarse_rhs(field, coarse_coeff):
    return laplace(field) / 4.0 + coarse_coeff * (field - field * field * field)


def restrict(field):
    leading = field.shape[:-3]
    extent = field.shape[-3:]
    blocks = field.reshape(leading + (extent[0] // 2, 2, extent[1] // 2, 2, extent[2] // 2, 2))
    return blocks.mean(axis=(-5, -3, -1))


def prolong(field):
    leading = field.shape[:-3]
    extent = field.shape[-3:]
    grown = jnp.broadcast_to(field[..., :, None, :, None, :, None], leading + (extent[0], 2, extent[1], 2, extent[2], 2))
    return grown.reshape(leading + (2 * extent[0], 2 * extent[1], 2 * extent[2]))


def integral(first_rate, second_rate, third_rate, row):
    return STEP * (QUAD[row][0] * first_rate + QUAD[row][1] * second_rate + QUAD[row][2] * third_rate)


def reference(initial, coeff, guess):
    coarse_coeff = restrict(coeff)
    coarse_initial = restrict(initial)
    nodes = jnp.stack([guess, guess, guess], axis=1)
    finishes = None
    for iteration in range(ITERS):
        last_nodes = nodes[:, 2]
        rates = lax.map(lambda stacked: fine_rhs(stacked, coeff), nodes)
        coarse_nodes = restrict(nodes)
        coarse_rates = coarse_rhs(coarse_nodes, coarse_coeff)
        carries = []
        for row in (1, 2):
            fas_term = restrict(integral(rates[:, 0], rates[:, 1], rates[:, 2], row)) - integral(coarse_rates[:, 0], coarse_rates[:, 1], coarse_rates[:, 2], row)
            carries.append(STEP * (QUAD[row][1] * coarse_rates[:, 1] + QUAD[row][2] * coarse_rates[:, 2]) + fas_term)
        begin_coarse = coarse_initial
        starts, middles, finishes = [], [], []
        for section_index in range(SECTIONS):
            slopes = coarse_rhs(begin_coarse, coarse_coeff)
            middle = begin_coarse + STEP * QUAD[1][0] * slopes + carries[0][section_index]
            finish = begin_coarse + STEP * QUAD[2][0] * slopes + carries[1][section_index]
            starts.append(begin_coarse)
            middles.append(middle)
            finishes.append(finish)
            begin_coarse = finish
        coarse_new = jnp.stack([jnp.stack(starts), jnp.stack(middles), jnp.stack(finishes)], axis=1)
        nodes = nodes + prolong(coarse_new - coarse_nodes)
        start_fine = jnp.concatenate([initial[None], last_nodes[:-1]], axis=0)
        rates = lax.map(lambda stacked: fine_rhs(stacked, coeff), nodes)
        nodes = jnp.stack([start_fine,
                           start_fine + integral(rates[:, 0], rates[:, 1], rates[:, 2], 1),
                           start_fine + integral(rates[:, 0], rates[:, 1], rates[:, 2], 2)], axis=1)
    return nodes[:, 1:], jnp.stack(finishes)
```

```python
import jax
import jax.numpy as jnp
from jax import lax
from jax.experimental import pallas as pl
from jax.experimental.pallas import tpu as pltpu
from jax.sharding import Mesh, PartitionSpec as P

STEP = 0.06
QUAD = ((0.0, 0.0, 0.0), (5.0 / 24.0, 1.0 / 3.0, -1.0 / 24.0), (1.0 / 6.0, 2.0 / 3.0, 1.0 / 6.0))
ROWSUM = tuple(sum(row) for row in QUAD)
START = tuple(STEP * (row[1] * QUAD[1][0] + row[2] * QUAD[2][0]) for row in QUAD)
SECTIONS = 8
BLOCK = 8
F32 = jnp.float32

COEF, NEAR1, NEAR2 = 10, 11, 12
ITEMS = (
    ((0, 8), (1, 7), (COEF, 7), (2, 6), (3, 5), (4, 4), (5, 3), (6, 2), (NEAR1, 1), (NEAR2, 1)),
    ((0, 8), (1, 7), (2, 6), (3, 5), (4, 4), (5, 3), (6, 2), (NEAR1, 1), (NEAR2, 1)),
)


def count(items, distance):
    return sum(1 for _, reach in items if reach >= distance)


def slots(items):
    return max(count(items, d) + count(items, BLOCK - d) for d in range(1, BLOCK))


def turn(x, by, axis):
    return pltpu.roll(x, by % x.shape[axis], axis)


def around(x):
    return turn(x, 1, 0) + turn(x, -1, 0) + turn(x, 1, 1) + turn(x, -1, 1)


def cubic(u):
    return u - u * u * u


def dot(a, b):
    return jnp.dot(a, b, precision=lax.Precision.HIGHEST, preferred_element_type=F32)


def pair_lanes():
    z = lax.broadcasted_iota(jnp.int32, (128, 128), 0)
    c = lax.broadcasted_iota(jnp.int32, (128, 128), 1)
    return jnp.where((z >> 1) == (c & 63), 1.0, 0.0).astype(F32)


def spread_lanes():
    c = lax.broadcasted_iota(jnp.int32, (128, 128), 0)
    z = lax.broadcasted_iota(jnp.int32, (128, 128), 1)
    return jnp.where((z >> 1) == c, 1.0, 0.0).astype(F32)


def squash(planes, scratch):
    for i, plane in enumerate(planes):
        scratch[64 * i : 64 * i + 64, :] = plane
    both = scratch[pl.ds(0, 32 * len(planes), 2), :] + scratch[pl.ds(1, 32 * len(planes), 2), :]
    sums = dot(both, pair_lanes())
    return [sums[32 * i : 32 * i + 32] for i in range(len(planes))]


def spread(planes, scratch):
    wide = dot(jnp.concatenate(planes, axis=0), spread_lanes())
    scratch[pl.ds(0, 32 * len(planes), 2), :] = wide
    scratch[pl.ds(1, 32 * len(planes), 2), :] = wide
    return [scratch[64 * i : 64 * i + 64, :] for i in range(len(planes))]


def left(shape):
    return lax.broadcasted_iota(jnp.int32, shape, 1) < 64


def pack(x):
    return jnp.where(left((16, 128)), x[:16], x[16:])


def unpack(t):
    other = turn(t, 64, 1)
    here = left((16, 128))
    return jnp.concatenate([jnp.where(here, t, other), jnp.where(here, other, t)], axis=0)


def coarse_slope(below, centre, above, coef):
    return 0.25 * (around(centre) + below + above - 6.0 * centre) + coef * cubic(centre)


def mix(row, nodes):
    return QUAD[row][0] * nodes[0] + QUAD[row][1] * nodes[1] + QUAD[row][2] * nodes[2]


def own_part(sums, rates, scratch):
    planes = []
    for m in (0, 1):
        total = None
        for x in (0, 1):
            part = around(sums[m][x]) - 6.0 * sums[m][x] + sums[m][1 - x] + rates[m][x]
            total = part if total is None else total + part
        planes.append(total)
    return squash(planes, scratch)


def first_kernel(initial, coeff, guess, up, down, keep, scratch):
    u = [guess[0], guess[1]]
    c = [coeff[0], coeff[1]]
    rate = [c[x] * cubic(u[x]) for x in (0, 1)]
    total = None
    for x in (0, 1):
        part = around(u[x]) - 6.0 * u[x] + u[1 - x] + rate[x]
        total = part if total is None else total + part
    own, value, coef, start = squash([total, u[0] + u[1], c[0] + c[1], initial[0] + initial[1]], scratch)
    value, coef, start = 0.125 * value, 0.125 * coef, 0.125 * start
    for out, plane in ((up, u[1]), (down, u[0])):
        out[0:64, :] = plane
        out[64:80, :] = pack(value)
        out[80:96, :] = pack(start)
    keep[0] = own
    keep[1] = value
    keep[2] = coef
    keep[3] = start


def hand_over(spot, own, values, value0, value0_sides, coef, start, start_slope, out, gathered):
    slope = coarse_slope(value0_sides[0], value0, value0_sides[1], coef)
    k = [(STEP / 8.0) * own[m] - (STEP * QUAD[m + 1][0]) * slope for m in (0, 1)]
    first = (jnp.full((32, 128), spot[0], jnp.int32) == 0)
    out[0:16, :] = pack(k[1] + jnp.where(first, start + STEP * QUAD[2][0] * start_slope, 0.0))
    for m in (0, 1):
        near = QUAD[m + 1][1] * k[0] + QUAD[m + 1][2] * k[1] - values[m]
        near = near + jnp.where(first, ROWSUM[m + 1] * start + START[m + 1] * start_slope, 0.0)
        out[16 * (m + 1) : 16 * (m + 2), :] = pack(near)
    gathered[0] = k[0]
    gathered[1] = k[1]


def complete_first(spot, below, above, kept, out, keep, scratch):
    own, value, coef, start = (kept[i] for i in range(4))
    low, high = squash([below[0:64, :], above[0:64, :]], scratch)
    whole = own + low + high
    sides = [unpack(below[64:80, :]), unpack(above[64:80, :])]
    start_sides = [unpack(below[80:96, :]), unpack(above[80:96, :])]
    start_slope = coarse_slope(start_sides[0], start, start_sides[1], coef)
    hand_over(
        spot, [ROWSUM[1] * whole, ROWSUM[2] * whole], [ROWSUM[1] * value, ROWSUM[2] * value],
        value, sides, coef, start, start_slope, out, keep,
    )
    out[48:64, :] = pack(coef)
    keep[2] = start
    keep[3] = start_slope
    keep[4] = start_sides[0]
    keep[5] = start_sides[1]


def complete_second(spot, below, above, kept, started, kept_first, out, keep, scratch):
    low1, low2, high1, high2 = squash(
        [below[0:64, :], below[64:128, :], above[0:64, :], above[64:128, :]], scratch
    )
    own = [kept[0] + low1 + high1, kept[1] + low2 + high2]
    values = [mix(m, [kept[2], kept[3], kept[4]]) for m in (1, 2)]
    sides = [unpack(below[128:144, :]), unpack(above[128:144, :])]
    hand_over(spot, own, values, kept[2], sides, kept_first[2], started[2], started[3], out, keep)


def pack_kernel(items):
    total = slots(items)

    def body(spot, owned, behind, ahead, sections, out):
        place = spot[1]

        def plane(side, item):
            if item < SECTIONS:
                return sections[item, 16 * side : 16 * side + 16, :]
            row = {NEAR1: 16, NEAR2: 32, COEF: 48}[item]
            return (owned, behind, ahead)[side][row : row + 16, :]

        def fill(to, distance, side):
            slot = 0
            for origin, least in ((0, distance), (side, BLOCK - distance)):
                for item, reach in items:
                    if reach >= least:
                        out[to, 16 * slot : 16 * slot + 16, :] = plane(origin, item)
                        slot += 1

        for d in range(1, BLOCK):

            @pl.when(place + d < BLOCK)
            def _():
                fill(place + d, d, 2)

            @pl.when(place + d >= BLOCK)
            def _():
                fill(place + d - BLOCK, BLOCK - d, 1)

    return body, total


def sweep(spot, items, owned, behind, ahead, sections, windows, coefs, started, line, history):
    place = spot[1]
    rank = {item: i for i, (item, _) in enumerate(items)}
    reach_of = dict(items)

    def fetch(item, w):
        if w in (0, -BLOCK, BLOCK):
            side = {0: 0, -BLOCK: 1, BLOCK: 2}[w]
            if item < SECTIONS:
                return unpack(sections[item, 16 * side : 16 * side + 16, :])
            row = {NEAR1: 16, NEAR2: 32, COEF: 48}[item]
            return unpack((owned, behind, ahead)[side][row : row + 16, :])
        at = place + w
        outside = jnp.logical_or(at < 0, at >= BLOCK)
        slot = rank[item] + jnp.where(outside, count(items, BLOCK - abs(w)), 0)
        return unpack(windows[at & (BLOCK - 1), pl.ds(pl.multiple_of(16 * slot, 16), 16), :])

    if COEF in rank:
        for w in range(-7, 8):
            coefs[w + 7] = fetch(COEF, w)
    history[0] = jnp.zeros((32, 128), F32)
    history[1] = started[4]
    history[2] = started[2]
    history[3] = started[5]
    history[4] = jnp.zeros((32, 128), F32)
    for w in range(-8, 9):
        value = fetch(0, w)
        line[0, w + 8] = value
        if abs(w) <= 2:
            history[5 + w + 2] = value
    for k in range(1, SECTIONS - 1):
        old, new = (k - 1) % 2, k % 2
        for w in range(-reach_of[k], reach_of[k] + 1):
            centre = line[old, w + 8]
            slope = coarse_slope(line[old, w + 7], centre, line[old, w + 9], coefs[w + 7])
            value = centre + (STEP * QUAD[2][0]) * slope + fetch(k, w)
            line[new, w + 8] = value
            if abs(w) <= 2:
                history[5 * (k + 1) + w + 2] = value
    return fetch


def correct(spot, fetch, coefs, started, history, kept, values, nodes, below, above, coeff, begin, scratch):
    section = spot[0]
    s = [history[5 * section + i] for i in range(5)]
    slope = [coarse_slope(s[i], s[i + 1], s[i + 2], coefs[6 + i]) for i in range(3)]
    later = jnp.full((32, 128), section, jnp.int32) > 0
    edges = []
    for w, i in ((-1, 0), (1, 2)):
        for m, near in ((1, NEAR1), (2, NEAR2)):
            edges.append(fetch(near, w) + jnp.where(later, ROWSUM[m] * s[i + 1] + START[m] * slope[i], 0.0))
    coarse = [s[2]] + [s[2] + (STEP * QUAD[m][0]) * slope[1] + kept[m - 1] for m in (1, 2)]
    wide = spread([coarse[j] - values[j] for j in range(3)] + edges, scratch)
    fixed = [[nodes[j][x] + wide[j] for x in (0, 1)] for j in range(3)]
    rates = [[cubic(fixed[j][x]) for x in (0, 1)] for j in range(3)]
    fresh = []
    for m in (1, 2):
        sums = [mix(m, [fixed[j][x] for j in range(3)]) for x in (0, 1)]
        ends = [below[m - 1] + wide[2 + m], above[m - 1] + wide[4 + m]]
        fresh.append([])
        for x in (0, 1):
            change = around(sums[x]) - 6.0 * sums[x] + sums[1 - x] + ends[x]
            change = change + coeff[x] * mix(m, [rates[j][x] for j in range(3)])
            fresh[-1].append(begin[x] + STEP * change)
    return coarse[2], fresh


def starting(spot, initial, received):
    first = jnp.full((64, 128), spot[0], jnp.int32) == 0
    return [jnp.where(first, initial[x], received[x]) for x in (0, 1)]


def finish_first(
    spot, owned, behind, ahead, sections, windows, started, kept, below, above, initial, coeff, guess, received,
    fresh_out, begin_out, up, down, keep, coefs, line, history, scratch,
):
    fetch = sweep(spot, ITEMS[0], owned, behind, ahead, sections, windows, coefs, started, line, history)
    begin = starting(spot, initial, received)
    u = [guess[0], guess[1]]
    c = [coeff[0], coeff[1]]
    low = [ROWSUM[m] * below[0:64, :] for m in (1, 2)]
    high = [ROWSUM[m] * above[0:64, :] for m in (1, 2)]
    value = kept[1]
    _, fresh = correct(
        spot, fetch, coefs, started, history, (started[0], started[1]), [value] * 3, [u] * 3, low, high, c, begin, scratch
    )
    nodes = [begin] + fresh
    rates = [[cubic(nodes[j][x]) for x in (0, 1)] for j in range(3)]
    planes = []
    for m in (1, 2):
        sums = [mix(m, [nodes[j][x] for j in range(3)]) for x in (0, 1)]
        down[64 * (m - 1) : 64 * m, :] = sums[0]
        up[64 * (m - 1) : 64 * m, :] = sums[1]
        both = sums[0] + sums[1]
        part = around(both) - 5.0 * both
        for x in (0, 1):
            part = part + c[x] * mix(m, [rates[j][x] for j in range(3)])
        planes.append(part)
    for j in range(3):
        planes.append(nodes[j][0] + nodes[j][1])
    for x in (0, 1):
        begin_out[x] = begin[x]
        for m in (0, 1):
            fresh_out[m, x] = fresh[m][x]
    small = squash(planes, scratch)
    keep[0] = small[0]
    keep[1] = small[1]
    for j in range(3):
        keep[2 + j] = 0.125 * small[2 + j]
    up[128:144, :] = pack(keep[2])
    down[128:144, :] = pack(keep[2])


def finish_second(
    spot, owned, behind, ahead, sections, windows, started, kept, kept_k, below, above, initial, coeff, begin_in, fresh_in,
    received, coefs, fresh_out, coarse_out, line, history, scratch,
):
    fetch = sweep(spot, ITEMS[1], owned, behind, ahead, sections, windows, coefs, started, line, history)
    begin = starting(spot, initial, received)
    nodes = [[begin_in[0], begin_in[1]]] + [[fresh_in[m, 0], fresh_in[m, 1]] for m in (0, 1)]
    low = [below[64 * m : 64 * m + 64, :] for m in (0, 1)]
    high = [above[64 * m : 64 * m + 64, :] for m in (0, 1)]
    end, fresh = correct(
        spot, fetch, coefs, started, history, (kept_k[0], kept_k[1]), [kept[2], kept[3], kept[4]], nodes, low, high,
        [coeff[0], coeff[1]], begin, scratch,
    )
    for m in (0, 1):
        for x in (0, 1):
            fresh_out[m, x] = fresh[m][x]
    coarse_out[...] = end[:, :64]


def run(body, args, outs, scratch=(), name=None):
    scalars = args[0].dtype == jnp.int32
    specs = [pl.BlockSpec(memory_space=pltpu.SMEM)] if scalars else []
    specs += [pl.BlockSpec(memory_space=pltpu.VMEM)] * (len(args) - len(specs))
    return pl.pallas_call(
        body,
        out_shape=[jax.ShapeDtypeStruct(shape, F32) for shape in outs],
        in_specs=specs,
        out_specs=[pl.BlockSpec(memory_space=pltpu.VMEM)] * len(outs),
        scratch_shapes=[pltpu.VMEM(shape, F32) for shape in scratch],
        name=name,
    )(*args)


class Links:
    call = staticmethod(run)

    @staticmethod
    def spot():
        return jnp.stack([lax.axis_index("tm"), lax.axis_index("place")]).astype(jnp.int32)

    @staticmethod
    def shift(x, by):
        n = lax.axis_size("block") * lax.axis_size("place")
        return lax.ppermute(x, ("block", "place"), [(i, (i + by) % n) for i in range(n)])

    @staticmethod
    def onward(x):
        n = lax.axis_size("tm")
        return lax.ppermute(x, "tm", [(i, i + 1) for i in range(n - 1)])

    @staticmethod
    def sections(x):
        return lax.all_to_all(jnp.broadcast_to(x, (SECTIONS,) + x.shape), "tm", 0, 0)

    @staticmethod
    def block(x):
        return lax.all_to_all(x, "place", 0, 0)

    @staticmethod
    def stack(*planes):
        return jnp.concatenate([p[:16] for p in planes], axis=0)


def iterate(links, initial, coeff, guess):
    spot = links.spot()
    coarse = (32, 128)
    work = [(2, 17) + coarse, (40,) + coarse]

    up, down, kept = links.call(
        first_kernel, (initial, coeff, guess), [(96, 128), (96, 128), (4,) + coarse], [(256, 128)], name="first"
    )
    below, above = links.shift(up, 1), links.shift(down, -1)
    received = links.onward(guess)
    owned, started = links.call(
        complete_first, (spot, below, above, kept), [(64, 128), (6,) + coarse], [(128, 128)], name="complete_first"
    )

    def windows(owned, items):
        behind, ahead = links.shift(owned, BLOCK), links.shift(owned, -BLOCK)
        sections = links.sections(links.stack(owned, behind, ahead))
        body, total = pack_kernel(items)
        (packets,) = links.call(
            body, (spot, owned, behind, ahead, sections), [(BLOCK, 16 * total, 128)], name="hand_out"
        )
        return behind, ahead, sections, links.block(packets)

    behind, ahead, sections, around_us = windows(owned, ITEMS[0])
    fresh, begin, up, down, kept2, coefs = links.call(
        finish_first,
        (spot, owned, behind, ahead, sections, around_us, started, kept, below, above, initial, coeff, guess, received),
        [(2, 2, 64, 128), (2, 64, 128), (144, 128), (144, 128), (5,) + coarse, (15,) + coarse],
        work + [(448, 128)],
        name="finish_first",
    )
    below, above = links.shift(up, 1), links.shift(down, -1)
    received = links.onward(fresh[1])
    owned, kept_k = links.call(
        complete_second, (spot, below, above, kept2, started, kept), [(48, 128), (2,) + coarse], [(256, 128)],
        name="complete_second",
    )
    behind, ahead, sections, around_us = windows(owned, ITEMS[1])
    fine, coarse_end = links.call(
        finish_second,
        (spot, owned, behind, ahead, sections, around_us, started, kept2, kept_k, below, above, initial, coeff, begin, fresh,
         received, coefs),
        [(2, 2, 64, 128), (32, 64)],
        work + [(448, 128)],
        name="finish_second",
    )
    return fine, coarse_end


def on_device(initial, coeff, guess):
    fine, coarse_end = iterate(Links, initial, coeff, guess[0])
    return fine[None], coarse_end[None, None]


def solution(mesh):
    split = Mesh(
        mesh.devices.reshape(mesh.shape["tm"], mesh.shape["space"] // BLOCK, BLOCK), ("tm", "block", "place")
    )
    space = ("block", "place")
    return jax.shard_map(
        on_device,
        mesh=split,
        in_specs=(P(space, None, None), P(space, None, None), P("tm", space, None, None)),
        out_specs=(P("tm", None, space, None, None), P("tm", space, None, None)),
        check_vma=False,
    )
```

```python
import jax
import jax.numpy as jnp
from jax import lax
from jax.experimental import pallas as pl
from jax.experimental.pallas import tpu as pltpu
from jax.sharding import Mesh, PartitionSpec as P

STEP = 0.06
QUAD = ((0.0, 0.0, 0.0), (5.0 / 24.0, 1.0 / 3.0, -1.0 / 24.0), (1.0 / 6.0, 2.0 / 3.0, 1.0 / 6.0))
ROWSUM = tuple(sum(row) for row in QUAD)
START = tuple(STEP * (row[1] * QUAD[1][0] + row[2] * QUAD[2][0]) for row in QUAD)
SECTIONS = 8
BLOCK = 8
F32 = jnp.float32

COEF, NEAR1, NEAR2 = 10, 11, 12
ITEMS = (
    ((0, 8), (1, 7), (COEF, 7), (2, 6), (3, 5), (4, 4), (5, 3), (6, 2), (NEAR1, 1), (NEAR2, 1)),
    ((0, 8), (1, 7), (2, 6), (3, 5), (4, 4), (5, 3), (6, 2), (NEAR1, 1), (NEAR2, 1)),
)


def count(items, distance):
    return sum(1 for _, reach in items if reach >= distance)


def slots(items):
    return max(count(items, d) + count(items, BLOCK - d) for d in range(1, BLOCK))


def turn(x, by, axis):
    return pltpu.roll(x, by % x.shape[axis], axis)


def around(x):
    return turn(x, 1, 0) + turn(x, -1, 0) + turn(x, 1, 1) + turn(x, -1, 1)


def cubic(u):
    return u - u * u * u


def dot(a, b):
    return jnp.dot(a, b, precision=lax.Precision.HIGHEST, preferred_element_type=F32)


def pair_lanes():
    z = lax.broadcasted_iota(jnp.int32, (128, 128), 0)
    c = lax.broadcasted_iota(jnp.int32, (128, 128), 1)
    return jnp.where((z >> 1) == (c & 63), 1.0, 0.0).astype(F32)


def spread_lanes():
    c = lax.broadcasted_iota(jnp.int32, (128, 128), 0)
    z = lax.broadcasted_iota(jnp.int32, (128, 128), 1)
    return jnp.where((z >> 1) == c, 1.0, 0.0).astype(F32)


def squash(planes, scratch):
    for i, plane in enumerate(planes):
        scratch[64 * i : 64 * i + 64, :] = plane
    both = scratch[pl.ds(0, 32 * len(planes), 2), :] + scratch[pl.ds(1, 32 * len(planes), 2), :]
    sums = dot(both, pair_lanes())
    return [sums[32 * i : 32 * i + 32] for i in range(len(planes))]


def spread(planes, scratch):
    wide = dot(jnp.concatenate(planes, axis=0), spread_lanes())
    scratch[pl.ds(0, 32 * len(planes), 2), :] = wide
    scratch[pl.ds(1, 32 * len(planes), 2), :] = wide
    return [scratch[64 * i : 64 * i + 64, :] for i in range(len(planes))]


def left(shape):
    return lax.broadcasted_iota(jnp.int32, shape, 1) < 64


def pack(x):
    return jnp.where(left((16, 128)), x[:16], x[16:])


def unpack(t):
    other = turn(t, 64, 1)
    here = left((16, 128))
    return jnp.concatenate([jnp.where(here, t, other), jnp.where(here, other, t)], axis=0)


def coarse_slope(below, centre, above, coef):
    return 0.25 * (around(centre) + below + above - 6.0 * centre) + coef * cubic(centre)


def mix(row, nodes):
    return QUAD[row][0] * nodes[0] + QUAD[row][1] * nodes[1] + QUAD[row][2] * nodes[2]


def first_kernel(initial, coeff, guess, up, down, keep, scratch):
    u = [guess[0], guess[1]]
    c = [coeff[0], coeff[1]]
    rate = [c[x] * cubic(u[x]) for x in (0, 1)]
    total = None
    for x in (0, 1):
        part = around(u[x]) - 6.0 * u[x] + u[1 - x] + rate[x]
        total = part if total is None else total + part
    own, value, coef, start = squash([total, u[0] + u[1], c[0] + c[1], initial[0] + initial[1]], scratch)
    value, coef, start = 0.125 * value, 0.125 * coef, 0.125 * start
    for out, plane in ((up, u[1]), (down, u[0])):
        out[0:64, :] = plane
        out[64:80, :] = pack(value)
        out[80:96, :] = pack(start)
    keep[0] = own
    keep[1] = value
    keep[2] = coef
    keep[3] = start


def hand_over(spot, own, values, value0, value0_sides, coef, start, start_slope, out, gathered):
    slope = coarse_slope(value0_sides[0], value0, value0_sides[1], coef)
    k = [(STEP / 8.0) * own[m] - (STEP * QUAD[m + 1][0]) * slope for m in (0, 1)]
    first = (jnp.full((32, 128), spot[0], jnp.int32) == 0)
    out[0:16, :] = pack(k[1] + jnp.where(first, start + STEP * QUAD[2][0] * start_slope, 0.0))
    for m in (0, 1):
        near = QUAD[m + 1][1] * k[0] + QUAD[m + 1][2] * k[1] - values[m]
        near = near + jnp.where(first, ROWSUM[m + 1] * start + START[m + 1] * start_slope, 0.0)
        out[16 * (m + 1) : 16 * (m + 2), :] = pack(near)
    gathered[0] = k[0]
    gathered[1] = k[1]


def complete_first(spot, below, above, kept, out, keep, scratch):
    own, value, coef, start = (kept[i] for i in range(4))
    low, high = squash([below[0:64, :], above[0:64, :]], scratch)
    whole = own + low + high
    sides = [unpack(below[64:80, :]), unpack(above[64:80, :])]
    start_sides = [unpack(below[80:96, :]), unpack(above[80:96, :])]
    start_slope = coarse_slope(start_sides[0], start, start_sides[1], coef)
    hand_over(
        spot, [ROWSUM[1] * whole, ROWSUM[2] * whole], [ROWSUM[1] * value, ROWSUM[2] * value],
        value, sides, coef, start, start_slope, out, keep,
    )
    out[48:64, :] = pack(coef)
    keep[2] = start
    keep[3] = start_slope
    keep[4] = start_sides[0]
    keep[5] = start_sides[1]


def complete_second(spot, below, above, kept, started, kept_first, out, keep, scratch):
    low1, low2, high1, high2 = squash(
        [below[0:64, :], below[64:128, :], above[0:64, :], above[64:128, :]], scratch
    )
    own = [kept[0] + low1 + high1, kept[1] + low2 + high2]
    values = [mix(m, [kept[2], kept[3], kept[4]]) for m in (1, 2)]
    sides = [unpack(below[128:144, :]), unpack(above[128:144, :])]
    hand_over(spot, own, values, kept[2], sides, kept_first[2], started[2], started[3], out, keep)


def pack_kernel(items):
    total = slots(items)

    def body(spot, owned, behind, ahead, sections, out):
        place = spot[1]

        def plane(side, item):
            if item < SECTIONS:
                return sections[item, 16 * side : 16 * side + 16, :]
            row = {NEAR1: 16, NEAR2: 32, COEF: 48}[item]
            return (owned, behind, ahead)[side][row : row + 16, :]

        def fill(to, distance, side):
            slot = 0
            for origin, least in ((0, distance), (side, BLOCK - distance)):
                for item, reach in items:
                    if reach >= least:
                        out[to, 16 * slot : 16 * slot + 16, :] = plane(origin, item)
                        slot += 1

        for d in range(1, BLOCK):

            @pl.when(place + d < BLOCK)
            def _():
                fill(place + d, d, 2)

            @pl.when(place + d >= BLOCK)
            def _():
                fill(place + d - BLOCK, BLOCK - d, 1)

    return body, total


def sweep(spot, items, owned, behind, ahead, sections, windows, coefs, started, line, history):
    place = spot[1]
    rank = {item: i for i, (item, _) in enumerate(items)}
    reach_of = dict(items)

    def fetch(item, w):
        if w in (0, -BLOCK, BLOCK):
            side = {0: 0, -BLOCK: 1, BLOCK: 2}[w]
            if item < SECTIONS:
                return unpack(sections[item, 16 * side : 16 * side + 16, :])
            row = {NEAR1: 16, NEAR2: 32, COEF: 48}[item]
            return unpack((owned, behind, ahead)[side][row : row + 16, :])
        at = place + w
        outside = jnp.logical_or(at < 0, at >= BLOCK)
        slot = rank[item] + jnp.where(outside, count(items, BLOCK - abs(w)), 0)
        return unpack(windows[at & (BLOCK - 1), pl.ds(pl.multiple_of(16 * slot, 16), 16), :])

    if COEF in rank:
        for w in range(-7, 8):
            coefs[w + 7] = fetch(COEF, w)
    history[0] = jnp.zeros((32, 128), F32)
    history[1] = started[4]
    history[2] = started[2]
    history[3] = started[5]
    history[4] = jnp.zeros((32, 128), F32)
    for w in range(-8, 9):
        value = fetch(0, w)
        line[0, w + 8] = value
        if abs(w) <= 2:
            history[5 + w + 2] = value
    for k in range(1, SECTIONS - 1):
        old, new = (k - 1) % 2, k % 2
        for w in range(-reach_of[k], reach_of[k] + 1):
            centre = line[old, w + 8]
            slope = coarse_slope(line[old, w + 7], centre, line[old, w + 9], coefs[w + 7])
            value = centre + (STEP * QUAD[2][0]) * slope + fetch(k, w)
            line[new, w + 8] = value
            if abs(w) <= 2:
                history[5 * (k + 1) + w + 2] = value
    return fetch


def correct(spot, fetch, coefs, started, history, kept, values, nodes, below, above, coeff, begin, scratch):
    section = spot[0]
    s = [history[5 * section + i] for i in range(5)]
    slope = [coarse_slope(s[i], s[i + 1], s[i + 2], coefs[6 + i]) for i in range(3)]
    later = jnp.full((32, 128), section, jnp.int32) > 0
    edges = []
    for w, i in ((-1, 0), (1, 2)):
        for m, near in ((1, NEAR1), (2, NEAR2)):
            edges.append(fetch(near, w) + jnp.where(later, ROWSUM[m] * s[i + 1] + START[m] * slope[i], 0.0))
    coarse = [s[2]] + [s[2] + (STEP * QUAD[m][0]) * slope[1] + kept[m - 1] for m in (1, 2)]
    wide = spread([coarse[j] - values[j] for j in range(3)] + edges, scratch)
    fixed = [[nodes[j][x] + wide[j] for x in (0, 1)] for j in range(3)]
    rates = [[cubic(fixed[j][x]) for x in (0, 1)] for j in range(3)]
    fresh = []
    for m in (1, 2):
        sums = [mix(m, [fixed[j][x] for j in range(3)]) for x in (0, 1)]
        ends = [below[m - 1] + wide[2 + m], above[m - 1] + wide[4 + m]]
        fresh.append([])
        for x in (0, 1):
            change = around(sums[x]) - 6.0 * sums[x] + sums[1 - x] + ends[x]
            change = change + coeff[x] * mix(m, [rates[j][x] for j in range(3)])
            fresh[-1].append(begin[x] + STEP * change)
    return coarse[2], fresh


def starting(spot, initial, received):
    first = jnp.full((64, 128), spot[0], jnp.int32) == 0
    return [jnp.where(first, initial[x], received[x]) for x in (0, 1)]


def finish_first(
    spot, owned, behind, ahead, sections, windows, started, kept, below, above, initial, coeff, guess, received,
    fresh_out, begin_out, up, down, keep, coefs, line, history, scratch,
):
    fetch = sweep(spot, ITEMS[0], owned, behind, ahead, sections, windows, coefs, started, line, history)
    begin = starting(spot, initial, received)
    u = [guess[0], guess[1]]
    c = [coeff[0], coeff[1]]
    low = [ROWSUM[m] * below[0:64, :] for m in (1, 2)]
    high = [ROWSUM[m] * above[0:64, :] for m in (1, 2)]
    value = kept[1]
    _, fresh = correct(
        spot, fetch, coefs, started, history, (started[0], started[1]), [value] * 3, [u] * 3, low, high, c, begin, scratch
    )
    nodes = [begin] + fresh
    rates = [[cubic(nodes[j][x]) for x in (0, 1)] for j in range(3)]
    planes = []
    for m in (1, 2):
        sums = [mix(m, [nodes[j][x] for j in range(3)]) for x in (0, 1)]
        down[64 * (m - 1) : 64 * m, :] = sums[0]
        up[64 * (m - 1) : 64 * m, :] = sums[1]
        both = sums[0] + sums[1]
        part = around(both) - 5.0 * both
        for x in (0, 1):
            part = part + c[x] * mix(m, [rates[j][x] for j in range(3)])
        planes.append(part)
    for j in range(3):
        planes.append(nodes[j][0] + nodes[j][1])
    for x in (0, 1):
        begin_out[x] = begin[x]
        for m in (0, 1):
            fresh_out[m, x] = fresh[m][x]
    small = squash(planes, scratch)
    keep[0] = small[0]
    keep[1] = small[1]
    for j in range(3):
        keep[2 + j] = 0.125 * small[2 + j]
    up[128:144, :] = pack(keep[2])
    down[128:144, :] = pack(keep[2])


def finish_second(
    spot, owned, behind, ahead, sections, windows, started, kept, kept_k, below, above, initial, coeff, begin_in, fresh_in,
    received, coefs, fresh_out, coarse_out, line, history, scratch,
):
    fetch = sweep(spot, ITEMS[1], owned, behind, ahead, sections, windows, coefs, started, line, history)
    begin = starting(spot, initial, received)
    nodes = [[begin_in[0], begin_in[1]]] + [[fresh_in[m, 0], fresh_in[m, 1]] for m in (0, 1)]
    low = [below[64 * m : 64 * m + 64, :] for m in (0, 1)]
    high = [above[64 * m : 64 * m + 64, :] for m in (0, 1)]
    end, fresh = correct(
        spot, fetch, coefs, started, history, (kept_k[0], kept_k[1]), [kept[2], kept[3], kept[4]], nodes, low, high,
        [coeff[0], coeff[1]], begin, scratch,
    )
    for m in (0, 1):
        for x in (0, 1):
            fresh_out[m, x] = fresh[m][x]
    coarse_out[...] = end[:, :64]


def run(body, args, outs, scratch=(), name=None):
    scalars = args[0].dtype == jnp.int32
    specs = [pl.BlockSpec(memory_space=pltpu.SMEM)] if scalars else []
    specs += [pl.BlockSpec(memory_space=pltpu.VMEM)] * (len(args) - len(specs))
    return pl.pallas_call(
        body,
        out_shape=[jax.ShapeDtypeStruct(shape, F32) for shape in outs],
        in_specs=specs,
        out_specs=[pl.BlockSpec(memory_space=pltpu.VMEM)] * len(outs),
        scratch_shapes=[pltpu.VMEM(shape, F32) for shape in scratch],
        name=name,
    )(*args)


class Links:
    call = staticmethod(run)

    @staticmethod
    def spot():
        return jnp.stack([lax.axis_index("tm"), lax.axis_index("place")]).astype(jnp.int32)

    @staticmethod
    def shift(x, by):
        n = lax.axis_size("block") * lax.axis_size("place")
        return lax.ppermute(x, ("block", "place"), [(i, (i + by) % n) for i in range(n)])

    @staticmethod
    def onward(x):
        n = lax.axis_size("tm")
        return lax.ppermute(x, "tm", [(i, i + 1) for i in range(n - 1)])

    @staticmethod
    def sections(x):
        return lax.all_to_all(jnp.broadcast_to(x, (SECTIONS,) + x.shape), "tm", 0, 0)

    @staticmethod
    def block(x):
        return lax.all_to_all(x, "place", 0, 0)

    @staticmethod
    def together(*values):
        return lax.optimization_barrier(values)

    @staticmethod
    def stack(*planes):
        return jnp.concatenate([p[:16] for p in planes], axis=0)


def iterate(links, initial, coeff, guess):
    spot = links.spot()
    coarse = (32, 128)
    work = [(2, 17) + coarse, (40,) + coarse]

    up, down, kept = links.call(
        first_kernel, (initial, coeff, guess), [(96, 128), (96, 128), (4,) + coarse], [(256, 128)], name="first"
    )
    below, above = links.shift(up, 1), links.shift(down, -1)
    below, above, received = links.together(below, above, links.onward(guess))
    owned, started = links.call(
        complete_first, (spot, below, above, kept), [(64, 128), (6,) + coarse], [(128, 128)], name="complete_first"
    )

    def windows(owned, items):
        behind, ahead = links.shift(owned, BLOCK), links.shift(owned, -BLOCK)
        sections = links.sections(links.stack(owned, behind, ahead))
        body, total = pack_kernel(items)
        (packets,) = links.call(
            body, (spot, owned, behind, ahead, sections), [(BLOCK, 16 * total, 128)], name="hand_out"
        )
        return behind, ahead, sections, links.block(packets)

    behind, ahead, sections, around_us = windows(owned, ITEMS[0])
    fresh, begin, up, down, kept2, coefs = links.call(
        finish_first,
        (spot, owned, behind, ahead, sections, around_us, started, kept, below, above, initial, coeff, guess, received),
        [(2, 2, 64, 128), (2, 64, 128), (144, 128), (144, 128), (5,) + coarse, (15,) + coarse],
        work + [(448, 128)],
        name="finish_first",
    )
    below, above = links.shift(up, 1), links.shift(down, -1)
    below, above, received = links.together(below, above, links.onward(fresh[1]))
    owned, kept_k = links.call(
        complete_second, (spot, below, above, kept2, started, kept), [(48, 128), (2,) + coarse], [(256, 128)],
        name="complete_second",
    )
    behind, ahead, sections, around_us = windows(owned, ITEMS[1])
    fine, coarse_end = links.call(
        finish_second,
        (spot, owned, behind, ahead, sections, around_us, started, kept2, kept_k, below, above, initial, coeff, begin, fresh,
         received, coefs),
        [(2, 2, 64, 128), (32, 64)],
        work + [(448, 128)],
        name="finish_second",
    )
    return fine, coarse_end


def on_device(initial, coeff, guess):
    fine, coarse_end = iterate(Links, initial, coeff, guess[0])
    return fine[None], coarse_end[None, None]


def solution(mesh):
    split = Mesh(
        mesh.devices.reshape(mesh.shape["tm"], mesh.shape["space"] // BLOCK, BLOCK), ("tm", "block", "place")
    )
    space = ("block", "place")
    return jax.shard_map(
        on_device,
        mesh=split,
        in_specs=(P(space, None, None), P(space, None, None), P("tm", space, None, None)),
        out_specs=(P("tm", None, space, None, None), P("tm", space, None, None)),
        check_vma=False,
    )
```

```python
import jax
import jax.numpy as jnp
from jax import lax
from jax.experimental import pallas as pl
from jax.experimental.pallas import tpu as pltpu
from jax.sharding import Mesh, PartitionSpec as P

STEP = 0.06
QUAD = ((0.0, 0.0, 0.0), (5.0 / 24.0, 1.0 / 3.0, -1.0 / 24.0), (1.0 / 6.0, 2.0 / 3.0, 1.0 / 6.0))
ROWSUM = tuple(sum(row) for row in QUAD)
START = tuple(STEP * (row[1] * QUAD[1][0] + row[2] * QUAD[2][0]) for row in QUAD)
SECTIONS = 8
BLOCK = 8
CHIPS = BLOCK // 2
F32 = jnp.float32

COEF, NEAR1, NEAR2 = 10, 11, 12
ITEMS = (
    ((0, 8), (1, 7), (COEF, 7), (2, 6), (3, 5), (4, 4), (5, 3), (6, 2), (NEAR1, 1), (NEAR2, 1)),
    ((0, 8), (1, 7), (2, 6), (3, 5), (4, 4), (5, 3), (6, 2), (NEAR1, 1), (NEAR2, 1)),
)


def count(items, distance):
    return sum(1 for _, reach in items if reach >= distance)


def shares(core, ahead):
    if ahead == 0:
        return (0, 1), (2 - core, BLOCK - 1)
    if ahead > 0:
        return (0, 2 * ahead - core), (2, BLOCK - 1 - 2 * ahead + core)
    return (0, -2 * ahead + core - 1), (1, BLOCK + 2 * ahead - core)


def slots(items):
    return max(sum(count(items, least) for _, least in shares(core, a)) for core in (0, 1) for a in range(-3, 4))


def turn(x, by, axis):
    return pltpu.roll(x, by % x.shape[axis], axis)


def around(x):
    return turn(x, 1, 0) + turn(x, -1, 0) + turn(x, 1, 1) + turn(x, -1, 1)


def cubic(u):
    return u - u * u * u


def dot(a, b):
    return jnp.dot(a, b, precision=lax.Precision.HIGHEST, preferred_element_type=F32)


def pair_lanes():
    z = lax.broadcasted_iota(jnp.int32, (128, 128), 0)
    c = lax.broadcasted_iota(jnp.int32, (128, 128), 1)
    return jnp.where((z >> 1) == (c & 63), 1.0, 0.0).astype(F32)


def spread_lanes():
    c = lax.broadcasted_iota(jnp.int32, (128, 128), 0)
    z = lax.broadcasted_iota(jnp.int32, (128, 128), 1)
    return jnp.where((z >> 1) == c, 1.0, 0.0).astype(F32)


def squash(planes, scratch):
    for i, plane in enumerate(planes):
        scratch[64 * i : 64 * i + 64, :] = plane
    both = scratch[pl.ds(0, 32 * len(planes), 2), :] + scratch[pl.ds(1, 32 * len(planes), 2), :]
    sums = dot(both, pair_lanes())
    return [sums[32 * i : 32 * i + 32] for i in range(len(planes))]


def spread(planes, scratch):
    wide = dot(jnp.concatenate(planes, axis=0), spread_lanes())
    scratch[pl.ds(0, 32 * len(planes), 2), :] = wide
    scratch[pl.ds(1, 32 * len(planes), 2), :] = wide
    return [scratch[64 * i : 64 * i + 64, :] for i in range(len(planes))]


def left(shape):
    return lax.broadcasted_iota(jnp.int32, shape, 1) < 64


def pack(x):
    return jnp.where(left((16, 128)), x[:16], x[16:])


def unpack(t):
    other = turn(t, 64, 1)
    here = left((16, 128))
    return jnp.concatenate([jnp.where(here, t, other), jnp.where(here, other, t)], axis=0)


def coarse_slope(below, centre, above, coef):
    return 0.25 * (around(centre) + below + above - 6.0 * centre) + coef * cubic(centre)


def mix(row, nodes):
    return QUAD[row][0] * nodes[0] + QUAD[row][1] * nodes[1] + QUAD[row][2] * nodes[2]


def packets(spot, up, down, inner, outer):
    low = spot[2] == 0

    @pl.when(low)
    def _():
        for row, part_up, part_down in zip_rows(up, down):
            inner[row : row + part_up.shape[0], :] = part_up
            outer[row : row + part_up.shape[0], :] = part_down

    @pl.when(jnp.logical_not(low))
    def _():
        for row, part_up, part_down in zip_rows(up, down):
            inner[row : row + part_up.shape[0], :] = part_down
            outer[row : row + part_up.shape[0], :] = part_up


def zip_rows(up, down):
    row = 0
    for part_up, part_down in zip(up, down):
        yield row, part_up, part_down
        row += part_up.shape[0]


def sides(spot, inner, outer):
    low = jnp.full(inner.shape, spot[2], jnp.int32) == 0
    a, b = inner[...], outer[...]
    return jnp.where(low, b, a), jnp.where(low, a, b)


def first_kernel(spot, initial, coeff, guess, inner, outer, keep, scratch):
    u = [guess[0], guess[1]]
    c = [coeff[0], coeff[1]]
    both = u[0] + u[1]
    total = around(both) - 5.0 * both + c[0] * cubic(u[0]) + c[1] * cubic(u[1])
    own, value, coef, start = squash([total, both, c[0] + c[1], initial[0] + initial[1]], scratch)
    value, coef, start = 0.125 * value, 0.125 * coef, 0.125 * start
    small = [pack(value), pack(start)]
    packets(spot, [u[1]] + small, [u[0]] + small, inner, outer)
    keep[0] = own
    keep[1] = value
    keep[2] = coef
    keep[3] = start


def hand_over(spot, own, values, value0, value0_sides, coef, start, start_slope, out, mine, gathered):
    slope = coarse_slope(value0_sides[0], value0, value0_sides[1], coef)
    k = [(STEP / 8.0) * own[m] - (STEP * QUAD[m + 1][0]) * slope for m in (0, 1)]
    first = (jnp.full((32, 128), spot[0], jnp.int32) == 0)
    ours = pack(k[1] + jnp.where(first, start + STEP * QUAD[2][0] * start_slope, 0.0))
    out[0:16, :] = ours
    mine[...] = ours
    for m in (0, 1):
        near = QUAD[m + 1][1] * k[0] + QUAD[m + 1][2] * k[1] - values[m]
        near = near + jnp.where(first, ROWSUM[m + 1] * start + START[m + 1] * start_slope, 0.0)
        out[16 * (m + 1) : 16 * (m + 2), :] = pack(near)
    gathered[0] = k[0]
    gathered[1] = k[1]


def complete_first(spot, inner, outer, kept, out, mine, keep, scratch):
    below, above = sides(spot, inner, outer)
    own, value, coef, start = (kept[i] for i in range(4))
    low, high = squash([below[0:64, :], above[0:64, :]], scratch)
    whole = own + low + high
    value_sides = [unpack(below[64:80, :]), unpack(above[64:80, :])]
    start_sides = [unpack(below[80:96, :]), unpack(above[80:96, :])]
    start_slope = coarse_slope(start_sides[0], start, start_sides[1], coef)
    hand_over(
        spot, [ROWSUM[1] * whole, ROWSUM[2] * whole], [ROWSUM[1] * value, ROWSUM[2] * value],
        value, value_sides, coef, start, start_slope, out, mine, keep,
    )
    out[48:64, :] = pack(coef)
    keep[2] = start
    keep[3] = start_slope
    keep[4] = start_sides[0]
    keep[5] = start_sides[1]


def complete_second(spot, inner, outer, kept, started, kept_first, out, mine, keep, scratch):
    below, above = sides(spot, inner, outer)
    low1, low2, high1, high2 = squash(
        [below[0:64, :], below[64:128, :], above[0:64, :], above[64:128, :]], scratch
    )
    own = [kept[0] + low1 + high1, kept[1] + low2 + high2]
    values = [mix(m, [kept[2], kept[3], kept[4]]) for m in (1, 2)]
    value_sides = [unpack(below[128:144, :]), unpack(above[128:144, :])]
    hand_over(spot, own, values, kept[2], value_sides, kept_first[2], started[2], started[3], out, mine, keep)


def pack_kernel(items):
    total = slots(items)

    def body(spot, owned, behind, ahead, sections, out):
        chip, core = spot[1], spot[2]

        def plane(side, item):
            if item < SECTIONS:
                return sections[item, 16 * side : 16 * side + 16, :]
            row = {NEAR1: 16, NEAR2: 32, COEF: 48}[item]
            return (owned, behind, ahead)[side][row : row + 16, :]

        def fill(own_core, away):
            slot = 0
            for side, least in shares(own_core, away):
                for item, reach in items:
                    if reach >= least:
                        out[chip + away, 16 * slot : 16 * slot + 16, :] = plane(side, item)
                        slot += 1

        for own_core in (0, 1):
            for away in range(1 - CHIPS, CHIPS):
                there = jnp.logical_and(chip + away >= 0, chip + away < CHIPS)

                @pl.when(jnp.logical_and(core == own_core, there))
                def _():
                    fill(own_core, away)

    return body, total


def sweep(spot, items, owned, behind, ahead, sections, windows, swapped, coefs, started, line, history):
    core = spot[2]
    place = 2 * spot[1] + core
    rank = {item: i for i, (item, _) in enumerate(items)}
    reach_of = dict(items)

    def fetch(item, w):
        if w in (0, -BLOCK, BLOCK):
            side = {0: 0, -BLOCK: 1, BLOCK: 2}[w]
            if item < SECTIONS:
                return unpack(sections[item, 16 * side : 16 * side + 16, :])
            row = {NEAR1: 16, NEAR2: 32, COEF: 48}[item]
            return unpack((owned, behind, ahead)[side][row : row + 16, :])
        at = place + w
        if w > 0:
            outside, least = at >= BLOCK, [max(1, BLOCK - w - i) for i in (0, 1)]
        else:
            outside, least = at < 0, [max(1, BLOCK - 1 + w + i) for i in (0, 1)]
        before = jnp.where(core == 0, count(items, least[0]), count(items, least[1]))
        slot = rank[item] + jnp.where(outside, before, 0)
        source = windows if w % 2 == 0 else swapped
        return unpack(source[(at & (BLOCK - 1)) >> 1, pl.ds(pl.multiple_of(16 * slot, 16), 16), :])

    if COEF in rank:
        for w in range(-7, 8):
            coefs[w + 7] = fetch(COEF, w)
    history[0] = jnp.zeros((32, 128), F32)
    history[1] = started[4]
    history[2] = started[2]
    history[3] = started[5]
    history[4] = jnp.zeros((32, 128), F32)
    for w in range(-8, 9):
        value = fetch(0, w)
        line[0, w + 8] = value
        if abs(w) <= 2:
            history[5 + w + 2] = value
    for k in range(1, SECTIONS - 1):
        old, new = (k - 1) % 2, k % 2
        for w in range(-reach_of[k], reach_of[k] + 1):
            centre = line[old, w + 8]
            slope = coarse_slope(line[old, w + 7], centre, line[old, w + 9], coefs[w + 7])
            value = centre + (STEP * QUAD[2][0]) * slope + fetch(k, w)
            line[new, w + 8] = value
            if abs(w) <= 2:
                history[5 * (k + 1) + w + 2] = value
    return fetch


def correct(spot, fetch, coefs, started, history, kept, values, nodes, below, above, coeff, begin, scratch):
    section = spot[0]
    s = [history[5 * section + i] for i in range(5)]
    slope = [coarse_slope(s[i], s[i + 1], s[i + 2], coefs[6 + i]) for i in range(3)]
    later = jnp.full((32, 128), section, jnp.int32) > 0
    edges = []
    for w, i in ((-1, 0), (1, 2)):
        for m, near in ((1, NEAR1), (2, NEAR2)):
            edges.append(fetch(near, w) + jnp.where(later, ROWSUM[m] * s[i + 1] + START[m] * slope[i], 0.0))
    coarse = [s[2]] + [s[2] + (STEP * QUAD[m][0]) * slope[1] + kept[m - 1] for m in (1, 2)]
    wide = spread([coarse[j] - values[j] for j in range(3)] + edges, scratch)
    fixed = [[nodes[j][x] + wide[j] for x in (0, 1)] for j in range(3)]
    rates = [[cubic(fixed[j][x]) for x in (0, 1)] for j in range(3)]
    fresh = []
    for m in (1, 2):
        sums = [mix(m, [fixed[j][x] for j in range(3)]) for x in (0, 1)]
        ends = [below[m - 1] + wide[2 + m], above[m - 1] + wide[4 + m]]
        fresh.append([])
        for x in (0, 1):
            change = around(sums[x]) - 6.0 * sums[x] + sums[1 - x] + ends[x]
            change = change + coeff[x] * mix(m, [rates[j][x] for j in range(3)])
            fresh[-1].append(begin[x] + STEP * change)
    return coarse[2], fresh


def starting(spot, initial, received):
    first = jnp.full((64, 128), spot[0], jnp.int32) == 0
    return [jnp.where(first, initial[x], received[x]) for x in (0, 1)]


def finish_first(
    spot, owned, behind, ahead, sections, windows, swapped, started, kept, inner, outer, initial, coeff, guess, received,
    fresh_out, begin_out, inner_out, outer_out, keep, coefs, line, history, scratch,
):
    below, above = sides(spot, inner, outer)
    fetch = sweep(spot, ITEMS[0], owned, behind, ahead, sections, windows, swapped, coefs, started, line, history)
    begin = starting(spot, initial, received)
    u = [guess[0], guess[1]]
    c = [coeff[0], coeff[1]]
    low = [ROWSUM[m] * below[0:64, :] for m in (1, 2)]
    high = [ROWSUM[m] * above[0:64, :] for m in (1, 2)]
    value = kept[1]
    _, fresh = correct(
        spot, fetch, coefs, started, history, (started[0], started[1]), [value] * 3, [u] * 3, low, high, c, begin, scratch
    )
    nodes = [begin] + fresh
    rates = [[cubic(nodes[j][x]) for x in (0, 1)] for j in range(3)]
    planes, up, down = [], [], []
    for m in (1, 2):
        sums = [mix(m, [nodes[j][x] for j in range(3)]) for x in (0, 1)]
        down.append(sums[0])
        up.append(sums[1])
        both = sums[0] + sums[1]
        part = around(both) - 5.0 * both
        for x in (0, 1):
            part = part + c[x] * mix(m, [rates[j][x] for j in range(3)])
        planes.append(part)
    for j in range(3):
        planes.append(nodes[j][0] + nodes[j][1])
    for x in (0, 1):
        begin_out[x] = begin[x]
        for m in (0, 1):
            fresh_out[m, x] = fresh[m][x]
    small = squash(planes, scratch)
    keep[0] = small[0]
    keep[1] = small[1]
    for j in range(3):
        keep[2 + j] = 0.125 * small[2 + j]
    small = [pack(0.125 * small[2])]
    packets(spot, up + small, down + small, inner_out, outer_out)


def finish_second(
    spot, owned, behind, ahead, sections, windows, swapped, started, kept, kept_k, inner, outer, initial, coeff, begin_in,
    fresh_in, received, coefs, fresh_out, coarse_out, line, history, scratch,
):
    below, above = sides(spot, inner, outer)
    fetch = sweep(spot, ITEMS[1], owned, behind, ahead, sections, windows, swapped, coefs, started, line, history)
    begin = starting(spot, initial, received)
    nodes = [[begin_in[0], begin_in[1]]] + [[fresh_in[m, 0], fresh_in[m, 1]] for m in (0, 1)]
    low = [below[64 * m : 64 * m + 64, :] for m in (0, 1)]
    high = [above[64 * m : 64 * m + 64, :] for m in (0, 1)]
    end, fresh = correct(
        spot, fetch, coefs, started, history, (kept_k[0], kept_k[1]), [kept[2], kept[3], kept[4]], nodes, low, high,
        [coeff[0], coeff[1]], begin, scratch,
    )
    for m in (0, 1):
        for x in (0, 1):
            fresh_out[m, x] = fresh[m][x]
    coarse_out[...] = end[:, :64]


def run(body, args, outs, scratch=(), name=None):
    scalars = args[0].dtype == jnp.int32
    specs = [pl.BlockSpec(memory_space=pltpu.SMEM)] if scalars else []
    specs += [pl.BlockSpec(memory_space=pltpu.VMEM)] * (len(args) - len(specs))
    return pl.pallas_call(
        body,
        out_shape=[jax.ShapeDtypeStruct(shape, F32) for shape in outs],
        in_specs=specs,
        out_specs=[pl.BlockSpec(memory_space=pltpu.VMEM)] * len(outs),
        scratch_shapes=[pltpu.VMEM(shape, F32) for shape in scratch],
        name=name,
    )(*args)


class Links:
    call = staticmethod(run)

    @staticmethod
    def spot():
        return jnp.stack([lax.axis_index(a) for a in ("tm", "chip", "core")]).astype(jnp.int32)

    @staticmethod
    def shift(x, by):
        n = lax.axis_size("block") * BLOCK
        return lax.ppermute(x, ("block", "chip", "core"), [(i, (i + by) % n) for i in range(n)])

    @staticmethod
    def swap_inner(x):
        return lax.ppermute(x, "core", [(0, 1), (1, 0)])

    @staticmethod
    def swap_outer(x):
        n = lax.axis_size("block") * BLOCK
        return lax.ppermute(x, ("block", "chip", "core"), [(i, (i + 2 * (i % 2) - 1) % n) for i in range(n)])

    @staticmethod
    def onward(x):
        n = lax.axis_size("tm")
        return lax.ppermute(x, "tm", [(i, i + 1) for i in range(n - 1)])

    @staticmethod
    def sections(x):
        return lax.all_to_all(jnp.broadcast_to(x, (SECTIONS,) + x.shape), "tm", 0, 0)

    @staticmethod
    def block(x):
        return lax.all_to_all(x, "chip", 0, 0)

    @staticmethod
    def together(*values):
        return lax.optimization_barrier(values)

    @staticmethod
    def stack(*planes):
        return jnp.concatenate([p[:16] for p in planes], axis=0)


def iterate(links, initial, coeff, guess):
    spot = links.spot()
    coarse = (32, 128)
    work = [(2, 17) + coarse, (40,) + coarse]

    def windows(owned, mine, items):
        behind, ahead = links.shift(owned, BLOCK), links.shift(owned, -BLOCK)
        sections = links.sections(links.stack(mine, behind, ahead))
        body, total = pack_kernel(items)
        (parcels,) = links.call(
            body, (spot, owned, behind, ahead, sections), [(CHIPS, 16 * total, 128)], name="hand_out"
        )
        parcels = links.block(parcels)
        return owned, behind, ahead, sections, parcels, links.swap_inner(parcels)

    inner, outer, kept = links.call(
        first_kernel, (spot, initial, coeff, guess), [(96, 128), (96, 128), (4,) + coarse], [(256, 128)], name="first"
    )
    inner, outer, received = links.together(links.swap_inner(inner), links.swap_outer(outer), links.onward(guess))
    owned, mine, started = links.call(
        complete_first, (spot, inner, outer, kept), [(64, 128), (16, 128), (6,) + coarse], [(128, 128)],
        name="complete_first",
    )
    fresh, begin, inner, outer, kept2, coefs = links.call(
        finish_first,
        (spot, *windows(owned, mine, ITEMS[0]), started, kept, inner, outer, initial, coeff, guess, received),
        [(2, 2, 64, 128), (2, 64, 128), (144, 128), (144, 128), (5,) + coarse, (15,) + coarse],
        work + [(448, 128)],
        name="finish_first",
    )
    inner, outer, received = links.together(links.swap_inner(inner), links.swap_outer(outer), links.onward(fresh[1]))
    owned, mine, kept_k = links.call(
        complete_second, (spot, inner, outer, kept2, started, kept), [(48, 128), (16, 128), (2,) + coarse], [(256, 128)],
        name="complete_second",
    )
    fine, coarse_end = links.call(
        finish_second,
        (spot, *windows(owned, mine, ITEMS[1]), started, kept2, kept_k, inner, outer, initial, coeff, begin, fresh,
         received, coefs),
        [(2, 2, 64, 128), (32, 64)],
        work + [(448, 128)],
        name="finish_second",
    )
    return fine, coarse_end


def on_device(initial, coeff, guess):
    fine, coarse_end = iterate(Links, initial, coeff, guess[0])
    return fine[None], coarse_end[None, None]


def solution(mesh):
    split = Mesh(
        mesh.devices.reshape(mesh.shape["tm"], mesh.shape["space"] // BLOCK, CHIPS, 2), ("tm", "block", "chip", "core")
    )
    space = ("block", "chip", "core")
    return jax.shard_map(
        on_device,
        mesh=split,
        in_specs=(P(space, None, None), P(space, None, None), P("tm", space, None, None)),
        out_specs=(P("tm", None, space, None, None), P("tm", space, None, None)),
        check_vma=False,
    )
```

```python
import jax
import jax.numpy as jnp
from jax import lax
from jax.experimental import pallas as pl
from jax.experimental.pallas import tpu as pltpu
from jax.sharding import Mesh, PartitionSpec as P

STEP = 0.06
QUAD = ((0.0, 0.0, 0.0), (5.0 / 24.0, 1.0 / 3.0, -1.0 / 24.0), (1.0 / 6.0, 2.0 / 3.0, 1.0 / 6.0))
ROWSUM = tuple(sum(row) for row in QUAD)
START = tuple(STEP * (row[1] * QUAD[1][0] + row[2] * QUAD[2][0]) for row in QUAD)
SECTIONS = 8
BLOCK = 8
CHIPS = BLOCK // 2
F32 = jnp.float32

COEF, NEAR1, NEAR2 = 10, 11, 12
ITEMS = (
    ((0, 8), (1, 7), (COEF, 7), (2, 6), (3, 5), (4, 4), (5, 3), (6, 2), (NEAR1, 1), (NEAR2, 1)),
    ((0, 8), (1, 7), (2, 6), (3, 5), (4, 4), (5, 3), (6, 2), (NEAR1, 1), (NEAR2, 1)),
)


def count(items, distance):
    return sum(1 for _, reach in items if reach >= distance)


def shares(core, ahead):
    if ahead == 0:
        return (0, 1), (2 - core, BLOCK - 1)
    if ahead > 0:
        return (0, 2 * ahead - core), (2, BLOCK - 1 - 2 * ahead + core)
    return (0, -2 * ahead + core - 1), (1, BLOCK + 2 * ahead - core)


def slots(items):
    return max(sum(count(items, least) for _, least in shares(core, a)) for core in (0, 1) for a in range(-3, 4))


def turn(x, by, axis):
    return pltpu.roll(x, by % x.shape[axis], axis)


def around(x):
    return turn(x, 1, 0) + turn(x, -1, 0) + turn(x, 1, 1) + turn(x, -1, 1)


def cubic(u):
    return u - u * u * u


def dot(a, b):
    return jnp.dot(a, b, precision=lax.Precision.HIGHEST, preferred_element_type=F32)


def pair_lanes():
    z = lax.broadcasted_iota(jnp.int32, (128, 128), 0)
    c = lax.broadcasted_iota(jnp.int32, (128, 128), 1)
    return jnp.where((z >> 1) == (c & 63), 1.0, 0.0).astype(F32)


def spread_lanes():
    c = lax.broadcasted_iota(jnp.int32, (128, 128), 0)
    z = lax.broadcasted_iota(jnp.int32, (128, 128), 1)
    return jnp.where((z >> 1) == c, 1.0, 0.0).astype(F32)


def squash(planes, scratch):
    for i, plane in enumerate(planes):
        scratch[64 * i : 64 * i + 64, :] = plane
    both = scratch[pl.ds(0, 32 * len(planes), 2), :] + scratch[pl.ds(1, 32 * len(planes), 2), :]
    sums = dot(both, pair_lanes())
    return [sums[32 * i : 32 * i + 32] for i in range(len(planes))]


def spread(planes, scratch):
    wide = dot(jnp.concatenate(planes, axis=0), spread_lanes())
    scratch[pl.ds(0, 32 * len(planes), 2), :] = wide
    scratch[pl.ds(1, 32 * len(planes), 2), :] = wide
    return [scratch[64 * i : 64 * i + 64, :] for i in range(len(planes))]


def left(shape):
    return lax.broadcasted_iota(jnp.int32, shape, 1) < 64


def pack(x):
    return jnp.where(left((16, 128)), x[:16], x[16:])


def unpack(t):
    other = turn(t, 64, 1)
    here = left((16, 128))
    return jnp.concatenate([jnp.where(here, t, other), jnp.where(here, other, t)], axis=0)


def coarse_slope(below, centre, above, coef):
    return 0.25 * (around(centre) + below + above - 6.0 * centre) + coef * cubic(centre)


def mix(row, nodes):
    return QUAD[row][0] * nodes[0] + QUAD[row][1] * nodes[1] + QUAD[row][2] * nodes[2]


def packets(spot, up, down, inner, outer):
    low = spot[2] == 0

    @pl.when(low)
    def _():
        for row, part_up, part_down in zip_rows(up, down):
            inner[row : row + part_up.shape[0], :] = part_up
            outer[row : row + part_up.shape[0], :] = part_down

    @pl.when(jnp.logical_not(low))
    def _():
        for row, part_up, part_down in zip_rows(up, down):
            inner[row : row + part_up.shape[0], :] = part_down
            outer[row : row + part_up.shape[0], :] = part_up


def zip_rows(up, down):
    row = 0
    for part_up, part_down in zip(up, down):
        yield row, part_up, part_down
        row += part_up.shape[0]


def sides(spot, inner, outer):
    low = jnp.full(inner.shape, spot[2], jnp.int32) == 0
    a, b = inner[...], outer[...]
    return jnp.where(low, b, a), jnp.where(low, a, b)


def first_kernel(spot, initial, coeff, guess, inner, outer, keep, scratch):
    u = [guess[0], guess[1]]
    c = [coeff[0], coeff[1]]
    both = u[0] + u[1]
    total = around(both) - 5.0 * both + c[0] * cubic(u[0]) + c[1] * cubic(u[1])
    own, value, coef, start = squash([total, both, c[0] + c[1], initial[0] + initial[1]], scratch)
    value, coef, start = 0.125 * value, 0.125 * coef, 0.125 * start
    small = [pack(value), pack(start)]
    packets(spot, [u[1]] + small, [u[0]] + small, inner, outer)
    keep[0] = own
    keep[1] = value
    keep[2] = coef
    keep[3] = start


def hand_over(spot, own, values, value0, value0_sides, coef, start, start_slope, out, mine, gathered):
    slope = coarse_slope(value0_sides[0], value0, value0_sides[1], coef)
    k = [(STEP / 8.0) * own[m] - (STEP * QUAD[m + 1][0]) * slope for m in (0, 1)]
    first = (jnp.full((32, 128), spot[0], jnp.int32) == 0)
    ours = pack(k[1] + jnp.where(first, start + STEP * QUAD[2][0] * start_slope, 0.0))
    out[0:16, :] = ours
    mine[...] = ours
    for m in (0, 1):
        near = QUAD[m + 1][1] * k[0] + QUAD[m + 1][2] * k[1] - values[m]
        near = near + jnp.where(first, ROWSUM[m + 1] * start + START[m + 1] * start_slope, 0.0)
        out[16 * (m + 1) : 16 * (m + 2), :] = pack(near)
    gathered[0] = k[0]
    gathered[1] = k[1]


def complete_first(spot, inner, outer, kept, out, mine, keep, scratch):
    below, above = sides(spot, inner, outer)
    own, value, coef, start = (kept[i] for i in range(4))
    low, high = squash([below[0:64, :], above[0:64, :]], scratch)
    whole = own + low + high
    value_sides = [unpack(below[64:80, :]), unpack(above[64:80, :])]
    start_sides = [unpack(below[80:96, :]), unpack(above[80:96, :])]
    start_slope = coarse_slope(start_sides[0], start, start_sides[1], coef)
    hand_over(
        spot, [ROWSUM[1] * whole, ROWSUM[2] * whole], [ROWSUM[1] * value, ROWSUM[2] * value],
        value, value_sides, coef, start, start_slope, out, mine, keep,
    )
    out[48:64, :] = pack(coef)
    keep[2] = start
    keep[3] = start_slope
    keep[4] = start_sides[0]
    keep[5] = start_sides[1]


def complete_second(spot, inner, outer, kept, started, kept_first, out, mine, keep, scratch):
    below, above = sides(spot, inner, outer)
    low1, low2, high1, high2 = squash(
        [below[0:64, :], below[64:128, :], above[0:64, :], above[64:128, :]], scratch
    )
    own = [kept[0] + low1 + high1, kept[1] + low2 + high2]
    values = [mix(m, [kept[2], kept[3], kept[4]]) for m in (1, 2)]
    value_sides = [unpack(below[128:144, :]), unpack(above[128:144, :])]
    hand_over(spot, own, values, kept[2], value_sides, kept_first[2], started[2], started[3], out, mine, keep)


def pack_kernel(items):
    total = slots(items)

    def body(spot, owned, behind, ahead, sections, out):
        chip, core = spot[1], spot[2]

        def plane(side, item):
            if item < SECTIONS:
                return sections[item, 16 * side : 16 * side + 16, :]
            row = {NEAR1: 16, NEAR2: 32, COEF: 48}[item]
            return (owned, behind, ahead)[side][row : row + 16, :]

        def fill(own_core, away):
            slot = 0
            for side, least in shares(own_core, away):
                for item, reach in items:
                    if reach >= least:
                        out[chip + away, 16 * slot : 16 * slot + 16, :] = plane(side, item)
                        slot += 1

        for own_core in (0, 1):
            for away in range(1 - CHIPS, CHIPS):
                there = jnp.logical_and(chip + away >= 0, chip + away < CHIPS)

                @pl.when(jnp.logical_and(core == own_core, there))
                def _():
                    fill(own_core, away)

    return body, total


def sweep(spot, items, owned, behind, ahead, sections, windows, swapped, coefs, started, line, history):
    core = spot[2]
    place = 2 * spot[1] + core
    rank = {item: i for i, (item, _) in enumerate(items)}
    reach_of = dict(items)

    def fetch(item, w):
        if w in (0, -BLOCK, BLOCK):
            side = {0: 0, -BLOCK: 1, BLOCK: 2}[w]
            if item < SECTIONS:
                return unpack(sections[item, 16 * side : 16 * side + 16, :])
            row = {NEAR1: 16, NEAR2: 32, COEF: 48}[item]
            return unpack((owned, behind, ahead)[side][row : row + 16, :])
        at = place + w
        if w > 0:
            outside, least = at >= BLOCK, [max(1, BLOCK - w - i) for i in (0, 1)]
        else:
            outside, least = at < 0, [max(1, BLOCK - 1 + w + i) for i in (0, 1)]
        before = jnp.where(core == 0, count(items, least[0]), count(items, least[1]))
        slot = rank[item] + jnp.where(outside, before, 0)
        source = windows if w % 2 == 0 else swapped
        return unpack(source[(at & (BLOCK - 1)) >> 1, pl.ds(pl.multiple_of(16 * slot, 16), 16), :])

    if COEF in rank:
        for w in range(-7, 8):
            coefs[w + 7] = fetch(COEF, w)
    history[0] = jnp.zeros((32, 128), F32)
    history[1] = started[4]
    history[2] = started[2]
    history[3] = started[5]
    history[4] = jnp.zeros((32, 128), F32)
    for w in range(-8, 9):
        value = fetch(0, w)
        line[0, w + 8] = value
        if abs(w) <= 2:
            history[5 + w + 2] = value
    for k in range(1, SECTIONS - 1):
        old, new = (k - 1) % 2, k % 2
        for w in range(-reach_of[k], reach_of[k] + 1):
            centre = line[old, w + 8]
            slope = coarse_slope(line[old, w + 7], centre, line[old, w + 9], coefs[w + 7])
            value = centre + (STEP * QUAD[2][0]) * slope + fetch(k, w)
            line[new, w + 8] = value
            if abs(w) <= 2:
                history[5 * (k + 1) + w + 2] = value
    return fetch


def correct(spot, fetch, coefs, started, history, kept, values, nodes, below, above, coeff, begin, scratch):
    section = spot[0]
    s = [history[5 * section + i] for i in range(5)]
    slope = [coarse_slope(s[i], s[i + 1], s[i + 2], coefs[6 + i]) for i in range(3)]
    later = jnp.full((32, 128), section, jnp.int32) > 0
    edges = []
    for w, i in ((-1, 0), (1, 2)):
        for m, near in ((1, NEAR1), (2, NEAR2)):
            edges.append(fetch(near, w) + jnp.where(later, ROWSUM[m] * s[i + 1] + START[m] * slope[i], 0.0))
    coarse = [s[2]] + [s[2] + (STEP * QUAD[m][0]) * slope[1] + kept[m - 1] for m in (1, 2)]
    wide = spread([coarse[j] - values[j] for j in range(3)] + edges, scratch)
    fixed = [[nodes[j][x] + wide[j] for x in (0, 1)] for j in range(3)]
    rates = [[cubic(fixed[j][x]) for x in (0, 1)] for j in range(3)]
    fresh = []
    for m in (1, 2):
        sums = [mix(m, [fixed[j][x] for j in range(3)]) for x in (0, 1)]
        ends = [below[m - 1] + wide[2 + m], above[m - 1] + wide[4 + m]]
        fresh.append([])
        for x in (0, 1):
            change = around(sums[x]) - 6.0 * sums[x] + sums[1 - x] + ends[x]
            change = change + coeff[x] * mix(m, [rates[j][x] for j in range(3)])
            fresh[-1].append(begin[x] + STEP * change)
    return coarse[2], fresh


def starting(spot, initial, received):
    first = jnp.full((64, 128), spot[0], jnp.int32) == 0
    return [jnp.where(first, initial[x], received[x]) for x in (0, 1)]


def finish_first(
    spot, owned, behind, ahead, sections, windows, swapped, started, kept, inner, outer, initial, coeff, guess, received,
    fresh_out, begin_out, inner_out, outer_out, keep, coefs, line, history, scratch,
):
    below, above = sides(spot, inner, outer)
    fetch = sweep(spot, ITEMS[0], owned, behind, ahead, sections, windows, swapped, coefs, started, line, history)
    begin = starting(spot, initial, received)
    u = [guess[0], guess[1]]
    c = [coeff[0], coeff[1]]
    low = [ROWSUM[m] * below[0:64, :] for m in (1, 2)]
    high = [ROWSUM[m] * above[0:64, :] for m in (1, 2)]
    value = kept[1]
    _, fresh = correct(
        spot, fetch, coefs, started, history, (started[0], started[1]), [value] * 3, [u] * 3, low, high, c, begin, scratch
    )
    nodes = [begin] + fresh
    rates = [[cubic(nodes[j][x]) for x in (0, 1)] for j in range(3)]
    planes, up, down = [], [], []
    for m in (1, 2):
        sums = [mix(m, [nodes[j][x] for j in range(3)]) for x in (0, 1)]
        down.append(sums[0])
        up.append(sums[1])
        both = sums[0] + sums[1]
        part = around(both) - 5.0 * both
        for x in (0, 1):
            part = part + c[x] * mix(m, [rates[j][x] for j in range(3)])
        planes.append(part)
    for j in range(3):
        planes.append(nodes[j][0] + nodes[j][1])
    for x in (0, 1):
        begin_out[x] = begin[x]
        for m in (0, 1):
            fresh_out[m, x] = fresh[m][x]
    small = squash(planes, scratch)
    keep[0] = small[0]
    keep[1] = small[1]
    for j in range(3):
        keep[2 + j] = 0.125 * small[2 + j]
    small = [pack(0.125 * small[2])]
    packets(spot, up + small, down + small, inner_out, outer_out)


def finish_second(
    spot, owned, behind, ahead, sections, windows, swapped, started, kept, kept_k, inner, outer, initial, coeff, begin_in,
    fresh_in, received, coefs, fresh_out, coarse_out, line, history, scratch,
):
    below, above = sides(spot, inner, outer)
    fetch = sweep(spot, ITEMS[1], owned, behind, ahead, sections, windows, swapped, coefs, started, line, history)
    begin = starting(spot, initial, received)
    nodes = [[begin_in[0], begin_in[1]]] + [[fresh_in[m, 0], fresh_in[m, 1]] for m in (0, 1)]
    low = [below[64 * m : 64 * m + 64, :] for m in (0, 1)]
    high = [above[64 * m : 64 * m + 64, :] for m in (0, 1)]
    end, fresh = correct(
        spot, fetch, coefs, started, history, (kept_k[0], kept_k[1]), [kept[2], kept[3], kept[4]], nodes, low, high,
        [coeff[0], coeff[1]], begin, scratch,
    )
    for m in (0, 1):
        for x in (0, 1):
            fresh_out[m, x] = fresh[m][x]
    coarse_out[...] = end[:, :64]


def run(body, args, outs, scratch=(), name=None, last=False):
    scalars = args[0].dtype == jnp.int32
    specs = [pl.BlockSpec(memory_space=pltpu.SMEM)] if scalars else []
    specs += [pl.BlockSpec(memory_space=pltpu.VMEM)] * (len(args) - len(specs))
    return pl.pallas_call(
        body,
        out_shape=[jax.ShapeDtypeStruct(shape, F32) if last else pltpu.VMEM(shape, F32) for shape in outs],
        in_specs=specs,
        out_specs=[pl.BlockSpec(memory_space=pltpu.VMEM)] * len(outs),
        scratch_shapes=[pltpu.VMEM(shape, F32) for shape in scratch],
        name=name,
    )(*(a if a.dtype == jnp.int32 else pltpu.with_memory_space_constraint(a, pltpu.VMEM) for a in args))


class Links:
    call = staticmethod(run)

    @staticmethod
    def spot():
        return jnp.stack([lax.axis_index(a) for a in ("tm", "chip", "core")]).astype(jnp.int32)

    @staticmethod
    def shift(x, by):
        n = lax.axis_size("block") * BLOCK
        return lax.ppermute(x, ("block", "chip", "core"), [(i, (i + by) % n) for i in range(n)])

    @staticmethod
    def swap_inner(x):
        return lax.ppermute(x, "core", [(0, 1), (1, 0)])

    @staticmethod
    def swap_outer(x):
        n = lax.axis_size("block") * BLOCK
        return lax.ppermute(x, ("block", "chip", "core"), [(i, (i + 2 * (i % 2) - 1) % n) for i in range(n)])

    @staticmethod
    def onward(x):
        n = lax.axis_size("tm")
        return lax.ppermute(x, "tm", [(i, i + 1) for i in range(n - 1)])

    @staticmethod
    def sections(x):
        return lax.all_to_all(jnp.broadcast_to(x, (SECTIONS,) + x.shape), "tm", 0, 0)

    @staticmethod
    def block(x):
        return lax.all_to_all(x, "chip", 0, 0)

    @staticmethod
    def together(*values):
        return lax.optimization_barrier(values)

    @staticmethod
    def stack(*planes):
        return jnp.concatenate([p[:16] for p in planes], axis=0)


def iterate(links, initial, coeff, guess):
    spot = links.spot()
    coarse = (32, 128)
    work = [(2, 17) + coarse, (40,) + coarse]

    def windows(owned, mine, items):
        behind, ahead = links.shift(owned, BLOCK), links.shift(owned, -BLOCK)
        sections = links.sections(links.stack(mine, behind, ahead))
        body, total = pack_kernel(items)
        (parcels,) = links.call(
            body, (spot, owned, behind, ahead, sections), [(CHIPS, 16 * total, 128)], name="hand_out"
        )
        parcels = links.block(parcels)
        return owned, behind, ahead, sections, parcels, links.swap_inner(parcels)

    inner, outer, kept = links.call(
        first_kernel, (spot, initial, coeff, guess), [(96, 128), (96, 128), (4,) + coarse], [(256, 128)], name="first"
    )
    inner, outer, received = links.together(links.swap_inner(inner), links.swap_outer(outer), links.onward(guess))
    owned, mine, started = links.call(
        complete_first, (spot, inner, outer, kept), [(64, 128), (16, 128), (6,) + coarse], [(128, 128)],
        name="complete_first",
    )
    fresh, begin, inner, outer, kept2, coefs = links.call(
        finish_first,
        (spot, *windows(owned, mine, ITEMS[0]), started, kept, inner, outer, initial, coeff, guess, received),
        [(2, 2, 64, 128), (2, 64, 128), (144, 128), (144, 128), (5,) + coarse, (15,) + coarse],
        work + [(448, 128)],
        name="finish_first",
    )
    inner, outer, received = links.together(links.swap_inner(inner), links.swap_outer(outer), links.onward(fresh[1]))
    owned, mine, kept_k = links.call(
        complete_second, (spot, inner, outer, kept2, started, kept), [(48, 128), (16, 128), (2,) + coarse], [(256, 128)],
        name="complete_second",
    )
    fine, coarse_end = links.call(
        finish_second,
        (spot, *windows(owned, mine, ITEMS[1]), started, kept2, kept_k, inner, outer, initial, coeff, begin, fresh,
         received, coefs),
        [(2, 2, 64, 128), (32, 64)],
        work + [(448, 128)],
        name="finish_second",
        last=True,
    )
    return fine, coarse_end


def on_device(initial, coeff, guess):
    fine, coarse_end = iterate(Links, initial, coeff, guess[0])
    return fine[None], coarse_end[None, None]


def solution(mesh):
    split = Mesh(
        mesh.devices.reshape(mesh.shape["tm"], mesh.shape["space"] // BLOCK, CHIPS, 2), ("tm", "block", "chip", "core")
    )
    space = ("block", "chip", "core")
    return jax.shard_map(
        on_device,
        mesh=split,
        in_specs=(P(space, None, None), P(space, None, None), P("tm", space, None, None)),
        out_specs=(P("tm", None, space, None, None), P("tm", space, None, None)),
        check_vma=False,
    )
```

```python
import jax
import jax.numpy as jnp
from jax import lax
from jax.experimental import pallas as pl
from jax.experimental.pallas import tpu as pltpu
from jax.sharding import Mesh, PartitionSpec as P

STEP = 0.06
QUAD = ((0.0, 0.0, 0.0), (5.0 / 24.0, 1.0 / 3.0, -1.0 / 24.0), (1.0 / 6.0, 2.0 / 3.0, 1.0 / 6.0))
ROWSUM = tuple(sum(row) for row in QUAD)
START = tuple(STEP * (row[1] * QUAD[1][0] + row[2] * QUAD[2][0]) for row in QUAD)
SECTIONS = 8
BLOCK = 8
CHIPS = BLOCK // 2
F32 = jnp.float32

COEF, NEAR1, NEAR2 = 10, 11, 12
ITEMS = (
    ((0, 8), (1, 7), (COEF, 7), (2, 6), (3, 5), (4, 4), (5, 3), (6, 2), (NEAR1, 1), (NEAR2, 1)),
    ((0, 8), (1, 7), (2, 6), (3, 5), (4, 4), (5, 3), (6, 2), (NEAR1, 1), (NEAR2, 1)),
)


def count(items, distance):
    return sum(1 for _, reach in items if reach >= distance)


def shares(core, ahead):
    if ahead == 0:
        return (0, 1), (2 - core, BLOCK - 1)
    if ahead > 0:
        return (0, 2 * ahead - core), (2, BLOCK - 1 - 2 * ahead + core)
    return (0, -2 * ahead + core - 1), (1, BLOCK + 2 * ahead - core)


def slots(items):
    return max(sum(count(items, least) for _, least in shares(core, a)) for core in (0, 1) for a in range(-3, 4))


def turn(x, by, axis):
    return pltpu.roll(x, by % x.shape[axis], axis)


def around(x):
    return turn(x, 1, 0) + turn(x, -1, 0) + turn(x, 1, 1) + turn(x, -1, 1)


def cubic(u):
    return u - u * u * u


def dot(a, b):
    return jnp.dot(a, b, precision=lax.Precision.HIGHEST, preferred_element_type=F32)


def pair_lanes():
    z = lax.broadcasted_iota(jnp.int32, (128, 128), 0)
    c = lax.broadcasted_iota(jnp.int32, (128, 128), 1)
    return jnp.where((z >> 1) == (c & 63), 1.0, 0.0).astype(F32)


def spread_lanes():
    c = lax.broadcasted_iota(jnp.int32, (128, 128), 0)
    z = lax.broadcasted_iota(jnp.int32, (128, 128), 1)
    return jnp.where((z >> 1) == c, 1.0, 0.0).astype(F32)


def squash(planes, scratch):
    for i, plane in enumerate(planes):
        scratch[64 * i : 64 * i + 64, :] = plane
    both = scratch[pl.ds(0, 32 * len(planes), 2), :] + scratch[pl.ds(1, 32 * len(planes), 2), :]
    sums = dot(both, pair_lanes())
    return [sums[32 * i : 32 * i + 32] for i in range(len(planes))]


def spread(planes, scratch):
    wide = dot(jnp.concatenate(planes, axis=0), spread_lanes())
    scratch[pl.ds(0, 32 * len(planes), 2), :] = wide
    scratch[pl.ds(1, 32 * len(planes), 2), :] = wide
    return [scratch[64 * i : 64 * i + 64, :] for i in range(len(planes))]


def left(shape):
    return lax.broadcasted_iota(jnp.int32, shape, 1) < 64


def pack(x):
    return jnp.where(left((16, 128)), x[:16], x[16:])


def unpack(t):
    other = turn(t, 64, 1)
    here = left((16, 128))
    return jnp.concatenate([jnp.where(here, t, other), jnp.where(here, other, t)], axis=0)


def coarse_slope(below, centre, above, coef):
    return 0.25 * (around(centre) + below + above - 6.0 * centre) + coef * cubic(centre)


def mix(row, nodes):
    return QUAD[row][0] * nodes[0] + QUAD[row][1] * nodes[1] + QUAD[row][2] * nodes[2]


def packets(spot, up, down, inner, outer):
    low = spot[2] == 0

    @pl.when(low)
    def _():
        for row, part_up, part_down in zip_rows(up, down):
            inner[row : row + part_up.shape[0], :] = part_up
            outer[row : row + part_up.shape[0], :] = part_down

    @pl.when(jnp.logical_not(low))
    def _():
        for row, part_up, part_down in zip_rows(up, down):
            inner[row : row + part_up.shape[0], :] = part_down
            outer[row : row + part_up.shape[0], :] = part_up


def zip_rows(up, down):
    row = 0
    for part_up, part_down in zip(up, down):
        yield row, part_up, part_down
        row += part_up.shape[0]


def sides(spot, inner, outer):
    low = jnp.full(inner.shape, spot[2], jnp.int32) == 0
    a, b = inner[...], outer[...]
    return jnp.where(low, b, a), jnp.where(low, a, b)


def first_kernel(spot, initial, coeff, guess, inner, outer, keep, scratch):
    u = [guess[0], guess[1]]
    c = [coeff[0], coeff[1]]
    both = u[0] + u[1]
    total = around(both) - 5.0 * both + c[0] * cubic(u[0]) + c[1] * cubic(u[1])
    own, value, coef, start = squash([total, both, c[0] + c[1], initial[0] + initial[1]], scratch)
    value, coef, start = 0.125 * value, 0.125 * coef, 0.125 * start
    small = [pack(value), pack(start)]
    packets(spot, [u[1]] + small, [u[0]] + small, inner, outer)
    keep[0] = own
    keep[1] = value
    keep[2] = coef
    keep[3] = start


def hand_over(spot, own, values, value0, value0_sides, coef, start, start_slope, out, mine, gathered):
    slope = coarse_slope(value0_sides[0], value0, value0_sides[1], coef)
    k = [(STEP / 8.0) * own[m] - (STEP * QUAD[m + 1][0]) * slope for m in (0, 1)]
    first = (jnp.full((32, 128), spot[0], jnp.int32) == 0)
    ours = pack(k[1] + jnp.where(first, start + STEP * QUAD[2][0] * start_slope, 0.0))
    out[0:16, :] = ours
    mine[...] = ours
    for m in (0, 1):
        near = QUAD[m + 1][1] * k[0] + QUAD[m + 1][2] * k[1] - values[m]
        near = near + jnp.where(first, ROWSUM[m + 1] * start + START[m + 1] * start_slope, 0.0)
        out[16 * (m + 1) : 16 * (m + 2), :] = pack(near)
    gathered[0] = k[0]
    gathered[1] = k[1]


def complete_first(spot, inner, outer, kept, out, mine, keep, scratch):
    below, above = sides(spot, inner, outer)
    own, value, coef, start = (kept[i] for i in range(4))
    low, high = squash([below[0:64, :], above[0:64, :]], scratch)
    whole = own + low + high
    value_sides = [unpack(below[64:80, :]), unpack(above[64:80, :])]
    start_sides = [unpack(below[80:96, :]), unpack(above[80:96, :])]
    start_slope = coarse_slope(start_sides[0], start, start_sides[1], coef)
    hand_over(
        spot, [ROWSUM[1] * whole, ROWSUM[2] * whole], [ROWSUM[1] * value, ROWSUM[2] * value],
        value, value_sides, coef, start, start_slope, out, mine, keep,
    )
    out[48:64, :] = pack(coef)
    keep[2] = start
    keep[3] = start_slope
    keep[4] = start_sides[0]
    keep[5] = start_sides[1]


def complete_second(spot, inner, outer, kept, started, kept_first, out, mine, keep, scratch):
    below, above = sides(spot, inner, outer)
    low1, low2, high1, high2 = squash(
        [below[0:64, :], below[64:128, :], above[0:64, :], above[64:128, :]], scratch
    )
    own = [kept[0] + low1 + high1, kept[1] + low2 + high2]
    values = [mix(m, [kept[2], kept[3], kept[4]]) for m in (1, 2)]
    value_sides = [unpack(below[128:144, :]), unpack(above[128:144, :])]
    hand_over(spot, own, values, kept[2], value_sides, kept_first[2], started[2], started[3], out, mine, keep)


def plane(spot, owned, beside, beyond, sections, side, item):
    odd = spot[3]
    if item < SECTIONS:
        if side == 0:
            return sections[item, 0:16, :]
        at = jnp.where(odd == 1, side, 3 - side)
        return sections[item, pl.ds(pl.multiple_of(16 * at, 16), 16), :]
    row = {NEAR1: 16, NEAR2: 32, COEF: 48}[item]
    if side == 0:
        return owned[row : row + 16, :]
    near, far = beside[row : row + 16, :], beyond[row : row + 16, :]
    picked = jnp.full((16, 128), odd, jnp.int32) == (1 if side == 1 else 0)
    return jnp.where(picked, near, far)


def pack_kernel(items):
    total = slots(items)

    def body(spot, owned, beside, beyond, sections, out):
        chip, core = spot[1], spot[2]

        def fill(own_core, away):
            slot = 0
            for side, least in shares(own_core, away):
                for item, reach in items:
                    if reach >= least:
                        out[chip + away, 16 * slot : 16 * slot + 16, :] = plane(spot, owned, beside, beyond, sections, side, item)
                        slot += 1

        for own_core in (0, 1):
            for away in range(1 - CHIPS, CHIPS):
                there = jnp.logical_and(chip + away >= 0, chip + away < CHIPS)

                @pl.when(jnp.logical_and(core == own_core, there))
                def _():
                    fill(own_core, away)

    return body, total


def sweep(spot, items, owned, beside, beyond, sections, windows, swapped, coefs, started, line, history):
    core = spot[2]
    place = 2 * spot[1] + core
    rank = {item: i for i, (item, _) in enumerate(items)}
    reach_of = dict(items)

    def fetch(item, w):
        if w in (0, -BLOCK, BLOCK):
            side = {0: 0, -BLOCK: 1, BLOCK: 2}[w]
            return unpack(plane(spot, owned, beside, beyond, sections, side, item))
        at = place + w
        if w > 0:
            outside, least = at >= BLOCK, [max(1, BLOCK - w - i) for i in (0, 1)]
        else:
            outside, least = at < 0, [max(1, BLOCK - 1 + w + i) for i in (0, 1)]
        before = jnp.where(core == 0, count(items, least[0]), count(items, least[1]))
        slot = rank[item] + jnp.where(outside, before, 0)
        source = windows if w % 2 == 0 else swapped
        return unpack(source[(at & (BLOCK - 1)) >> 1, pl.ds(pl.multiple_of(16 * slot, 16), 16), :])

    if COEF in rank:
        for w in range(-7, 8):
            coefs[w + 7] = fetch(COEF, w)
    history[0] = jnp.zeros((32, 128), F32)
    history[1] = started[4]
    history[2] = started[2]
    history[3] = started[5]
    history[4] = jnp.zeros((32, 128), F32)
    for w in range(-8, 9):
        value = fetch(0, w)
        line[0, w + 8] = value
        if abs(w) <= 2:
            history[5 + w + 2] = value
    for k in range(1, SECTIONS - 1):
        old, new = (k - 1) % 2, k % 2
        for w in range(-reach_of[k], reach_of[k] + 1):
            centre = line[old, w + 8]
            slope = coarse_slope(line[old, w + 7], centre, line[old, w + 9], coefs[w + 7])
            value = centre + (STEP * QUAD[2][0]) * slope + fetch(k, w)
            line[new, w + 8] = value
            if abs(w) <= 2:
                history[5 * (k + 1) + w + 2] = value
    return fetch


def correct(spot, fetch, coefs, started, history, kept, values, nodes, below, above, coeff, begin, scratch):
    section = spot[0]
    s = [history[5 * section + i] for i in range(5)]
    slope = [coarse_slope(s[i], s[i + 1], s[i + 2], coefs[6 + i]) for i in range(3)]
    later = jnp.full((32, 128), section, jnp.int32) > 0
    edges = []
    for w, i in ((-1, 0), (1, 2)):
        for m, near in ((1, NEAR1), (2, NEAR2)):
            edges.append(fetch(near, w) + jnp.where(later, ROWSUM[m] * s[i + 1] + START[m] * slope[i], 0.0))
    coarse = [s[2]] + [s[2] + (STEP * QUAD[m][0]) * slope[1] + kept[m - 1] for m in (1, 2)]
    wide = spread([coarse[j] - values[j] for j in range(3)] + edges, scratch)
    fixed = [[nodes[j][x] + wide[j] for x in (0, 1)] for j in range(3)]
    rates = [[cubic(fixed[j][x]) for x in (0, 1)] for j in range(3)]
    fresh = []
    for m in (1, 2):
        sums = [mix(m, [fixed[j][x] for j in range(3)]) for x in (0, 1)]
        ends = [below[m - 1] + wide[2 + m], above[m - 1] + wide[4 + m]]
        fresh.append([])
        for x in (0, 1):
            change = around(sums[x]) - 6.0 * sums[x] + sums[1 - x] + ends[x]
            change = change + coeff[x] * mix(m, [rates[j][x] for j in range(3)])
            fresh[-1].append(begin[x] + STEP * change)
    return coarse[2], fresh


def starting(spot, initial, received):
    first = jnp.full((64, 128), spot[0], jnp.int32) == 0
    return [jnp.where(first, initial[x], received[x]) for x in (0, 1)]


def finish_first(
    spot, owned, beside, beyond, sections, windows, swapped, started, kept, inner, outer, initial, coeff, guess, received,
    fresh_out, begin_out, inner_out, outer_out, keep, coefs, line, history, scratch,
):
    below, above = sides(spot, inner, outer)
    fetch = sweep(spot, ITEMS[0], owned, beside, beyond, sections, windows, swapped, coefs, started, line, history)
    begin = starting(spot, initial, received)
    u = [guess[0], guess[1]]
    c = [coeff[0], coeff[1]]
    low = [ROWSUM[m] * below[0:64, :] for m in (1, 2)]
    high = [ROWSUM[m] * above[0:64, :] for m in (1, 2)]
    value = kept[1]
    _, fresh = correct(
        spot, fetch, coefs, started, history, (started[0], started[1]), [value] * 3, [u] * 3, low, high, c, begin, scratch
    )
    nodes = [begin] + fresh
    rates = [[cubic(nodes[j][x]) for x in (0, 1)] for j in range(3)]
    planes, up, down = [], [], []
    for m in (1, 2):
        sums = [mix(m, [nodes[j][x] for j in range(3)]) for x in (0, 1)]
        down.append(sums[0])
        up.append(sums[1])
        both = sums[0] + sums[1]
        part = around(both) - 5.0 * both
        for x in (0, 1):
            part = part + c[x] * mix(m, [rates[j][x] for j in range(3)])
        planes.append(part)
    for j in range(3):
        planes.append(nodes[j][0] + nodes[j][1])
    for x in (0, 1):
        begin_out[x] = begin[x]
        for m in (0, 1):
            fresh_out[m, x] = fresh[m][x]
    small = squash(planes, scratch)
    keep[0] = small[0]
    keep[1] = small[1]
    for j in range(3):
        keep[2 + j] = 0.125 * small[2 + j]
    small = [pack(0.125 * small[2])]
    packets(spot, up + small, down + small, inner_out, outer_out)


def finish_second(
    spot, owned, beside, beyond, sections, windows, swapped, started, kept, kept_k, inner, outer, initial, coeff, begin_in,
    fresh_in, received, coefs, fresh_out, coarse_out, line, history, scratch,
):
    below, above = sides(spot, inner, outer)
    fetch = sweep(spot, ITEMS[1], owned, beside, beyond, sections, windows, swapped, coefs, started, line, history)
    begin = starting(spot, initial, received)
    nodes = [[begin_in[0], begin_in[1]]] + [[fresh_in[m, 0], fresh_in[m, 1]] for m in (0, 1)]
    low = [below[64 * m : 64 * m + 64, :] for m in (0, 1)]
    high = [above[64 * m : 64 * m + 64, :] for m in (0, 1)]
    end, fresh = correct(
        spot, fetch, coefs, started, history, (kept_k[0], kept_k[1]), [kept[2], kept[3], kept[4]], nodes, low, high,
        [coeff[0], coeff[1]], begin, scratch,
    )
    for m in (0, 1):
        for x in (0, 1):
            fresh_out[m, x] = fresh[m][x]
    coarse_out[...] = end[:, :64]


def run(body, args, outs, scratch=(), name=None, first=False, last=False):
    def placed(*refs):
        spot = [lax.axis_index(a) for a in ("tm", "chip", "core", "block")]
        body(spot[:3] + [spot[3] & 1], *refs)

    return pl.pallas_call(
        placed,
        out_shape=[jax.ShapeDtypeStruct(shape, F32) if last else pltpu.VMEM(shape, F32) for shape in outs],
        in_specs=[pl.BlockSpec(memory_space=pltpu.VMEM)] * len(args),
        out_specs=[pl.BlockSpec(memory_space=pltpu.VMEM)] * len(outs),
        scratch_shapes=[pltpu.VMEM(shape, F32) for shape in scratch],
        name=name,
    )(*(a if first else pltpu.with_memory_space_constraint(a, pltpu.VMEM) for a in args))


class Links:
    call = staticmethod(run)

    @staticmethod
    def swap_block(x, row):
        n = lax.axis_size("block")
        pairs = [(i, i ^ 1 if row else (i + 2 * (i % 2) - 1) % n) for i in range(n)]
        return lax.ppermute(x, "block", pairs)

    @staticmethod
    def swap_inner(x):
        return lax.ppermute(x, "core", [(0, 1), (1, 0)])

    @staticmethod
    def swap_outer(x):
        n = lax.axis_size("block") * BLOCK
        return lax.ppermute(x, ("block", "chip", "core"), [(i, (i + 2 * (i % 2) - 1) % n) for i in range(n)])

    @staticmethod
    def onward(x):
        n = lax.axis_size("tm")
        return lax.ppermute(x, "tm", [(i, i + 1) for i in range(n - 1)])

    @staticmethod
    def sections(x):
        return lax.all_to_all(jnp.broadcast_to(x, (SECTIONS,) + x.shape), "tm", 0, 0)

    @staticmethod
    def block(x):
        return lax.all_to_all(x, "chip", 0, 0)

    @staticmethod
    def together(*values):
        return lax.optimization_barrier(values)

    @staticmethod
    def stack(*planes):
        return jnp.concatenate([p[:16] for p in planes], axis=0)


def iterate(links, initial, coeff, guess):
    coarse = (32, 128)
    work = [(2, 17) + coarse, (40,) + coarse]

    def windows(owned, mine, items):
        beside, beyond = links.swap_block(owned, True), links.swap_block(owned, False)
        sections = links.sections(links.stack(mine, beside, beyond))
        body, total = pack_kernel(items)
        (parcels,) = links.call(
            body, (owned, beside, beyond, sections), [(CHIPS, 16 * total, 128)], name="hand_out"
        )
        parcels = links.block(parcels)
        return owned, beside, beyond, sections, parcels, links.swap_inner(parcels)

    inner, outer, kept = links.call(
        first_kernel, (initial, coeff, guess), [(96, 128), (96, 128), (4,) + coarse], [(256, 128)], name="first",
        first=True,
    )
    inner, outer, received = links.together(links.swap_inner(inner), links.swap_outer(outer), links.onward(guess))
    owned, mine, started = links.call(
        complete_first, (inner, outer, kept), [(64, 128), (16, 128), (6,) + coarse], [(128, 128)],
        name="complete_first",
    )
    fresh, begin, inner, outer, kept2, coefs = links.call(
        finish_first,
        (*windows(owned, mine, ITEMS[0]), started, kept, inner, outer, initial, coeff, guess, received),
        [(2, 2, 64, 128), (2, 64, 128), (144, 128), (144, 128), (5,) + coarse, (15,) + coarse],
        work + [(448, 128)],
        name="finish_first",
    )
    inner, outer, received = links.together(links.swap_inner(inner), links.swap_outer(outer), links.onward(fresh[1]))
    owned, mine, kept_k = links.call(
        complete_second, (inner, outer, kept2, started, kept), [(48, 128), (16, 128), (2,) + coarse], [(256, 128)],
        name="complete_second",
    )
    fine, coarse_end = links.call(
        finish_second,
        (*windows(owned, mine, ITEMS[1]), started, kept2, kept_k, inner, outer, initial, coeff, begin, fresh,
         received, coefs),
        [(2, 2, 64, 128), (32, 64)],
        work + [(448, 128)],
        name="finish_second",
        last=True,
    )
    return fine, coarse_end


def on_device(initial, coeff, guess):
    fine, coarse_end = iterate(Links, initial, coeff, guess[0])
    return fine[None], coarse_end[None, None]


def solution(mesh):
    split = Mesh(
        mesh.devices.reshape(mesh.shape["tm"], mesh.shape["space"] // BLOCK, CHIPS, 2), ("tm", "block", "chip", "core")
    )
    space = ("block", "chip", "core")
    return jax.shard_map(
        on_device,
        mesh=split,
        in_specs=(P(space, None, None), P(space, None, None), P("tm", space, None, None)),
        out_specs=(P("tm", None, space, None, None), P("tm", space, None, None)),
        check_vma=False,
    )
```

```python
import jax
import jax.numpy as jnp
from jax import lax
from jax.experimental import pallas as pl
from jax.experimental.pallas import tpu as pltpu
from jax.sharding import Mesh, PartitionSpec as P

STEP = 0.06
QUAD = ((0.0, 0.0, 0.0), (5.0 / 24.0, 1.0 / 3.0, -1.0 / 24.0), (1.0 / 6.0, 2.0 / 3.0, 1.0 / 6.0))
ROWSUM = tuple(sum(row) for row in QUAD)
START = tuple(STEP * (row[1] * QUAD[1][0] + row[2] * QUAD[2][0]) for row in QUAD)
SECTIONS = 8
BLOCK = 8
CHIPS = BLOCK // 2
F32 = jnp.float32

COEF, NEAR1, NEAR2, BEGIN, EDGE = 10, 11, 12, 13, 14
ITEMS = (
    ((0, 8), (1, 7), (COEF, 7), (2, 6), (3, 5), (4, 4), (5, 3), (6, 2), (7, 1), (NEAR1, 1), (BEGIN, 1))
    + tuple((EDGE + i, 1) for i in range(4)),
    ((0, 8), (1, 7), (2, 6), (3, 5), (4, 4), (5, 3), (6, 2), (NEAR1, 1), (NEAR2, 1)),
)
ROWS = ({NEAR1: 16, COEF: 32, BEGIN: 48, **{EDGE + i: 64 + 16 * i for i in range(4)}}, {NEAR1: 16, NEAR2: 32})


def count(items, distance):
    return sum(1 for _, reach in items if reach >= distance)


def shares(core, ahead):
    if ahead == 0:
        return (0, 1), (2 - core, BLOCK - 1)
    if ahead > 0:
        return (0, 2 * ahead - core), (2, BLOCK - 1 - 2 * ahead + core)
    return (0, -2 * ahead + core - 1), (1, BLOCK + 2 * ahead - core)


def slots(items):
    return max(sum(count(items, least) for _, least in shares(core, a)) for core in (0, 1) for a in range(-3, 4))


def turn(x, by, axis):
    return pltpu.roll(x, by % x.shape[axis], axis)


def around(x):
    return turn(x, 1, 0) + turn(x, -1, 0) + turn(x, 1, 1) + turn(x, -1, 1)


def cubic(u):
    return u - u * u * u


def dot(a, b):
    return jnp.dot(a, b, precision=lax.Precision.HIGHEST, preferred_element_type=F32)


def pair_lanes():
    z = lax.broadcasted_iota(jnp.int32, (128, 128), 0)
    c = lax.broadcasted_iota(jnp.int32, (128, 128), 1)
    return jnp.where((z >> 1) == (c & 63), 1.0, 0.0).astype(F32)


def spread_lanes():
    c = lax.broadcasted_iota(jnp.int32, (128, 128), 0)
    z = lax.broadcasted_iota(jnp.int32, (128, 128), 1)
    return jnp.where((z >> 1) == c, 1.0, 0.0).astype(F32)


def squash(planes, scratch):
    for i, plane in enumerate(planes):
        scratch[64 * i : 64 * i + 64, :] = plane
    both = scratch[pl.ds(0, 32 * len(planes), 2), :] + scratch[pl.ds(1, 32 * len(planes), 2), :]
    sums = dot(both, pair_lanes())
    return [sums[32 * i : 32 * i + 32] for i in range(len(planes))]


def spread(planes, scratch):
    wide = dot(jnp.concatenate(planes, axis=0), spread_lanes())
    scratch[pl.ds(0, 32 * len(planes), 2), :] = wide
    scratch[pl.ds(1, 32 * len(planes), 2), :] = wide
    return [scratch[64 * i : 64 * i + 64, :] for i in range(len(planes))]


def left(shape):
    return lax.broadcasted_iota(jnp.int32, shape, 1) < 64


def pack(x):
    return jnp.where(left((16, 128)), x[:16], x[16:])


def unpack(t):
    other = turn(t, 64, 1)
    here = left((16, 128))
    return jnp.concatenate([jnp.where(here, t, other), jnp.where(here, other, t)], axis=0)


def coarse_slope(below, centre, above, coef):
    return 0.25 * (around(centre) + below + above - 6.0 * centre) + coef * cubic(centre)


def mix(row, nodes):
    return QUAD[row][0] * nodes[0] + QUAD[row][1] * nodes[1] + QUAD[row][2] * nodes[2]


def packets(spot, up, down, inner, outer):
    low = spot[2] == 0

    @pl.when(low)
    def _():
        for row, part_up, part_down in zip_rows(up, down):
            inner[row : row + part_up.shape[0], :] = part_up
            outer[row : row + part_up.shape[0], :] = part_down

    @pl.when(jnp.logical_not(low))
    def _():
        for row, part_up, part_down in zip_rows(up, down):
            inner[row : row + part_up.shape[0], :] = part_down
            outer[row : row + part_up.shape[0], :] = part_up


def zip_rows(up, down):
    row = 0
    for part_up, part_down in zip(up, down):
        yield row, part_up, part_down
        row += part_up.shape[0]


def sides(spot, inner, outer):
    low = jnp.full(inner.shape, spot[2], jnp.int32) == 0
    a, b = inner[...], outer[...]
    return jnp.where(low, b, a), jnp.where(low, a, b)


def first_kernel(spot, initial, coeff, guess, inner, outer, keep, scratch):
    u = [guess[0], guess[1]]
    c = [coeff[0], coeff[1]]
    both = u[0] + u[1]
    total = around(both) - 5.0 * both + c[0] * cubic(u[0]) + c[1] * cubic(u[1])
    own, value, coef, start = squash([total, both, c[0] + c[1], initial[0] + initial[1]], scratch)
    value, coef, start = 0.125 * value, 0.125 * coef, 0.125 * start
    packets(spot, u + [c[1], pack(start)], u + [c[0], pack(start)], inner, outer)
    keep[0] = own
    keep[1] = value
    keep[2] = coef
    keep[3] = start


def own_k(own, value0, value0_sides, coef):
    slope = coarse_slope(value0_sides[0], value0, value0_sides[1], coef)
    return [(STEP / 8.0) * own[m] - (STEP * QUAD[m + 1][0]) * slope for m in (0, 1)]


def complete_first(
    spot, inner, outer, kept, initial, received, owned, beside, beyond, mine, keep, begin_out, scratch
):
    below, above = sides(spot, inner, outer)
    begin = starting(spot, initial, received)
    own, value, coef, start = (kept[i] for i in range(4))
    low, high, value_low, value_high, value_begin = squash(
        [below[64:128, :], above[0:64, :], below[0:64, :] + below[64:128, :], above[0:64, :] + above[64:128, :],
         begin[0] + begin[1]],
        scratch,
    )
    value_low, value_high = 0.125 * value_low, 0.125 * value_high
    start_low, start_high = unpack(below[192:208, :]), unpack(above[192:208, :])
    start_slope = coarse_slope(start_low, start, start_high, coef)
    whole = own + low + high
    k = own_k([ROWSUM[1] * whole, ROWSUM[2] * whole], value, [value_low, value_high], coef)
    first = jnp.full((32, 128), spot[0], jnp.int32) == 0
    given = [pack(k[m - 1] + jnp.where(first, start + (STEP * QUAD[m][0]) * start_slope, 0.0)) for m in (2, 1)]
    given += [pack(coef), pack(0.125 * value_begin)]
    mine[...] = given[0]
    odd = jnp.full((64, 128), spot[3], jnp.int32) == 1
    for i, part in enumerate(given):
        for out in (owned, beside, beyond):
            out[16 * i : 16 * i + 16, :] = part
    beside[64:128, :] = jnp.where(odd, begin[0], begin[1])
    beyond[64:128, :] = jnp.where(odd, begin[1], begin[0])
    for x in (0, 1):
        owned[64 * (x + 1) : 64 * (x + 2), :] = begin[x]
        begin_out[x] = begin[x]
    for i, part in enumerate([k[0], k[1], start, start_slope, start_low, start_high, value_low, value_high]):
        keep[i] = part


def plane(spot, rows, owned, beside, beyond, sections, side, item, up=False):
    odd = spot[3]
    if item < SECTIONS:
        if side == 0:
            return sections[item, 0:16, :]
        at = jnp.where(odd == 1, side, 3 - side)
        return sections[item, pl.ds(pl.multiple_of(16 * at, 16), 16), :]
    row = rows[item]
    if side == 0:
        row += 64 if item >= EDGE and up else 0
        return owned[row : row + 16, :]
    near, far = beside[row : row + 16, :], beyond[row : row + 16, :]
    picked = jnp.full((16, 128), odd, jnp.int32) == (1 if side == 1 else 0)
    return jnp.where(picked, near, far)


def pack_kernel(items, rows):
    total = slots(items)

    def body(spot, owned, beside, beyond, sections, out):
        chip, core = spot[1], spot[2]

        def fill(own_core, away):
            slot = 0
            up = away > 0 or (away == 0 and own_core == 0)
            for side, least in shares(own_core, away):
                for item, reach in items:
                    if reach >= least:
                        part = plane(spot, rows, owned, beside, beyond, sections, side, item, up)
                        out[chip + away, 16 * slot : 16 * slot + 16, :] = part
                        slot += 1

        for own_core in (0, 1):
            for away in range(1 - CHIPS, CHIPS):
                there = jnp.logical_and(chip + away >= 0, chip + away < CHIPS)

                @pl.when(jnp.logical_and(core == own_core, there))
                def _():
                    fill(own_core, away)

    return body, total


def sweep(spot, items, rows, owned, beside, beyond, sections, windows, swapped, coefs, started, line, history):
    core = spot[2]
    place = 2 * spot[1] + core
    rank = {item: i for i, (item, _) in enumerate(items)}
    reach_of = dict(items)

    def fetch(item, w, whole=False):
        if w in (0, -BLOCK, BLOCK):
            side = {0: 0, -BLOCK: 1, BLOCK: 2}[w]
            return unpack(plane(spot, rows, owned, beside, beyond, sections, side, item))
        at = place + w
        if w > 0:
            outside, least = at >= BLOCK, [max(1, BLOCK - w - i) for i in (0, 1)]
        else:
            outside, least = at < 0, [max(1, BLOCK - 1 + w + i) for i in (0, 1)]
        before = jnp.where(core == 0, count(items, least[0]), count(items, least[1]))
        slot = rank[item] + jnp.where(outside, before, 0)
        source = windows if w % 2 == 0 else swapped
        found = source[(at & (BLOCK - 1)) >> 1, pl.ds(pl.multiple_of(16 * slot, 16), 16), :]
        return found if whole else unpack(found)

    if COEF in rank:
        for w in range(-7, 8):
            coefs[w + 7] = fetch(COEF, w)
    history[0] = jnp.zeros((32, 128), F32)
    history[1] = started[4]
    history[2] = started[2]
    history[3] = started[5]
    history[4] = jnp.zeros((32, 128), F32)
    for w in range(-8, 9):
        value = fetch(0, w)
        line[0, w + 8] = value
        if abs(w) <= 2:
            history[5 + w + 2] = value
    for k in range(1, SECTIONS):
        if k not in rank:
            continue
        old, new = (k - 1) % 2, k % 2
        for w in range(-reach_of[k], reach_of[k] + 1):
            centre = line[old, w + 8]
            slope = coarse_slope(line[old, w + 7], centre, line[old, w + 9], coefs[w + 7])
            value = centre + (STEP * QUAD[2][0]) * slope + fetch(k, w)
            line[new, w + 8] = value
            if abs(w) <= 2:
                history[5 * (k + 1) + w + 2] = value
    return fetch


def correct(spot, fetch, coefs, started, history, kept, values, nodes, below, above, coeff, begin, scratch):
    section = spot[0]
    s = [history[5 * section + i] for i in range(5)]
    slope = [coarse_slope(s[i], s[i + 1], s[i + 2], coefs[6 + i]) for i in range(3)]
    later = jnp.full((32, 128), section, jnp.int32) > 0
    edges = []
    for w, i in ((-1, 0), (1, 2)):
        for m, near in ((1, NEAR1), (2, NEAR2)):
            edges.append(fetch(near, w) + jnp.where(later, ROWSUM[m] * s[i + 1] + START[m] * slope[i], 0.0))
    coarse = [s[2]] + [s[2] + (STEP * QUAD[m][0]) * slope[1] + kept[m - 1] for m in (1, 2)]
    wide = spread([coarse[j] - values[j] for j in range(3)] + edges, scratch)
    fixed = [[nodes[j][x] + wide[j] for x in (0, 1)] for j in range(3)]
    rates = [[cubic(fixed[j][x]) for x in (0, 1)] for j in range(3)]
    fresh = []
    for m in (1, 2):
        sums = [mix(m, [fixed[j][x] for j in range(3)]) for x in (0, 1)]
        ends = [below[m - 1] + wide[2 + m], above[m - 1] + wide[4 + m]]
        fresh.append([])
        for x in (0, 1):
            change = around(sums[x]) - 6.0 * sums[x] + sums[1 - x] + ends[x]
            change = change + coeff[x] * mix(m, [rates[j][x] for j in range(3)])
            fresh[-1].append(begin[x] + STEP * change)
    return coarse[2], fresh


def starting(spot, initial, received):
    first = jnp.full((64, 128), spot[0], jnp.int32) == 0
    return [jnp.where(first, initial[x], received[x]) for x in (0, 1)]


def finish_first(
    spot, owned, beside, beyond, sections, windows, swapped, started, kept, inner, outer, coeff, guess, begin,
    middle_out, end_out, ends, keep, owned_out, mine, coefs, line, history, scratch,
):
    fetch = sweep(
        spot, ITEMS[0], ROWS[0], owned, beside, beyond, sections, windows, swapped, coefs, started, line, history
    )
    below, above = sides(spot, inner, outer)
    section = spot[0]
    later = jnp.full((32, 128), section, jnp.int32) > 0
    s = [history[5 * section + i] for i in range(5)]
    slope = [coarse_slope(s[i], s[i + 1], s[i + 2], coefs[6 + i]) for i in range(3)]
    step = [s[i + 1] + (STEP * QUAD[1][0]) * slope[i] for i in range(3)]
    value = [started[6], kept[1], started[7]]
    coarse = []
    for i in range(3):
        if i == 1:
            one, two = step[1] + started[0], s[2] + (STEP * QUAD[2][0]) * slope[1] + started[1]
        else:
            one = fetch(NEAR1, i - 1) + jnp.where(later, step[i], 0.0)
            two = history[5 * section + 6 + i]
        coarse += [s[i + 1] - value[i], one - value[i], two - value[i]]
    wide = spread(coarse, scratch)
    u = [below[0:64, :], below[64:128, :], guess[0], guess[1], above[0:64, :], above[64:128, :]]
    c = [None, below[128:192, :], coeff[0], coeff[1], above[128:192, :], None]
    b = [None] + [None] * 4 + [None]
    b[2], b[3] = begin[0], begin[1]
    for x, w in ((1, -1), (4, 1)):
        b[x] = jnp.concatenate([fetch(EDGE + i, w, whole=True) for i in range(4)], axis=0)
    fixed = [[u[x] + wide[3 * (x // 2) + j] for j in range(3)] for x in range(6)]
    nodes = [None] + [[b[x]] for x in range(1, 5)] + [None]
    rates = [None] + [[cubic(fixed[x][j]) for j in range(3)] for x in range(1, 5)] + [None]
    for m in (1, 2):
        sums = [mix(m, fixed[x]) for x in range(6)]
        for x in range(1, 5):
            change = around(sums[x]) - 6.0 * sums[x] + sums[x - 1] + sums[x + 1] + c[x] * mix(m, rates[x])
            nodes[x].append(b[x] + STEP * change)
    for x in (0, 1):
        middle_out[x] = nodes[x + 2][1]
        end_out[x] = nodes[x + 2][2]
    rates = [[cubic(nodes[x][j]) for j in range(3)] for x in (2, 3)]
    planes = []
    for m in (1, 2):
        sums = [mix(m, nodes[x]) for x in range(1, 5)]
        ends[m - 1] = sums[0]
        ends[m + 1] = sums[3]
        both = sums[1] + sums[2]
        planes.append(
            around(both) - 5.0 * both + sums[0] + sums[3] + c[2] * mix(m, rates[0]) + c[3] * mix(m, rates[1])
        )
    for j in range(3):
        planes.append(nodes[2][j] + nodes[3][j])
    small = squash(planes, scratch)
    values = [0.125 * small[2 + j] for j in range(3)]
    k = own_k(small[:2], values[0], [fetch(BEGIN, -1), fetch(BEGIN, 1)], kept[2])
    first = jnp.logical_not(later)
    ours = pack(k[1] + jnp.where(first, started[2] + (STEP * QUAD[2][0]) * started[3], 0.0))
    owned_out[0:16, :] = ours
    mine[...] = ours
    for m in (1, 2):
        near = QUAD[m][1] * k[0] + QUAD[m][2] * k[1] - mix(m, values)
        near = near + jnp.where(first, ROWSUM[m] * started[2] + START[m] * started[3], 0.0)
        owned_out[16 * m : 16 * m + 16, :] = pack(near)
    for i, part in enumerate(values + k):
        keep[i] = part


def finish_second(
    spot, owned, beside, beyond, sections, windows, swapped, started, kept, ends, initial, coeff, begin_in, middle_in,
    end_in, received, coefs, fresh_out, coarse_out, line, history, scratch,
):
    fetch = sweep(
        spot, ITEMS[1], ROWS[1], owned, beside, beyond, sections, windows, swapped, coefs, started, line, history
    )
    begin = starting(spot, initial, received)
    nodes = [[part[0], part[1]] for part in (begin_in, middle_in, end_in)]
    end, fresh = correct(
        spot, fetch, coefs, started, history, (kept[3], kept[4]), [kept[0], kept[1], kept[2]], nodes,
        [ends[0], ends[1]], [ends[2], ends[3]], [coeff[0], coeff[1]], begin, scratch,
    )
    for m in (0, 1):
        for x in (0, 1):
            fresh_out[m, x] = fresh[m][x]
    coarse_out[...] = end[:, :64]


def run(body, args, outs, scratch=(), name=None, first=False, last=False):
    def placed(*refs):
        spot = [lax.axis_index(a) for a in ("tm", "chip", "core", "block")]
        body(spot[:3] + [spot[3] & 1], *refs)

    return pl.pallas_call(
        placed,
        out_shape=[jax.ShapeDtypeStruct(shape, F32) if last else pltpu.VMEM(shape, F32) for shape in outs],
        in_specs=[pl.BlockSpec(memory_space=pltpu.VMEM)] * len(args),
        out_specs=[pl.BlockSpec(memory_space=pltpu.VMEM)] * len(outs),
        scratch_shapes=[pltpu.VMEM(shape, F32) for shape in scratch],
        name=name,
    )(*(a if first else pltpu.with_memory_space_constraint(a, pltpu.VMEM) for a in args))


class Links:
    call = staticmethod(run)

    @staticmethod
    def swap_block(x, row):
        n = lax.axis_size("block")
        pairs = [(i, i ^ 1 if row else (i + 2 * (i % 2) - 1) % n) for i in range(n)]
        return lax.ppermute(x, "block", pairs)

    @staticmethod
    def swap_inner(x):
        return lax.ppermute(x, "core", [(0, 1), (1, 0)])

    @staticmethod
    def swap_outer(x):
        n = lax.axis_size("block") * BLOCK
        return lax.ppermute(x, ("block", "chip", "core"), [(i, (i + 2 * (i % 2) - 1) % n) for i in range(n)])

    @staticmethod
    def onward(x):
        n = lax.axis_size("tm")
        return lax.ppermute(x, "tm", [(i, i + 1) for i in range(n - 1)])

    @staticmethod
    def sections(x):
        return lax.all_to_all(jnp.broadcast_to(x, (SECTIONS,) + x.shape), "tm", 0, 0)

    @staticmethod
    def block(x):
        return lax.all_to_all(x, "chip", 0, 0)

    @staticmethod
    def together(*values):
        return lax.optimization_barrier(values)

    @staticmethod
    def stack(*planes):
        return jnp.concatenate([p[:16] for p in planes], axis=0)


def iterate(links, initial, coeff, guess):
    coarse, slab = (32, 128), (2, 64, 128)
    work = [(2, 17) + coarse, (45,) + coarse]

    def windows(owned, beside, beyond, mine, iteration):
        sections = links.sections(links.stack(mine, beside, beyond))
        body, total = pack_kernel(ITEMS[iteration], ROWS[iteration])
        (parcels,) = links.call(
            body, (owned, beside, beyond, sections), [(CHIPS, 16 * total, 128)], name="hand_out"
        )
        parcels = links.block(parcels)
        return owned, beside, beyond, sections, parcels, links.swap_inner(parcels)

    inner, outer, kept = links.call(
        first_kernel, (initial, coeff, guess), [(208, 128), (208, 128), (4,) + coarse], [(256, 128)], name="first",
        first=True,
    )
    inner, outer, received = links.together(links.swap_inner(inner), links.swap_outer(outer), links.onward(guess))
    owned, beside, beyond, mine, started, begin = links.call(
        complete_first, (inner, outer, kept, initial, received),
        [(192, 128), (128, 128), (128, 128), (16, 128), (8,) + coarse, slab], [(320, 128)], name="complete_first",
    )
    beside, beyond = links.swap_block(beside, True), links.swap_block(beyond, False)
    middle, end, ends, kept, owned, mine, coefs = links.call(
        finish_first,
        (*windows(owned, beside, beyond, mine, 0), started, kept, inner, outer, coeff, guess, begin),
        [slab, slab, (4, 64, 128), (5,) + coarse, (48, 128), (16, 128), (15,) + coarse],
        work + [(576, 128)],
        name="finish_first",
    )
    beside, beyond, received = links.together(
        links.swap_block(owned, True), links.swap_block(owned, False), links.onward(end)
    )
    fine, coarse_end = links.call(
        finish_second,
        (*windows(owned, beside, beyond, mine, 1), started, kept, ends, initial, coeff, begin, middle, end, received, coefs),
        [(2, 2, 64, 128), (32, 64)],
        work + [(448, 128)],
        name="finish_second",
        last=True,
    )
    return fine, coarse_end


def on_device(initial, coeff, guess):
    fine, coarse_end = iterate(Links, initial, coeff, guess[0])
    return fine[None], coarse_end[None, None]


def solution(mesh):
    split = Mesh(
        mesh.devices.reshape(mesh.shape["tm"], mesh.shape["space"] // BLOCK, CHIPS, 2), ("tm", "block", "chip", "core")
    )
    space = ("block", "chip", "core")
    return jax.shard_map(
        on_device,
        mesh=split,
        in_specs=(P(space, None, None), P(space, None, None), P("tm", space, None, None)),
        out_specs=(P("tm", None, space, None, None), P("tm", space, None, None)),
        check_vma=False,
    )
```

```python
import jax
import jax.numpy as jnp
from jax import lax
from jax.experimental import pallas as pl
from jax.experimental.pallas import tpu as pltpu
from jax.sharding import Mesh, PartitionSpec as P

STEP = 0.06
QUAD = ((0.0, 0.0, 0.0), (5.0 / 24.0, 1.0 / 3.0, -1.0 / 24.0), (1.0 / 6.0, 2.0 / 3.0, 1.0 / 6.0))
ROWSUM = tuple(sum(row) for row in QUAD)
START = tuple(STEP * (row[1] * QUAD[1][0] + row[2] * QUAD[2][0]) for row in QUAD)
SECTIONS = 8
BLOCK = 8
CHIPS = BLOCK // 2
F32 = jnp.float32

COEF, NEAR1, NEAR2, BEGIN, INITIAL, EDGE = 10, 11, 12, 13, 14, 15
ITEMS = (
    ((0, 8), (1, 7), (COEF, 7), (2, 6), (3, 5), (4, 4), (5, 3), (6, 2), (BEGIN, 2), (INITIAL, 2), (7, 1),
     (NEAR1, 1))
    + tuple((EDGE + i, 1) for i in range(4)),
    ((0, 8), (1, 7), (2, 6), (3, 5), (4, 4), (5, 3), (6, 2), (NEAR1, 1), (NEAR2, 1)),
)
ROWS = ({NEAR1: 16, COEF: 32, BEGIN: 48, INITIAL: 64, **{EDGE + i: 80 + 16 * i for i in range(4)}}, {NEAR1: 16, NEAR2: 32})


def count(items, distance):
    return sum(1 for _, reach in items if reach >= distance)


def shares(core, ahead):
    if ahead == 0:
        return (0, 1), (2 - core, BLOCK - 1)
    if ahead > 0:
        return (0, 2 * ahead - core), (2, BLOCK - 1 - 2 * ahead + core)
    return (0, -2 * ahead + core - 1), (1, BLOCK + 2 * ahead - core)


def slots(items):
    return max(sum(count(items, least) for _, least in shares(core, a)) for core in (0, 1) for a in range(-3, 4))


def turn(x, by, axis):
    return pltpu.roll(x, by % x.shape[axis], axis)


def around(x):
    return turn(x, 1, 0) + turn(x, -1, 0) + turn(x, 1, 1) + turn(x, -1, 1)


def cubic(u):
    return u - u * u * u


def dot(a, b):
    return jnp.dot(a, b, precision=lax.Precision.HIGHEST, preferred_element_type=F32)


def pair_lanes():
    z = lax.broadcasted_iota(jnp.int32, (128, 128), 0)
    c = lax.broadcasted_iota(jnp.int32, (128, 128), 1)
    return jnp.where((z >> 1) == (c & 63), 1.0, 0.0).astype(F32)


def spread_lanes():
    c = lax.broadcasted_iota(jnp.int32, (128, 128), 0)
    z = lax.broadcasted_iota(jnp.int32, (128, 128), 1)
    return jnp.where((z >> 1) == c, 1.0, 0.0).astype(F32)


def squash(planes, scratch):
    for i, plane in enumerate(planes):
        scratch[64 * i : 64 * i + 64, :] = plane
    both = scratch[pl.ds(0, 32 * len(planes), 2), :] + scratch[pl.ds(1, 32 * len(planes), 2), :]
    sums = dot(both, pair_lanes())
    return [sums[32 * i : 32 * i + 32] for i in range(len(planes))]


def spread(planes, scratch):
    wide = dot(jnp.concatenate(planes, axis=0), spread_lanes())
    scratch[pl.ds(0, 32 * len(planes), 2), :] = wide
    scratch[pl.ds(1, 32 * len(planes), 2), :] = wide
    return [scratch[64 * i : 64 * i + 64, :] for i in range(len(planes))]


def left(shape):
    return lax.broadcasted_iota(jnp.int32, shape, 1) < 64


def pack(x):
    return jnp.where(left((16, 128)), x[:16], x[16:])


def unpack(t):
    other = turn(t, 64, 1)
    here = left((16, 128))
    return jnp.concatenate([jnp.where(here, t, other), jnp.where(here, other, t)], axis=0)


def coarse_slope(below, centre, above, coef):
    return 0.25 * (around(centre) + below + above - 6.0 * centre) + coef * cubic(centre)


def mix(row, nodes):
    return QUAD[row][0] * nodes[0] + QUAD[row][1] * nodes[1] + QUAD[row][2] * nodes[2]


def packets(spot, up, down, inner, outer):
    low = spot[2] == 0

    @pl.when(low)
    def _():
        for row, part_up, part_down in zip_rows(up, down):
            inner[row : row + part_up.shape[0], :] = part_up
            outer[row : row + part_up.shape[0], :] = part_down

    @pl.when(jnp.logical_not(low))
    def _():
        for row, part_up, part_down in zip_rows(up, down):
            inner[row : row + part_up.shape[0], :] = part_down
            outer[row : row + part_up.shape[0], :] = part_up


def zip_rows(up, down):
    row = 0
    for part_up, part_down in zip(up, down):
        yield row, part_up, part_down
        row += part_up.shape[0]


def sides(spot, inner, outer):
    low = jnp.full(inner.shape, spot[2], jnp.int32) == 0
    a, b = inner[...], outer[...]
    return jnp.where(low, b, a), jnp.where(low, a, b)


def first_kernel(spot, initial, coeff, guess, inner, outer, keep, scratch):
    u = [guess[0], guess[1]]
    c = [coeff[0], coeff[1]]
    both = u[0] + u[1]
    total = around(both) - 5.0 * both + c[0] * cubic(u[0]) + c[1] * cubic(u[1])
    own, value, coef, start = squash([total, both, c[0] + c[1], initial[0] + initial[1]], scratch)
    value, coef, start = 0.125 * value, 0.125 * coef, 0.125 * start
    packets(spot, u + [c[1], pack(start)], u + [c[0], pack(start)], inner, outer)
    keep[0] = own
    keep[1] = value
    keep[2] = coef
    keep[3] = start


def own_k(own, value0, value0_sides, coef):
    slope = coarse_slope(value0_sides[0], value0, value0_sides[1], coef)
    return [(STEP / 8.0) * own[m] - (STEP * QUAD[m + 1][0]) * slope for m in (0, 1)]


def complete_first(
    spot, inner, outer, kept, initial, received, owned, beside, beyond, mine, keep, begin_out, scratch
):
    below, above = sides(spot, inner, outer)
    begin = starting(spot, initial, received)
    own, value, coef, start = (kept[i] for i in range(4))
    low, high, value_low, value_high, value_begin = squash(
        [below[64:128, :], above[0:64, :], below[0:64, :] + below[64:128, :], above[0:64, :] + above[64:128, :],
         begin[0] + begin[1]],
        scratch,
    )
    value_low, value_high = 0.125 * value_low, 0.125 * value_high
    start_low, start_high = unpack(below[192:208, :]), unpack(above[192:208, :])
    start_slope = coarse_slope(start_low, start, start_high, coef)
    whole = own + low + high
    k = own_k([ROWSUM[1] * whole, ROWSUM[2] * whole], value, [value_low, value_high], coef)
    first = jnp.full((32, 128), spot[0], jnp.int32) == 0
    given = [pack(k[m - 1] + jnp.where(first, start + (STEP * QUAD[m][0]) * start_slope, 0.0)) for m in (2, 1)]
    given += [pack(coef), pack(0.125 * value_begin), pack(start)]
    mine[...] = given[0]
    odd = jnp.full((64, 128), spot[3], jnp.int32) == 1
    for i, part in enumerate(given):
        for out in (owned, beside, beyond):
            out[16 * i : 16 * i + 16, :] = part
    beside[80:144, :] = jnp.where(odd, begin[0], begin[1])
    beyond[80:144, :] = jnp.where(odd, begin[1], begin[0])
    for x in (0, 1):
        owned[80 + 64 * x : 144 + 64 * x, :] = begin[x]
        begin_out[x] = begin[x]
    for i, part in enumerate([k[0], k[1], start, start_slope, start_low, start_high, value_low, value_high]):
        keep[i] = part


def plane(spot, rows, owned, beside, beyond, sections, side, item, up=False):
    odd = spot[3]
    if item < SECTIONS:
        if side == 0:
            return sections[item, 0:16, :]
        at = jnp.where(odd == 1, side, 3 - side)
        return sections[item, pl.ds(pl.multiple_of(16 * at, 16), 16), :]
    row = rows[item]
    if side == 0:
        row += 64 if item >= EDGE and up else 0
        return owned[row : row + 16, :]
    near, far = beside[row : row + 16, :], beyond[row : row + 16, :]
    picked = jnp.full((16, 128), odd, jnp.int32) == (1 if side == 1 else 0)
    return jnp.where(picked, near, far)


def pack_kernel(items, rows):
    total = slots(items)

    def body(spot, owned, beside, beyond, sections, out):
        chip, core = spot[1], spot[2]

        def fill(own_core, away):
            slot = 0
            up = away > 0 or (away == 0 and own_core == 0)
            for side, least in shares(own_core, away):
                for item, reach in items:
                    if reach >= least:
                        part = plane(spot, rows, owned, beside, beyond, sections, side, item, up)
                        out[chip + away, 16 * slot : 16 * slot + 16, :] = part
                        slot += 1

        for own_core in (0, 1):
            for away in range(1 - CHIPS, CHIPS):
                there = jnp.logical_and(chip + away >= 0, chip + away < CHIPS)

                @pl.when(jnp.logical_and(core == own_core, there))
                def _():
                    fill(own_core, away)

    return body, total


def sweep(spot, items, rows, owned, beside, beyond, sections, windows, swapped, coefs, started, line, history):
    core = spot[2]
    place = 2 * spot[1] + core
    rank = {item: i for i, (item, _) in enumerate(items)}
    reach_of = dict(items)

    def fetch(item, w, whole=False):
        if w in (0, -BLOCK, BLOCK):
            side = {0: 0, -BLOCK: 1, BLOCK: 2}[w]
            return unpack(plane(spot, rows, owned, beside, beyond, sections, side, item))
        at = place + w
        if w > 0:
            outside, least = at >= BLOCK, [max(1, BLOCK - w - i) for i in (0, 1)]
        else:
            outside, least = at < 0, [max(1, BLOCK - 1 + w + i) for i in (0, 1)]
        before = jnp.where(core == 0, count(items, least[0]), count(items, least[1]))
        slot = rank[item] + jnp.where(outside, before, 0)
        source = windows if w % 2 == 0 else swapped
        found = source[(at & (BLOCK - 1)) >> 1, pl.ds(pl.multiple_of(16 * slot, 16), 16), :]
        return found if whole else unpack(found)

    if COEF in rank:
        for w in range(-7, 8):
            coefs[w + 7] = fetch(COEF, w)
    outermost = [fetch(INITIAL, w) if INITIAL in rank else jnp.zeros((32, 128), F32) for w in (-2, 2)]
    history[0] = outermost[0]
    history[1] = started[4]
    history[2] = started[2]
    history[3] = started[5]
    history[4] = outermost[1]
    for w in range(-8, 9):
        value = fetch(0, w)
        line[0, w + 8] = value
        if abs(w) <= 2:
            history[5 + w + 2] = value
    for k in range(1, SECTIONS):
        if k not in rank:
            continue
        old, new = (k - 1) % 2, k % 2
        for w in range(-reach_of[k], reach_of[k] + 1):
            centre = line[old, w + 8]
            slope = coarse_slope(line[old, w + 7], centre, line[old, w + 9], coefs[w + 7])
            value = centre + (STEP * QUAD[2][0]) * slope + fetch(k, w)
            line[new, w + 8] = value
            if abs(w) <= 2:
                history[5 * (k + 1) + w + 2] = value
    return fetch


def correct(spot, fetch, coefs, started, history, kept, values, nodes, below, above, coeff, begin, scratch):
    section = spot[0]
    s = [history[5 * section + i] for i in range(5)]
    slope = [coarse_slope(s[i], s[i + 1], s[i + 2], coefs[6 + i]) for i in range(3)]
    later = jnp.full((32, 128), section, jnp.int32) > 0
    edges = []
    for w, i in ((-1, 0), (1, 2)):
        for m, near in ((1, NEAR1), (2, NEAR2)):
            edges.append(fetch(near, w) + jnp.where(later, ROWSUM[m] * s[i + 1] + START[m] * slope[i], 0.0))
    coarse = [s[2]] + [s[2] + (STEP * QUAD[m][0]) * slope[1] + kept[m - 1] for m in (1, 2)]
    wide = spread([coarse[j] - values[j] for j in range(3)] + edges, scratch)
    fixed = [[nodes[j][x] + wide[j] for x in (0, 1)] for j in range(3)]
    rates = [[cubic(fixed[j][x]) for x in (0, 1)] for j in range(3)]
    fresh = []
    for m in (1, 2):
        sums = [mix(m, [fixed[j][x] for j in range(3)]) for x in (0, 1)]
        ends = [below[m - 1] + wide[2 + m], above[m - 1] + wide[4 + m]]
        fresh.append([])
        for x in (0, 1):
            change = around(sums[x]) - 6.0 * sums[x] + sums[1 - x] + ends[x]
            change = change + coeff[x] * mix(m, [rates[j][x] for j in range(3)])
            fresh[-1].append(begin[x] + STEP * change)
    return coarse[2], fresh


def starting(spot, initial, received):
    first = jnp.full((64, 128), spot[0], jnp.int32) == 0
    return [jnp.where(first, initial[x], received[x]) for x in (0, 1)]


def previous_end(section, fetch, coefs, history, starts, coeff, initial, earlier, scratch):
    before = jnp.maximum(section - 1, 0)
    s = [history[5 * before + i] for i in range(5)]
    value = [fetch(BEGIN, w) for w in range(-2, 3)]
    shift = []
    for i in range(3):
        two = history[5 * section + 1 + i]
        slope = coarse_slope(s[i], s[i + 1], s[i + 2], coefs[6 + i])
        slope = slope - coarse_slope(value[i], value[i + 1], value[i + 2], coefs[6 + i])
        one = 0.5 * (s[i + 1] + two) + (STEP * (QUAD[1][0] - 0.5 * QUAD[2][0])) * slope
        shift.append([s[i + 1] - value[i + 1], one - value[i + 1], two - value[i + 1]])
    wide = spread([mix(2, shift[0])] + shift[1] + [mix(2, shift[2])], scratch)
    fixed = [[starts[x] + wide[1 + j] for j in range(3)] for x in (1, 2)]
    sums = [ROWSUM[2] * starts[0] + wide[0], mix(2, fixed[0]), mix(2, fixed[1]), ROWSUM[2] * starts[3] + wide[4]]
    number = jnp.full((64, 128), section, jnp.int32)
    out = []
    for x in (0, 1):
        change = around(sums[x + 1]) - 6.0 * sums[x + 1] + sums[x] + sums[x + 2]
        change = change + coeff[x] * mix(2, [cubic(part) for part in fixed[x]])
        end = jnp.where(number == 1, initial[x], earlier[x]) + STEP * change
        out.append(jnp.where(number == 0, initial[x], end))
    return out


def finish_first(
    spot, owned, beside, beyond, sections, windows, swapped, started, kept, inner, outer, initial, coeff, guess, begin,
    earlier, middle_out, end_out, ends, begin_out, keep, owned_out, mine, coefs, line, history, scratch,
):
    fetch = sweep(
        spot, ITEMS[0], ROWS[0], owned, beside, beyond, sections, windows, swapped, coefs, started, line, history
    )
    below, above = sides(spot, inner, outer)
    section = spot[0]
    later = jnp.full((32, 128), section, jnp.int32) > 0
    s = [history[5 * section + i] for i in range(5)]
    slope = [coarse_slope(s[i], s[i + 1], s[i + 2], coefs[6 + i]) for i in range(3)]
    step = [s[i + 1] + (STEP * QUAD[1][0]) * slope[i] for i in range(3)]
    value = [started[6], kept[1], started[7]]
    coarse = []
    for i in range(3):
        if i == 1:
            one, two = step[1] + started[0], s[2] + (STEP * QUAD[2][0]) * slope[1] + started[1]
        else:
            one = fetch(NEAR1, i - 1) + jnp.where(later, step[i], 0.0)
            two = history[5 * section + 6 + i]
        coarse += [s[i + 1] - value[i], one - value[i], two - value[i]]
    wide = spread(coarse, scratch)
    u = [below[0:64, :], below[64:128, :], guess[0], guess[1], above[0:64, :], above[64:128, :]]
    c = [None, below[128:192, :], coeff[0], coeff[1], above[128:192, :], None]
    b = [None] + [None] * 4 + [None]
    b[2], b[3] = begin[0], begin[1]
    for x, w in ((1, -1), (4, 1)):
        b[x] = jnp.concatenate([fetch(EDGE + i, w, whole=True) for i in range(4)], axis=0)
    begin_next = previous_end(section, fetch, coefs, history, b[1:5], coeff, initial, earlier, scratch)
    for x in (0, 1):
        begin_out[x] = begin_next[x]
    fixed = [[u[x] + wide[3 * (x // 2) + j] for j in range(3)] for x in range(6)]
    nodes = [None] + [[b[x]] for x in range(1, 5)] + [None]
    rates = [None] + [[cubic(fixed[x][j]) for j in range(3)] for x in range(1, 5)] + [None]
    for m in (1, 2):
        sums = [mix(m, fixed[x]) for x in range(6)]
        for x in range(1, 5):
            change = around(sums[x]) - 6.0 * sums[x] + sums[x - 1] + sums[x + 1] + c[x] * mix(m, rates[x])
            nodes[x].append(b[x] + STEP * change)
    for x in (0, 1):
        middle_out[x] = nodes[x + 2][1]
        end_out[x] = nodes[x + 2][2]
    rates = [[cubic(nodes[x][j]) for j in range(3)] for x in (2, 3)]
    planes = []
    for m in (1, 2):
        sums = [mix(m, nodes[x]) for x in range(1, 5)]
        ends[m - 1] = sums[0]
        ends[m + 1] = sums[3]
        both = sums[1] + sums[2]
        planes.append(
            around(both) - 5.0 * both + sums[0] + sums[3] + c[2] * mix(m, rates[0]) + c[3] * mix(m, rates[1])
        )
    for j in range(3):
        planes.append(nodes[2][j] + nodes[3][j])
    small = squash(planes, scratch)
    values = [0.125 * small[2 + j] for j in range(3)]
    k = own_k(small[:2], values[0], [fetch(BEGIN, -1), fetch(BEGIN, 1)], kept[2])
    first = jnp.logical_not(later)
    ours = pack(k[1] + jnp.where(first, started[2] + (STEP * QUAD[2][0]) * started[3], 0.0))
    owned_out[0:16, :] = ours
    mine[...] = ours
    for m in (1, 2):
        near = QUAD[m][1] * k[0] + QUAD[m][2] * k[1] - mix(m, values)
        near = near + jnp.where(first, ROWSUM[m] * started[2] + START[m] * started[3], 0.0)
        owned_out[16 * m : 16 * m + 16, :] = pack(near)
    for i, part in enumerate(values + k):
        keep[i] = part


def finish_second(
    spot, owned, beside, beyond, sections, windows, swapped, started, kept, ends, coeff, begin_in, middle_in, end_in,
    begin, coefs, fresh_out, coarse_out, line, history, scratch,
):
    fetch = sweep(
        spot, ITEMS[1], ROWS[1], owned, beside, beyond, sections, windows, swapped, coefs, started, line, history
    )
    nodes = [[part[0], part[1]] for part in (begin_in, middle_in, end_in)]
    end, fresh = correct(
        spot, fetch, coefs, started, history, (kept[3], kept[4]), [kept[0], kept[1], kept[2]], nodes,
        [ends[0], ends[1]], [ends[2], ends[3]], [coeff[0], coeff[1]], [begin[0], begin[1]], scratch,
    )
    for m in (0, 1):
        for x in (0, 1):
            fresh_out[m, x] = fresh[m][x]
    coarse_out[...] = end[:, :64]


def run(body, args, outs, scratch=(), name=None, first=False, last=False):
    def placed(*refs):
        spot = [lax.axis_index(a) for a in ("tm", "chip", "core", "block")]
        body(spot[:3] + [spot[3] & 1], *refs)

    return pl.pallas_call(
        placed,
        out_shape=[jax.ShapeDtypeStruct(shape, F32) if last else pltpu.VMEM(shape, F32) for shape in outs],
        in_specs=[pl.BlockSpec(memory_space=pltpu.VMEM)] * len(args),
        out_specs=[pl.BlockSpec(memory_space=pltpu.VMEM)] * len(outs),
        scratch_shapes=[pltpu.VMEM(shape, F32) for shape in scratch],
        compiler_params=pltpu.CompilerParams(vmem_limit_bytes=16 << 20),
        name=name,
    )(*(a if first else pltpu.with_memory_space_constraint(a, pltpu.VMEM) for a in args))


class Links:
    call = staticmethod(run)

    @staticmethod
    def swap_block(x, row):
        n = lax.axis_size("block")
        pairs = [(i, i ^ 1 if row else (i + 2 * (i % 2) - 1) % n) for i in range(n)]
        return lax.ppermute(x, "block", pairs)

    @staticmethod
    def swap_inner(x):
        return lax.ppermute(x, "core", [(0, 1), (1, 0)])

    @staticmethod
    def swap_outer(x):
        n = lax.axis_size("block") * BLOCK
        return lax.ppermute(x, ("block", "chip", "core"), [(i, (i + 2 * (i % 2) - 1) % n) for i in range(n)])

    @staticmethod
    def onward(x, by):
        n = lax.axis_size("tm")
        return lax.ppermute(x, "tm", [(i, i + by) for i in range(n - by)])

    @staticmethod
    def sections(x):
        return lax.all_to_all(jnp.broadcast_to(x, (SECTIONS,) + x.shape), "tm", 0, 0)

    @staticmethod
    def block(x):
        return lax.all_to_all(x, "chip", 0, 0)

    @staticmethod
    def together(*values):
        return lax.optimization_barrier(values)

    @staticmethod
    def stack(*planes):
        return jnp.concatenate([p[:16] for p in planes], axis=0)


def iterate(links, initial, coeff, guess):
    coarse, slab = (32, 128), (2, 64, 128)
    work = [(2, 17) + coarse, (45,) + coarse]

    def windows(owned, beside, beyond, mine, iteration):
        sections = links.sections(links.stack(mine, beside, beyond))
        body, total = pack_kernel(ITEMS[iteration], ROWS[iteration])
        (parcels,) = links.call(
            body, (owned, beside, beyond, sections), [(CHIPS, 16 * total, 128)], name="hand_out"
        )
        parcels = links.block(parcels)
        return owned, beside, beyond, sections, parcels, links.swap_inner(parcels)

    inner, outer, kept = links.call(
        first_kernel, (initial, coeff, guess), [(208, 128), (208, 128), (4,) + coarse], [(256, 128)], name="first",
        first=True,
    )
    inner, outer, received, earlier = links.together(
        links.swap_inner(inner), links.swap_outer(outer), links.onward(guess, 1), links.onward(guess, 2)
    )
    owned, beside, beyond, mine, started, begin = links.call(
        complete_first, (inner, outer, kept, initial, received),
        [(208, 128), (144, 128), (144, 128), (16, 128), (8,) + coarse, slab], [(320, 128)], name="complete_first",
    )
    beside, beyond = links.swap_block(beside, True), links.swap_block(beyond, False)
    middle, end, ends, begin_next, kept, owned, mine, coefs = links.call(
        finish_first,
        (*windows(owned, beside, beyond, mine, 0), started, kept, inner, outer, initial, coeff, guess, begin, earlier),
        [slab, slab, (4, 64, 128), slab, (5,) + coarse, (48, 128), (16, 128), (15,) + coarse],
        work + [(576, 128)],
        name="finish_first",
    )
    beside, beyond = links.swap_block(owned, True), links.swap_block(owned, False)
    fine, coarse_end = links.call(
        finish_second,
        (*windows(owned, beside, beyond, mine, 1), started, kept, ends, coeff, begin, middle, end, begin_next, coefs),
        [(2, 2, 64, 128), (32, 64)],
        work + [(448, 128)],
        name="finish_second",
        last=True,
    )
    return fine, coarse_end


def on_device(initial, coeff, guess):
    fine, coarse_end = iterate(Links, initial, coeff, guess[0])
    return fine[None], coarse_end[None, None]


def solution(mesh):
    split = Mesh(
        mesh.devices.reshape(mesh.shape["tm"], mesh.shape["space"] // BLOCK, CHIPS, 2), ("tm", "block", "chip", "core")
    )
    space = ("block", "chip", "core")
    return jax.shard_map(
        on_device,
        mesh=split,
        in_specs=(P(space, None, None), P(space, None, None), P("tm", space, None, None)),
        out_specs=(P("tm", None, space, None, None), P("tm", space, None, None)),
        check_vma=False,
    )
```

```python
import jax
import jax.numpy as jnp
from jax import lax
from jax.experimental import pallas as pl
from jax.experimental.pallas import tpu as pltpu
from jax.sharding import Mesh, PartitionSpec as P

STEP = 0.06
QUAD = ((0.0, 0.0, 0.0), (5.0 / 24.0, 1.0 / 3.0, -1.0 / 24.0), (1.0 / 6.0, 2.0 / 3.0, 1.0 / 6.0))
ROWSUM = tuple(sum(row) for row in QUAD)
START = tuple(STEP * (row[1] * QUAD[1][0] + row[2] * QUAD[2][0]) for row in QUAD)
SECTIONS = 8
BLOCK = 8
CHIPS = BLOCK // 2
F32 = jnp.float32

COEF, NEAR1, NEAR2, BEGIN, INITIAL, EDGE = 10, 11, 12, 13, 14, 15
ITEMS = (
    ((0, 8), (1, 7), (COEF, 7), (2, 6), (3, 5), (4, 4), (5, 3), (6, 2), (BEGIN, 2), (INITIAL, 2), (7, 1),
     (NEAR1, 1))
    + tuple((EDGE + i, 1) for i in range(4)),
    ((0, 8), (1, 7), (2, 6), (3, 5), (4, 4), (5, 3), (6, 2), (NEAR1, 1), (NEAR2, 1)),
)
ROWS = ({NEAR1: 16, COEF: 32, BEGIN: 48, INITIAL: 64, **{EDGE + i: 80 + 16 * i for i in range(4)}}, {NEAR1: 16, NEAR2: 32})


def count(items, distance):
    return sum(1 for _, reach in items if reach >= distance)


def shares(core, ahead):
    if ahead == 0:
        return (0, 1), (2 - core, BLOCK - 1)
    if ahead > 0:
        return (0, 2 * ahead - core), (2, BLOCK - 1 - 2 * ahead + core)
    return (0, -2 * ahead + core - 1), (1, BLOCK + 2 * ahead - core)


def slots(items):
    return max(sum(count(items, least) for _, least in shares(core, a)) for core in (0, 1) for a in range(-3, 4))


def turn(x, by, axis):
    return pltpu.roll(x, by % x.shape[axis], axis)


def around(x):
    return turn(x, 1, 0) + turn(x, -1, 0) + turn(x, 1, 1) + turn(x, -1, 1)


def cubic(u):
    return u - u * u * u


def dot(a, b):
    return jnp.dot(a, b, precision=lax.Precision.HIGHEST, preferred_element_type=F32)


def pair_lanes():
    z = lax.broadcasted_iota(jnp.int32, (128, 128), 0)
    c = lax.broadcasted_iota(jnp.int32, (128, 128), 1)
    return jnp.where((z >> 1) == (c & 63), 1.0, 0.0).astype(F32)


def spread_lanes():
    c = lax.broadcasted_iota(jnp.int32, (128, 128), 0)
    z = lax.broadcasted_iota(jnp.int32, (128, 128), 1)
    return jnp.where((z >> 1) == c, 1.0, 0.0).astype(F32)


def squash(planes, scratch):
    for i, plane in enumerate(planes):
        scratch[64 * i : 64 * i + 64, :] = plane
    both = scratch[pl.ds(0, 32 * len(planes), 2), :] + scratch[pl.ds(1, 32 * len(planes), 2), :]
    sums = dot(both, pair_lanes())
    return [sums[32 * i : 32 * i + 32] for i in range(len(planes))]


def spread(planes, scratch):
    wide = dot(jnp.concatenate(planes, axis=0), spread_lanes())
    scratch[pl.ds(0, 32 * len(planes), 2), :] = wide
    scratch[pl.ds(1, 32 * len(planes), 2), :] = wide
    return [scratch[64 * i : 64 * i + 64, :] for i in range(len(planes))]


def left(shape):
    return lax.broadcasted_iota(jnp.int32, shape, 1) < 64


def pack(x):
    return jnp.where(left((16, 128)), x[:16], x[16:])


def unpack(t):
    other = turn(t, 64, 1)
    here = left((16, 128))
    return jnp.concatenate([jnp.where(here, t, other), jnp.where(here, other, t)], axis=0)


def coarse_slope(below, centre, above, coef):
    return 0.25 * (around(centre) + below + above - 6.0 * centre) + coef * cubic(centre)


def mix(row, nodes):
    return QUAD[row][0] * nodes[0] + QUAD[row][1] * nodes[1] + QUAD[row][2] * nodes[2]


def packets(spot, up, down, inner, outers):
    def put(to_inner, to_outer):
        whole = jnp.concatenate(to_outer, axis=0)
        half = whole.shape[0] // 2
        inner[...] = jnp.concatenate(to_inner, axis=0)
        outers[0][...] = whole[:half]
        outers[1][...] = whole[half:]

    @pl.when(spot[2] == 0)
    def _():
        put(up, down)

    @pl.when(spot[2] != 0)
    def _():
        put(down, up)


def sides(spot, inner, outer, outer_rest):
    low = jnp.full(inner.shape, spot[2], jnp.int32) == 0
    a, b = inner[...], jnp.concatenate([outer[...], outer_rest[...]], axis=0)
    return jnp.where(low, b, a), jnp.where(low, a, b)


def first_kernel(
    spot, initial, coeff, guess, inner, outer, outer_rest, keep, initial_out, coeff_out, guess_out, scratch
):
    for out, given in ((initial_out, initial), (coeff_out, coeff), (guess_out, guess)):
        out[...] = given[...]
    u = [guess[0], guess[1]]
    c = [coeff[0], coeff[1]]
    both = u[0] + u[1]
    total = around(both) - 5.0 * both + c[0] * cubic(u[0]) + c[1] * cubic(u[1])
    own, value, coef, start = squash([total, both, c[0] + c[1], initial[0] + initial[1]], scratch)
    value, coef, start = 0.125 * value, 0.125 * coef, 0.125 * start
    packets(spot, u + [c[1], pack(start)], u + [c[0], pack(start)], inner, [outer, outer_rest])
    keep[0] = own
    keep[1] = value
    keep[2] = coef
    keep[3] = start


def own_k(own, value0, value0_sides, coef):
    slope = coarse_slope(value0_sides[0], value0, value0_sides[1], coef)
    return [(STEP / 8.0) * own[m] - (STEP * QUAD[m + 1][0]) * slope for m in (0, 1)]


def complete_first(
    spot, inner, outer, outer_rest, kept, initial, received, owned, beside, beyond, mine, keep, begin_out, scratch
):
    below, above = sides(spot, inner, outer, outer_rest)
    begin = starting(spot, initial, received)
    own, value, coef, start = (kept[i] for i in range(4))
    low, high, value_low, value_high, value_begin = squash(
        [below[64:128, :], above[0:64, :], below[0:64, :] + below[64:128, :], above[0:64, :] + above[64:128, :],
         begin[0] + begin[1]],
        scratch,
    )
    value_low, value_high = 0.125 * value_low, 0.125 * value_high
    start_low, start_high = unpack(below[192:208, :]), unpack(above[192:208, :])
    start_slope = coarse_slope(start_low, start, start_high, coef)
    whole = own + low + high
    k = own_k([ROWSUM[1] * whole, ROWSUM[2] * whole], value, [value_low, value_high], coef)
    first = jnp.full((32, 128), spot[0], jnp.int32) == 0
    given = [pack(k[m - 1] + jnp.where(first, start + (STEP * QUAD[m][0]) * start_slope, 0.0)) for m in (2, 1)]
    given += [pack(coef), pack(0.125 * value_begin), pack(start)]
    mine[...] = given[0]
    odd = jnp.full((64, 128), spot[3], jnp.int32) == 1
    for i, part in enumerate(given):
        for out in (owned, beside, beyond):
            out[16 * i : 16 * i + 16, :] = part
    beside[80:144, :] = jnp.where(odd, begin[0], begin[1])
    beyond[80:144, :] = jnp.where(odd, begin[1], begin[0])
    for x in (0, 1):
        owned[80 + 64 * x : 144 + 64 * x, :] = begin[x]
        begin_out[x] = begin[x]
    for i, part in enumerate([k[0], k[1], start, start_slope, start_low, start_high, value_low, value_high]):
        keep[i] = part


def plane(spot, rows, owned, beside, beyond, sections, side, item, up=False):
    odd = spot[3]
    if item < SECTIONS:
        if side == 0:
            return sections[item, 0:16, :]
        at = jnp.where(odd == 1, side, 3 - side)
        return sections[item, pl.ds(pl.multiple_of(16 * at, 16), 16), :]
    row = rows[item]
    if side == 0:
        row += 64 if item >= EDGE and up else 0
        return owned[row : row + 16, :]
    near, far = beside[row : row + 16, :], beyond[row : row + 16, :]
    picked = jnp.full((16, 128), odd, jnp.int32) == (1 if side == 1 else 0)
    return jnp.where(picked, near, far)


def pack_kernel(items, rows):
    total = slots(items)

    def body(spot, owned, beside, beyond, sections, out):
        chip, core = spot[1], spot[2]

        def fill(own_core, away):
            slot = 0
            up = away > 0 or (away == 0 and own_core == 0)
            for side, least in shares(own_core, away):
                for item, reach in items:
                    if reach >= least:
                        part = plane(spot, rows, owned, beside, beyond, sections, side, item, up)
                        out[chip + away, 16 * slot : 16 * slot + 16, :] = part
                        slot += 1

        for own_core in (0, 1):
            for away in range(1 - CHIPS, CHIPS):
                there = jnp.logical_and(chip + away >= 0, chip + away < CHIPS)

                @pl.when(jnp.logical_and(core == own_core, there))
                def _():
                    fill(own_core, away)

    return body, total


def sweep(spot, items, rows, owned, beside, beyond, sections, windows, swapped, coefs, started, line, history):
    core = spot[2]
    place = 2 * spot[1] + core
    rank = {item: i for i, (item, _) in enumerate(items)}
    reach_of = dict(items)

    def fetch(item, w, whole=False):
        if w in (0, -BLOCK, BLOCK):
            side = {0: 0, -BLOCK: 1, BLOCK: 2}[w]
            return unpack(plane(spot, rows, owned, beside, beyond, sections, side, item))
        at = place + w
        if w > 0:
            outside, least = at >= BLOCK, [max(1, BLOCK - w - i) for i in (0, 1)]
        else:
            outside, least = at < 0, [max(1, BLOCK - 1 + w + i) for i in (0, 1)]
        before = jnp.where(core == 0, count(items, least[0]), count(items, least[1]))
        slot = rank[item] + jnp.where(outside, before, 0)
        source = windows if w % 2 == 0 else swapped
        found = source[(at & (BLOCK - 1)) >> 1, pl.ds(pl.multiple_of(16 * slot, 16), 16), :]
        return found if whole else unpack(found)

    if COEF in rank:
        for w in range(-7, 8):
            coefs[w + 7] = fetch(COEF, w)
    outermost = [fetch(INITIAL, w) if INITIAL in rank else jnp.zeros((32, 128), F32) for w in (-2, 2)]
    history[0] = outermost[0]
    history[1] = started[4]
    history[2] = started[2]
    history[3] = started[5]
    history[4] = outermost[1]
    for w in range(-8, 9):
        value = fetch(0, w)
        line[0, w + 8] = value
        if abs(w) <= 2:
            history[5 + w + 2] = value
    for k in range(1, SECTIONS):
        if k not in rank:
            continue
        old, new = (k - 1) % 2, k % 2
        for w in range(-reach_of[k], reach_of[k] + 1):
            centre = line[old, w + 8]
            slope = coarse_slope(line[old, w + 7], centre, line[old, w + 9], coefs[w + 7])
            value = centre + (STEP * QUAD[2][0]) * slope + fetch(k, w)
            line[new, w + 8] = value
            if abs(w) <= 2:
                history[5 * (k + 1) + w + 2] = value
    return fetch


def correct(spot, fetch, coefs, started, history, kept, values, nodes, below, above, coeff, begin, scratch):
    section = spot[0]
    s = [history[5 * section + i] for i in range(5)]
    slope = [coarse_slope(s[i], s[i + 1], s[i + 2], coefs[6 + i]) for i in range(3)]
    later = jnp.full((32, 128), section, jnp.int32) > 0
    edges = []
    for w, i in ((-1, 0), (1, 2)):
        for m, near in ((1, NEAR1), (2, NEAR2)):
            edges.append(fetch(near, w) + jnp.where(later, ROWSUM[m] * s[i + 1] + START[m] * slope[i], 0.0))
    coarse = [s[2]] + [s[2] + (STEP * QUAD[m][0]) * slope[1] + kept[m - 1] for m in (1, 2)]
    wide = spread([coarse[j] - values[j] for j in range(3)] + edges, scratch)
    fixed = [[nodes[j][x] + wide[j] for x in (0, 1)] for j in range(3)]
    rates = [[cubic(fixed[j][x]) for x in (0, 1)] for j in range(3)]
    fresh = []
    for m in (1, 2):
        sums = [mix(m, [fixed[j][x] for j in range(3)]) for x in (0, 1)]
        ends = [below[m - 1] + wide[2 + m], above[m - 1] + wide[4 + m]]
        fresh.append([])
        for x in (0, 1):
            change = around(sums[x]) - 6.0 * sums[x] + sums[1 - x] + ends[x]
            change = change + coeff[x] * mix(m, [rates[j][x] for j in range(3)])
            fresh[-1].append(begin[x] + STEP * change)
    return coarse[2], fresh


def starting(spot, initial, received):
    first = jnp.full((64, 128), spot[0], jnp.int32) == 0
    return [jnp.where(first, initial[x], received[x]) for x in (0, 1)]


def previous_end(section, fetch, coefs, history, starts, coeff, initial, earlier, scratch):
    before = jnp.maximum(section - 1, 0)
    s = [history[5 * before + i] for i in range(5)]
    value = [fetch(BEGIN, w) for w in range(-2, 3)]
    shift = []
    for i in range(3):
        two = history[5 * section + 1 + i]
        slope = coarse_slope(s[i], s[i + 1], s[i + 2], coefs[6 + i])
        slope = slope - coarse_slope(value[i], value[i + 1], value[i + 2], coefs[6 + i])
        one = 0.5 * (s[i + 1] + two) + (STEP * (QUAD[1][0] - 0.5 * QUAD[2][0])) * slope
        shift.append([s[i + 1] - value[i + 1], one - value[i + 1], two - value[i + 1]])
    wide = spread([mix(2, shift[0])] + shift[1] + [mix(2, shift[2])], scratch)
    fixed = [[starts[x] + wide[1 + j] for j in range(3)] for x in (1, 2)]
    sums = [ROWSUM[2] * starts[0] + wide[0], mix(2, fixed[0]), mix(2, fixed[1]), ROWSUM[2] * starts[3] + wide[4]]
    number = jnp.full((64, 128), section, jnp.int32)
    out = []
    for x in (0, 1):
        change = around(sums[x + 1]) - 6.0 * sums[x + 1] + sums[x] + sums[x + 2]
        change = change + coeff[x] * mix(2, [cubic(part) for part in fixed[x]])
        end = jnp.where(number == 1, initial[x], earlier[x]) + STEP * change
        out.append(jnp.where(number == 0, initial[x], end))
    return out


def finish_first(
    spot, owned, beside, beyond, sections, windows, swapped, started, kept, inner, outer, outer_rest, initial, coeff,
    guess, begin, earlier, middle_out, end_out, ends, begin_out, keep, owned_out, mine, coefs, line, history, scratch,
):
    fetch = sweep(
        spot, ITEMS[0], ROWS[0], owned, beside, beyond, sections, windows, swapped, coefs, started, line, history
    )
    below, above = sides(spot, inner, outer, outer_rest)
    section = spot[0]
    later = jnp.full((32, 128), section, jnp.int32) > 0
    s = [history[5 * section + i] for i in range(5)]
    slope = [coarse_slope(s[i], s[i + 1], s[i + 2], coefs[6 + i]) for i in range(3)]
    step = [s[i + 1] + (STEP * QUAD[1][0]) * slope[i] for i in range(3)]
    value = [started[6], kept[1], started[7]]
    coarse = []
    for i in range(3):
        if i == 1:
            one, two = step[1] + started[0], s[2] + (STEP * QUAD[2][0]) * slope[1] + started[1]
        else:
            one = fetch(NEAR1, i - 1) + jnp.where(later, step[i], 0.0)
            two = history[5 * section + 6 + i]
        coarse += [s[i + 1] - value[i], one - value[i], two - value[i]]
    wide = spread(coarse, scratch)
    u = [below[0:64, :], below[64:128, :], guess[0], guess[1], above[0:64, :], above[64:128, :]]
    c = [None, below[128:192, :], coeff[0], coeff[1], above[128:192, :], None]
    b = [None] + [None] * 4 + [None]
    b[2], b[3] = begin[0], begin[1]
    for x, w in ((1, -1), (4, 1)):
        b[x] = jnp.concatenate([fetch(EDGE + i, w, whole=True) for i in range(4)], axis=0)
    begin_next = previous_end(section, fetch, coefs, history, b[1:5], coeff, initial, earlier, scratch)
    for x in (0, 1):
        begin_out[x] = begin_next[x]
    fixed = [[u[x] + wide[3 * (x // 2) + j] for j in range(3)] for x in range(6)]
    nodes = [None] + [[b[x]] for x in range(1, 5)] + [None]
    rates = [None] + [[cubic(fixed[x][j]) for j in range(3)] for x in range(1, 5)] + [None]
    for m in (1, 2):
        sums = [mix(m, fixed[x]) for x in range(6)]
        for x in range(1, 5):
            change = around(sums[x]) - 6.0 * sums[x] + sums[x - 1] + sums[x + 1] + c[x] * mix(m, rates[x])
            nodes[x].append(b[x] + STEP * change)
    for x in (0, 1):
        middle_out[x] = nodes[x + 2][1]
        end_out[x] = nodes[x + 2][2]
    rates = [[cubic(nodes[x][j]) for j in range(3)] for x in (2, 3)]
    planes = []
    for m in (1, 2):
        sums = [mix(m, nodes[x]) for x in range(1, 5)]
        ends[m - 1] = sums[0]
        ends[m + 1] = sums[3]
        both = sums[1] + sums[2]
        planes.append(
            around(both) - 5.0 * both + sums[0] + sums[3] + c[2] * mix(m, rates[0]) + c[3] * mix(m, rates[1])
        )
    for j in range(3):
        planes.append(nodes[2][j] + nodes[3][j])
    small = squash(planes, scratch)
    values = [0.125 * small[2 + j] for j in range(3)]
    k = own_k(small[:2], values[0], [fetch(BEGIN, -1), fetch(BEGIN, 1)], kept[2])
    first = jnp.logical_not(later)
    ours = pack(k[1] + jnp.where(first, started[2] + (STEP * QUAD[2][0]) * started[3], 0.0))
    owned_out[0:16, :] = ours
    mine[...] = ours
    for m in (1, 2):
        near = QUAD[m][1] * k[0] + QUAD[m][2] * k[1] - mix(m, values)
        near = near + jnp.where(first, ROWSUM[m] * started[2] + START[m] * started[3], 0.0)
        owned_out[16 * m : 16 * m + 16, :] = pack(near)
    for i, part in enumerate(values + k):
        keep[i] = part


def finish_second(
    spot, owned, beside, beyond, sections, windows, swapped, started, kept, ends, coeff, begin_in, middle_in, end_in,
    begin, coefs, fresh_out, coarse_out, line, history, scratch,
):
    fetch = sweep(
        spot, ITEMS[1], ROWS[1], owned, beside, beyond, sections, windows, swapped, coefs, started, line, history
    )
    nodes = [[part[0], part[1]] for part in (begin_in, middle_in, end_in)]
    end, fresh = correct(
        spot, fetch, coefs, started, history, (kept[3], kept[4]), [kept[0], kept[1], kept[2]], nodes,
        [ends[0], ends[1]], [ends[2], ends[3]], [coeff[0], coeff[1]], [begin[0], begin[1]], scratch,
    )
    for m in (0, 1):
        for x in (0, 1):
            fresh_out[m, x] = fresh[m][x]
    coarse_out[...] = end[:, :64]


def run(body, args, outs, scratch=(), name=None, first=False, last=False):
    def placed(*refs):
        spot = [lax.axis_index(a) for a in ("tm", "chip", "core", "block")]
        body(spot[:3] + [spot[3] & 1], *refs)

    return pl.pallas_call(
        placed,
        out_shape=[jax.ShapeDtypeStruct(shape, F32) if last else pltpu.VMEM(shape, F32) for shape in outs],
        in_specs=[pl.BlockSpec(memory_space=pltpu.VMEM)] * len(args),
        out_specs=[pl.BlockSpec(memory_space=pltpu.VMEM)] * len(outs),
        scratch_shapes=[pltpu.VMEM(shape, F32) for shape in scratch],
        compiler_params=None if first else pltpu.CompilerParams(vmem_limit_bytes=16 << 20),
        name=name,
    )(*(a if first else pltpu.with_memory_space_constraint(a, pltpu.VMEM) for a in args))


class Links:
    call = staticmethod(run)

    @staticmethod
    def swap_block(x, row):
        n = lax.axis_size("block")
        pairs = [(i, i ^ 1 if row else (i + 2 * (i % 2) - 1) % n) for i in range(n)]
        return lax.ppermute(x, "block", pairs)

    @staticmethod
    def swap_inner(x):
        return lax.ppermute(x, "core", [(0, 1), (1, 0)])

    @staticmethod
    def swap_outer(x):
        n = lax.axis_size("block") * BLOCK
        return lax.ppermute(x, ("block", "chip", "core"), [(i, (i + 2 * (i % 2) - 1) % n) for i in range(n)])

    @staticmethod
    def onward(x, by):
        n = lax.axis_size("tm")
        return lax.ppermute(x, "tm", [(i, i + by) for i in range(n - by)])

    @staticmethod
    def sections(x):
        return lax.all_to_all(jnp.broadcast_to(x, (SECTIONS,) + x.shape), "tm", 0, 0)

    @staticmethod
    def block(x):
        return lax.all_to_all(x, "chip", 0, 0)

    @staticmethod
    def together(*values):
        return lax.optimization_barrier(values)

    @staticmethod
    def stack(*planes):
        return jnp.concatenate([p[:16] for p in planes], axis=0)


def iterate(links, initial, coeff, guess):
    coarse, slab = (32, 128), (2, 64, 128)
    work = [(2, 17) + coarse, (45,) + coarse]

    def windows(owned, beside, beyond, mine, iteration):
        sections = links.sections(links.stack(mine, beside, beyond))
        body, total = pack_kernel(ITEMS[iteration], ROWS[iteration])
        (parcels,) = links.call(
            body, (owned, beside, beyond, sections), [(CHIPS, 16 * total, 128)], name="hand_out"
        )
        parcels = links.block(parcels)
        return owned, beside, beyond, sections, parcels, links.swap_inner(parcels)

    sent = guess
    inner, outer, outer_rest, kept, initial, coeff, guess = links.call(
        first_kernel, (initial, coeff, guess),
        [(208, 128), (104, 128), (104, 128), (4,) + coarse, slab, slab, slab], [(256, 128)], name="first", first=True,
    )
    inner, outer, outer_rest, received, earlier = links.together(
        links.swap_inner(inner), links.swap_outer(outer), links.swap_outer(outer_rest), links.onward(sent, 1),
        links.onward(sent, 2),
    )
    owned, beside, beyond, mine, started, begin = links.call(
        complete_first, (inner, outer, outer_rest, kept, initial, received),
        [(208, 128), (144, 128), (144, 128), (16, 128), (8,) + coarse, slab], [(320, 128)], name="complete_first",
    )
    beside, beyond = links.swap_block(beside, True), links.swap_block(beyond, False)
    middle, end, ends, begin_next, kept, owned, mine, coefs = links.call(
        finish_first,
        (*windows(owned, beside, beyond, mine, 0), started, kept, inner, outer, outer_rest, initial, coeff, guess, begin,
         earlier),
        [slab, slab, (4, 64, 128), slab, (5,) + coarse, (48, 128), (16, 128), (15,) + coarse],
        work + [(576, 128)],
        name="finish_first",
    )
    beside, beyond = links.swap_block(owned, True), links.swap_block(owned, False)
    fine, coarse_end = links.call(
        finish_second,
        (*windows(owned, beside, beyond, mine, 1), started, kept, ends, coeff, begin, middle, end, begin_next, coefs),
        [(2, 2, 64, 128), (32, 64)],
        work + [(448, 128)],
        name="finish_second",
        last=True,
    )
    return fine, coarse_end


def on_device(initial, coeff, guess):
    fine, coarse_end = iterate(Links, initial, coeff, guess[0])
    return fine[None], coarse_end[None, None]


def solution(mesh):
    split = Mesh(
        mesh.devices.reshape(mesh.shape["tm"], mesh.shape["space"] // BLOCK, CHIPS, 2), ("tm", "block", "chip", "core")
    )
    space = ("block", "chip", "core")
    return jax.shard_map(
        on_device,
        mesh=split,
        in_specs=(P(space, None, None), P(space, None, None), P("tm", space, None, None)),
        out_specs=(P("tm", None, space, None, None), P("tm", space, None, None)),
        check_vma=False,
    )
```

```python
import jax
import jax.numpy as jnp
from jax import lax
from jax.experimental import pallas as pl
from jax.experimental.pallas import tpu as pltpu
from jax.sharding import Mesh, PartitionSpec as P

STEP = 0.06
QUAD = ((0.0, 0.0, 0.0), (5.0 / 24.0, 1.0 / 3.0, -1.0 / 24.0), (1.0 / 6.0, 2.0 / 3.0, 1.0 / 6.0))
ROWSUM = tuple(sum(row) for row in QUAD)
START = tuple(STEP * (row[1] * QUAD[1][0] + row[2] * QUAD[2][0]) for row in QUAD)
SECTIONS = 8
BLOCK = 8
CHIPS = BLOCK // 2
F32 = jnp.float32

COEF, NEAR1, NEAR2, BEGIN, INITIAL, EDGE = 10, 11, 12, 13, 14, 15
ITEMS = (
    ((0, 8), (1, 7), (COEF, 7), (2, 6), (3, 5), (4, 4), (5, 3), (6, 2), (BEGIN, 2), (INITIAL, 2), (7, 1),
     (NEAR1, 1))
    + tuple((EDGE + i, 1) for i in range(4)),
    ((0, 8), (1, 7), (2, 6), (3, 5), (4, 4), (5, 3), (6, 2), (NEAR1, 1), (NEAR2, 1)),
)
ROWS = ({NEAR1: 16, COEF: 32, BEGIN: 48, INITIAL: 64, **{EDGE + i: 80 + 16 * i for i in range(4)}}, {NEAR1: 16, NEAR2: 32})


def count(items, distance):
    return sum(1 for _, reach in items if reach >= distance)


def shares(core, ahead):
    if ahead == 0:
        return (0, 1), (2 - core, BLOCK - 1)
    if ahead > 0:
        return (0, 2 * ahead - core), (2, BLOCK - 1 - 2 * ahead + core)
    return (0, -2 * ahead + core - 1), (1, BLOCK + 2 * ahead - core)


def slots(items):
    return max(sum(count(items, least) for _, least in shares(core, a)) for core in (0, 1) for a in range(-3, 4))


def turn(x, by, axis):
    return pltpu.roll(x, by % x.shape[axis], axis)


def around(x):
    return turn(x, 1, 0) + turn(x, -1, 0) + turn(x, 1, 1) + turn(x, -1, 1)


def cubic(u):
    return u - u * u * u


def dot(a, b):
    return jnp.dot(a, b, precision=lax.Precision.HIGHEST, preferred_element_type=F32)


def pair_lanes():
    z = lax.broadcasted_iota(jnp.int32, (128, 128), 0)
    c = lax.broadcasted_iota(jnp.int32, (128, 128), 1)
    return jnp.where((z >> 1) == (c & 63), 1.0, 0.0).astype(F32)


def spread_lanes():
    c = lax.broadcasted_iota(jnp.int32, (128, 128), 0)
    z = lax.broadcasted_iota(jnp.int32, (128, 128), 1)
    return jnp.where((z >> 1) == c, 1.0, 0.0).astype(F32)


def squash(planes, scratch):
    for i, plane in enumerate(planes):
        scratch[64 * i : 64 * i + 64, :] = plane
    both = scratch[pl.ds(0, 32 * len(planes), 2), :] + scratch[pl.ds(1, 32 * len(planes), 2), :]
    sums = dot(both, pair_lanes())
    return [sums[32 * i : 32 * i + 32] for i in range(len(planes))]


def spread(planes, scratch):
    wide = dot(jnp.concatenate(planes, axis=0), spread_lanes())
    scratch[pl.ds(0, 32 * len(planes), 2), :] = wide
    scratch[pl.ds(1, 32 * len(planes), 2), :] = wide
    return [scratch[64 * i : 64 * i + 64, :] for i in range(len(planes))]


def left(shape):
    return lax.broadcasted_iota(jnp.int32, shape, 1) < 64


def pack(x):
    return jnp.where(left((16, 128)), x[:16], x[16:])


def unpack(t):
    other = turn(t, 64, 1)
    here = left((16, 128))
    return jnp.concatenate([jnp.where(here, t, other), jnp.where(here, other, t)], axis=0)


def coarse_slope(below, centre, above, coef):
    return 0.25 * (around(centre) + below + above - 6.0 * centre) + coef * cubic(centre)


def mix(row, nodes):
    return QUAD[row][0] * nodes[0] + QUAD[row][1] * nodes[1] + QUAD[row][2] * nodes[2]


def packets(spot, up, down, inners, outers):
    def put(to_inner, to_outer):
        for parts, outs in ((to_inner, inners), (to_outer, outers)):
            whole = jnp.concatenate(parts, axis=0)
            half = whole.shape[0] // 2
            outs[0][...] = whole[:half]
            outs[1][...] = whole[half:]

    @pl.when(spot[2] == 0)
    def _():
        put(up, down)

    @pl.when(spot[2] != 0)
    def _():
        put(down, up)


def sides(spot, inner, inner_rest, outer, outer_rest):
    a = jnp.concatenate([inner[...], inner_rest[...]], axis=0)
    b = jnp.concatenate([outer[...], outer_rest[...]], axis=0)
    low = jnp.full(a.shape, spot[2], jnp.int32) == 0
    return jnp.where(low, b, a), jnp.where(low, a, b)


def first_kernel(
    spot, initial, coeff, guess, inner, inner_rest, outer, outer_rest, keep, initial_out, coeff_out, guess_out, scratch
):
    for out, given in ((initial_out, initial), (coeff_out, coeff), (guess_out, guess)):
        out[...] = given[...]
    u = [guess[0], guess[1]]
    c = [coeff[0], coeff[1]]
    both = u[0] + u[1]
    total = around(both) - 5.0 * both + c[0] * cubic(u[0]) + c[1] * cubic(u[1])
    own, value, coef, start = squash([total, both, c[0] + c[1], initial[0] + initial[1]], scratch)
    value, coef, start = 0.125 * value, 0.125 * coef, 0.125 * start
    packets(spot, u + [c[1], pack(start)], u + [c[0], pack(start)], [inner, inner_rest], [outer, outer_rest])
    keep[0] = own
    keep[1] = value
    keep[2] = coef
    keep[3] = start


def own_k(own, value0, value0_sides, coef):
    slope = coarse_slope(value0_sides[0], value0, value0_sides[1], coef)
    return [(STEP / 8.0) * own[m] - (STEP * QUAD[m + 1][0]) * slope for m in (0, 1)]


def complete_first(
    spot, inner, inner_rest, outer, outer_rest, kept, initial, received, owned, beside, beyond, mine, keep, begin_out,
    scratch,
):
    below, above = sides(spot, inner, inner_rest, outer, outer_rest)
    begin = starting(spot, initial, received)
    own, value, coef, start = (kept[i] for i in range(4))
    low, high, value_low, value_high, value_begin = squash(
        [below[64:128, :], above[0:64, :], below[0:64, :] + below[64:128, :], above[0:64, :] + above[64:128, :],
         begin[0] + begin[1]],
        scratch,
    )
    value_low, value_high = 0.125 * value_low, 0.125 * value_high
    start_low, start_high = unpack(below[192:208, :]), unpack(above[192:208, :])
    start_slope = coarse_slope(start_low, start, start_high, coef)
    whole = own + low + high
    k = own_k([ROWSUM[1] * whole, ROWSUM[2] * whole], value, [value_low, value_high], coef)
    first = jnp.full((32, 128), spot[0], jnp.int32) == 0
    given = [pack(k[m - 1] + jnp.where(first, start + (STEP * QUAD[m][0]) * start_slope, 0.0)) for m in (2, 1)]
    given += [pack(coef), pack(0.125 * value_begin), pack(start)]
    mine[...] = given[0]
    odd = jnp.full((64, 128), spot[3], jnp.int32) == 1
    for i, part in enumerate(given):
        for out in (owned, beside, beyond):
            out[16 * i : 16 * i + 16, :] = part
    beside[80:144, :] = jnp.where(odd, begin[0], begin[1])
    beyond[80:144, :] = jnp.where(odd, begin[1], begin[0])
    for x in (0, 1):
        owned[80 + 64 * x : 144 + 64 * x, :] = begin[x]
        begin_out[x] = begin[x]
    for i, part in enumerate([k[0], k[1], start, start_slope, start_low, start_high, value_low, value_high]):
        keep[i] = part


def plane(spot, rows, owned, beside, beyond, sections, side, item, up=False):
    odd = spot[3]
    if item < SECTIONS:
        if side == 0:
            return sections[item, 0:16, :]
        at = jnp.where(odd == 1, side, 3 - side)
        return sections[item, pl.ds(pl.multiple_of(16 * at, 16), 16), :]
    row = rows[item]
    if side == 0:
        row += 64 if item >= EDGE and up else 0
        return owned[row : row + 16, :]
    near, far = beside[row : row + 16, :], beyond[row : row + 16, :]
    picked = jnp.full((16, 128), odd, jnp.int32) == (1 if side == 1 else 0)
    return jnp.where(picked, near, far)


def pack_kernel(items, rows):
    total = slots(items)

    def body(spot, owned, beside, beyond, sections, out):
        chip, core = spot[1], spot[2]

        def fill(own_core, away):
            slot = 0
            up = away > 0 or (away == 0 and own_core == 0)
            for side, least in shares(own_core, away):
                for item, reach in items:
                    if reach >= least:
                        part = plane(spot, rows, owned, beside, beyond, sections, side, item, up)
                        out[chip + away, 16 * slot : 16 * slot + 16, :] = part
                        slot += 1

        for own_core in (0, 1):
            for away in range(1 - CHIPS, CHIPS):
                there = jnp.logical_and(chip + away >= 0, chip + away < CHIPS)

                @pl.when(jnp.logical_and(core == own_core, there))
                def _():
                    fill(own_core, away)

    return body, total


def sweep(spot, items, rows, owned, beside, beyond, sections, windows, swapped, coefs, started, line, history):
    core = spot[2]
    place = 2 * spot[1] + core
    rank = {item: i for i, (item, _) in enumerate(items)}
    reach_of = dict(items)

    def fetch(item, w, whole=False):
        if w in (0, -BLOCK, BLOCK):
            side = {0: 0, -BLOCK: 1, BLOCK: 2}[w]
            return unpack(plane(spot, rows, owned, beside, beyond, sections, side, item))
        at = place + w
        if w > 0:
            outside, least = at >= BLOCK, [max(1, BLOCK - w - i) for i in (0, 1)]
        else:
            outside, least = at < 0, [max(1, BLOCK - 1 + w + i) for i in (0, 1)]
        before = jnp.where(core == 0, count(items, least[0]), count(items, least[1]))
        slot = rank[item] + jnp.where(outside, before, 0)
        source = windows if w % 2 == 0 else swapped
        found = source[(at & (BLOCK - 1)) >> 1, pl.ds(pl.multiple_of(16 * slot, 16), 16), :]
        return found if whole else unpack(found)

    if COEF in rank:
        for w in range(-7, 8):
            coefs[w + 7] = fetch(COEF, w)
    outermost = [fetch(INITIAL, w) if INITIAL in rank else jnp.zeros((32, 128), F32) for w in (-2, 2)]
    history[0] = outermost[0]
    history[1] = started[4]
    history[2] = started[2]
    history[3] = started[5]
    history[4] = outermost[1]
    for w in range(-8, 9):
        value = fetch(0, w)
        line[0, w + 8] = value
        if abs(w) <= 2:
            history[5 + w + 2] = value
    for k in range(1, SECTIONS):
        if k not in rank:
            continue
        old, new = (k - 1) % 2, k % 2
        for w in range(-reach_of[k], reach_of[k] + 1):
            centre = line[old, w + 8]
            slope = coarse_slope(line[old, w + 7], centre, line[old, w + 9], coefs[w + 7])
            value = centre + (STEP * QUAD[2][0]) * slope + fetch(k, w)
            line[new, w + 8] = value
            if abs(w) <= 2:
                history[5 * (k + 1) + w + 2] = value
    return fetch


def correct(spot, fetch, coefs, started, history, kept, values, nodes, below, above, coeff, begin, scratch):
    section = spot[0]
    s = [history[5 * section + i] for i in range(5)]
    slope = [coarse_slope(s[i], s[i + 1], s[i + 2], coefs[6 + i]) for i in range(3)]
    later = jnp.full((32, 128), section, jnp.int32) > 0
    edges = []
    for w, i in ((-1, 0), (1, 2)):
        for m, near in ((1, NEAR1), (2, NEAR2)):
            edges.append(fetch(near, w) + jnp.where(later, ROWSUM[m] * s[i + 1] + START[m] * slope[i], 0.0))
    coarse = [s[2]] + [s[2] + (STEP * QUAD[m][0]) * slope[1] + kept[m - 1] for m in (1, 2)]
    wide = spread([coarse[j] - values[j] for j in range(3)] + edges, scratch)
    fixed = [[nodes[j][x] + wide[j] for x in (0, 1)] for j in range(3)]
    rates = [[cubic(fixed[j][x]) for x in (0, 1)] for j in range(3)]
    fresh = []
    for m in (1, 2):
        sums = [mix(m, [fixed[j][x] for j in range(3)]) for x in (0, 1)]
        ends = [below[m - 1] + wide[2 + m], above[m - 1] + wide[4 + m]]
        fresh.append([])
        for x in (0, 1):
            change = around(sums[x]) - 6.0 * sums[x] + sums[1 - x] + ends[x]
            change = change + coeff[x] * mix(m, [rates[j][x] for j in range(3)])
            fresh[-1].append(begin[x] + STEP * change)
    return coarse[2], fresh


def starting(spot, initial, received):
    first = jnp.full((64, 128), spot[0], jnp.int32) == 0
    return [jnp.where(first, initial[x], received[x]) for x in (0, 1)]


def previous_end(section, fetch, coefs, history, starts, coeff, initial, earlier, scratch):
    before = jnp.maximum(section - 1, 0)
    s = [history[5 * before + i] for i in range(5)]
    value = [fetch(BEGIN, w) for w in range(-2, 3)]
    shift = []
    for i in range(3):
        two = history[5 * section + 1 + i]
        slope = coarse_slope(s[i], s[i + 1], s[i + 2], coefs[6 + i])
        slope = slope - coarse_slope(value[i], value[i + 1], value[i + 2], coefs[6 + i])
        one = 0.5 * (s[i + 1] + two) + (STEP * (QUAD[1][0] - 0.5 * QUAD[2][0])) * slope
        shift.append([s[i + 1] - value[i + 1], one - value[i + 1], two - value[i + 1]])
    wide = spread([mix(2, shift[0])] + shift[1] + [mix(2, shift[2])], scratch)
    fixed = [[starts[x] + wide[1 + j] for j in range(3)] for x in (1, 2)]
    sums = [ROWSUM[2] * starts[0] + wide[0], mix(2, fixed[0]), mix(2, fixed[1]), ROWSUM[2] * starts[3] + wide[4]]
    number = jnp.full((64, 128), section, jnp.int32)
    out = []
    for x in (0, 1):
        change = around(sums[x + 1]) - 6.0 * sums[x + 1] + sums[x] + sums[x + 2]
        change = change + coeff[x] * mix(2, [cubic(part) for part in fixed[x]])
        end = jnp.where(number == 1, initial[x], earlier[x]) + STEP * change
        out.append(jnp.where(number == 0, initial[x], end))
    return out


def finish_first(
    spot, owned, beside, beyond, sections, windows, swapped, started, kept, inner, inner_rest, outer, outer_rest,
    initial, coeff, guess, begin, earlier, middle_out, end_out, ends, begin_out, keep, owned_out, mine, coefs, line, history, scratch,
):
    fetch = sweep(
        spot, ITEMS[0], ROWS[0], owned, beside, beyond, sections, windows, swapped, coefs, started, line, history
    )
    below, above = sides(spot, inner, inner_rest, outer, outer_rest)
    section = spot[0]
    later = jnp.full((32, 128), section, jnp.int32) > 0
    s = [history[5 * section + i] for i in range(5)]
    slope = [coarse_slope(s[i], s[i + 1], s[i + 2], coefs[6 + i]) for i in range(3)]
    step = [s[i + 1] + (STEP * QUAD[1][0]) * slope[i] for i in range(3)]
    value = [started[6], kept[1], started[7]]
    coarse = []
    for i in range(3):
        if i == 1:
            one, two = step[1] + started[0], s[2] + (STEP * QUAD[2][0]) * slope[1] + started[1]
        else:
            one = fetch(NEAR1, i - 1) + jnp.where(later, step[i], 0.0)
            two = history[5 * section + 6 + i]
        coarse += [s[i + 1] - value[i], one - value[i], two - value[i]]
    wide = spread(coarse, scratch)
    u = [below[0:64, :], below[64:128, :], guess[0], guess[1], above[0:64, :], above[64:128, :]]
    c = [None, below[128:192, :], coeff[0], coeff[1], above[128:192, :], None]
    b = [None] + [None] * 4 + [None]
    b[2], b[3] = begin[0], begin[1]
    for x, w in ((1, -1), (4, 1)):
        b[x] = jnp.concatenate([fetch(EDGE + i, w, whole=True) for i in range(4)], axis=0)
    begin_next = previous_end(section, fetch, coefs, history, b[1:5], coeff, initial, earlier, scratch)
    for x in (0, 1):
        begin_out[x] = begin_next[x]
    fixed = [[u[x] + wide[3 * (x // 2) + j] for j in range(3)] for x in range(6)]
    nodes = [None] + [[b[x]] for x in range(1, 5)] + [None]
    rates = [None] + [[cubic(fixed[x][j]) for j in range(3)] for x in range(1, 5)] + [None]
    for m in (1, 2):
        sums = [mix(m, fixed[x]) for x in range(6)]
        for x in range(1, 5):
            change = around(sums[x]) - 6.0 * sums[x] + sums[x - 1] + sums[x + 1] + c[x] * mix(m, rates[x])
            nodes[x].append(b[x] + STEP * change)
    for x in (0, 1):
        middle_out[x] = nodes[x + 2][1]
        end_out[x] = nodes[x + 2][2]
    rates = [[cubic(nodes[x][j]) for j in range(3)] for x in (2, 3)]
    planes = []
    for m in (1, 2):
        sums = [mix(m, nodes[x]) for x in range(1, 5)]
        ends[m - 1] = sums[0]
        ends[m + 1] = sums[3]
        both = sums[1] + sums[2]
        planes.append(
            around(both) - 5.0 * both + sums[0] + sums[3] + c[2] * mix(m, rates[0]) + c[3] * mix(m, rates[1])
        )
    for j in range(3):
        planes.append(nodes[2][j] + nodes[3][j])
    small = squash(planes, scratch)
    values = [0.125 * small[2 + j] for j in range(3)]
    k = own_k(small[:2], values[0], [fetch(BEGIN, -1), fetch(BEGIN, 1)], kept[2])
    first = jnp.logical_not(later)
    ours = pack(k[1] + jnp.where(first, started[2] + (STEP * QUAD[2][0]) * started[3], 0.0))
    owned_out[0:16, :] = ours
    mine[...] = ours
    for m in (1, 2):
        near = QUAD[m][1] * k[0] + QUAD[m][2] * k[1] - mix(m, values)
        near = near + jnp.where(first, ROWSUM[m] * started[2] + START[m] * started[3], 0.0)
        owned_out[16 * m : 16 * m + 16, :] = pack(near)
    for i, part in enumerate(values + k):
        keep[i] = part


def finish_second(
    spot, owned, beside, beyond, sections, windows, swapped, started, kept, ends, coeff, begin_in, middle_in, end_in,
    begin, coefs, fresh_out, coarse_out, line, history, scratch,
):
    fetch = sweep(
        spot, ITEMS[1], ROWS[1], owned, beside, beyond, sections, windows, swapped, coefs, started, line, history
    )
    nodes = [[part[0], part[1]] for part in (begin_in, middle_in, end_in)]
    end, fresh = correct(
        spot, fetch, coefs, started, history, (kept[3], kept[4]), [kept[0], kept[1], kept[2]], nodes,
        [ends[0], ends[1]], [ends[2], ends[3]], [coeff[0], coeff[1]], [begin[0], begin[1]], scratch,
    )
    for m in (0, 1):
        for x in (0, 1):
            fresh_out[m, x] = fresh[m][x]
    coarse_out[...] = end[:, :64]


def run(body, args, outs, scratch=(), name=None, first=False, last=False):
    def placed(*refs):
        spot = [lax.axis_index(a) for a in ("tm", "chip", "core", "block")]
        body(spot[:3] + [spot[3] & 1], *refs)

    return pl.pallas_call(
        placed,
        out_shape=[jax.ShapeDtypeStruct(shape, F32) if last else pltpu.VMEM(shape, F32) for shape in outs],
        in_specs=[pl.BlockSpec(memory_space=pltpu.VMEM)] * len(args),
        out_specs=[pl.BlockSpec(memory_space=pltpu.VMEM)] * len(outs),
        scratch_shapes=[pltpu.VMEM(shape, F32) for shape in scratch],
        compiler_params=None if first else pltpu.CompilerParams(vmem_limit_bytes=16 << 20),
        name=name,
    )(*(a if first else pltpu.with_memory_space_constraint(a, pltpu.VMEM) for a in args))


class Links:
    call = staticmethod(run)

    @staticmethod
    def swap_block(x, row):
        n = lax.axis_size("block")
        pairs = [(i, i ^ 1 if row else (i + 2 * (i % 2) - 1) % n) for i in range(n)]
        return lax.ppermute(x, "block", pairs)

    @staticmethod
    def swap_inner(x):
        return lax.ppermute(x, "core", [(0, 1), (1, 0)])

    @staticmethod
    def swap_outer(x):
        n = lax.axis_size("block") * BLOCK
        return lax.ppermute(x, ("block", "chip", "core"), [(i, (i + 2 * (i % 2) - 1) % n) for i in range(n)])

    @staticmethod
    def onward(x, by):
        n = lax.axis_size("tm")
        return lax.ppermute(x, "tm", [(i, i + by) for i in range(n - by)])

    @staticmethod
    def sections(x):
        return lax.all_to_all(jnp.broadcast_to(x, (SECTIONS,) + x.shape), "tm", 0, 0)

    @staticmethod
    def block(x):
        return lax.all_to_all(x, "chip", 0, 0)

    @staticmethod
    def together(*values):
        return lax.optimization_barrier(values)

    @staticmethod
    def stack(*planes):
        return jnp.concatenate([p[:16] for p in planes], axis=0)


def iterate(links, initial, coeff, guess):
    coarse, slab = (32, 128), (2, 64, 128)
    work = [(2, 17) + coarse, (45,) + coarse]

    def windows(owned, beside, beyond, mine, iteration):
        sections = links.sections(links.stack(mine, beside, beyond))
        body, total = pack_kernel(ITEMS[iteration], ROWS[iteration])
        (parcels,) = links.call(
            body, (owned, beside, beyond, sections), [(CHIPS, 16 * total, 128)], name="hand_out"
        )
        parcels = links.block(parcels)
        return owned, beside, beyond, sections, parcels, links.swap_inner(parcels)

    sent = guess
    inner, inner_rest, outer, outer_rest, kept, initial, coeff, guess = links.call(
        first_kernel, (initial, coeff, guess),
        [(104, 128)] * 4 + [(4,) + coarse, slab, slab, slab], [(256, 128)], name="first", first=True,
    )
    outer, outer_rest, inner, inner_rest, received = links.together(
        links.swap_outer(outer), links.swap_outer(outer_rest), links.swap_inner(inner), links.swap_inner(inner_rest),
        links.onward(sent, 1),
    )
    owned, beside, beyond, mine, started, begin = links.call(
        complete_first, (inner, inner_rest, outer, outer_rest, kept, initial, received),
        [(208, 128), (144, 128), (144, 128), (16, 128), (8,) + coarse, slab], [(320, 128)], name="complete_first",
    )
    beside, beyond, earlier = links.together(
        links.swap_block(beside, True), links.swap_block(beyond, False), links.onward(sent, 2)
    )
    middle, end, ends, begin_next, kept, owned, mine, coefs = links.call(
        finish_first,
        (*windows(owned, beside, beyond, mine, 0), started, kept, inner, inner_rest, outer, outer_rest, initial,
         coeff, guess, begin, earlier),
        [slab, slab, (4, 64, 128), slab, (5,) + coarse, (48, 128), (16, 128), (15,) + coarse],
        work + [(576, 128)],
        name="finish_first",
    )
    beside, beyond = links.swap_block(owned, True), links.swap_block(owned, False)
    fine, coarse_end = links.call(
        finish_second,
        (*windows(owned, beside, beyond, mine, 1), started, kept, ends, coeff, begin, middle, end, begin_next, coefs),
        [(2, 2, 64, 128), (32, 64)],
        work + [(448, 128)],
        name="finish_second",
        last=True,
    )
    return fine, coarse_end


def on_device(initial, coeff, guess):
    fine, coarse_end = iterate(Links, initial, coeff, guess[0])
    return fine[None], coarse_end[None, None]


def solution(mesh):
    split = Mesh(
        mesh.devices.reshape(mesh.shape["tm"], mesh.shape["space"] // BLOCK, CHIPS, 2), ("tm", "block", "chip", "core")
    )
    space = ("block", "chip", "core")
    return jax.shard_map(
        on_device,
        mesh=split,
        in_specs=(P(space, None, None), P(space, None, None), P("tm", space, None, None)),
        out_specs=(P("tm", None, space, None, None), P("tm", space, None, None)),
        check_vma=False,
    )
```

```python
import jax
import jax.numpy as jnp
from jax import lax
from jax.experimental import pallas as pl
from jax.experimental.pallas import tpu as pltpu
from jax.sharding import Mesh, PartitionSpec as P

STEP = 0.06
QUAD = ((0.0, 0.0, 0.0), (5.0 / 24.0, 1.0 / 3.0, -1.0 / 24.0), (1.0 / 6.0, 2.0 / 3.0, 1.0 / 6.0))
ROWSUM = tuple(sum(row) for row in QUAD)
START = tuple(STEP * (row[1] * QUAD[1][0] + row[2] * QUAD[2][0]) for row in QUAD)
SECTIONS = 8
BLOCK = 8
CHIPS = BLOCK // 2
F32 = jnp.float32

COEF, NEAR1, NEAR2, BEGIN, INITIAL, EDGE = 10, 11, 12, 13, 14, 15
ITEMS = (
    ((0, 8), (1, 7), (COEF, 7), (2, 6), (3, 5), (4, 4), (5, 3), (6, 2), (BEGIN, 2), (INITIAL, 2), (7, 1),
     (NEAR1, 1))
    + tuple((EDGE + i, 1) for i in range(4)),
    ((0, 8), (1, 7), (2, 6), (3, 5), (4, 4), (5, 3), (6, 2), (NEAR1, 1), (NEAR2, 1)),
)
ROWS = ({NEAR1: 16, COEF: 32, BEGIN: 48, INITIAL: 64, **{EDGE + i: 80 + 16 * i for i in range(4)}}, {NEAR1: 16, NEAR2: 32})


def count(items, distance):
    return sum(1 for _, reach in items if reach >= distance)


def shares(core, ahead):
    if ahead == 0:
        return (0, 1), (2 - core, BLOCK - 1)
    if ahead > 0:
        return (0, 2 * ahead - core), (2, BLOCK - 1 - 2 * ahead + core)
    return (0, -2 * ahead + core - 1), (1, BLOCK + 2 * ahead - core)


def slots(items):
    return max(sum(count(items, least) for _, least in shares(core, a)) for core in (0, 1) for a in range(-3, 4))


def turn(x, by, axis):
    return pltpu.roll(x, by % x.shape[axis], axis)


def around(x):
    return turn(x, 1, 0) + turn(x, -1, 0) + turn(x, 1, 1) + turn(x, -1, 1)


def cubic(u):
    return u - u * u * u


def dot(a, b):
    return jnp.dot(a, b, precision=lax.Precision.HIGHEST, preferred_element_type=F32)


def pair_lanes():
    z = lax.broadcasted_iota(jnp.int32, (128, 128), 0)
    c = lax.broadcasted_iota(jnp.int32, (128, 128), 1)
    return jnp.where((z >> 1) == (c & 63), 1.0, 0.0).astype(F32)


def spread_lanes():
    c = lax.broadcasted_iota(jnp.int32, (128, 128), 0)
    z = lax.broadcasted_iota(jnp.int32, (128, 128), 1)
    return jnp.where((z >> 1) == c, 1.0, 0.0).astype(F32)


def squash(planes, scratch):
    for i, plane in enumerate(planes):
        scratch[64 * i : 64 * i + 64, :] = plane
    both = scratch[pl.ds(0, 32 * len(planes), 2), :] + scratch[pl.ds(1, 32 * len(planes), 2), :]
    sums = dot(both, pair_lanes())
    return [sums[32 * i : 32 * i + 32] for i in range(len(planes))]


def spread(planes, scratch):
    wide = dot(jnp.concatenate(planes, axis=0), spread_lanes())
    scratch[pl.ds(0, 32 * len(planes), 2), :] = wide
    scratch[pl.ds(1, 32 * len(planes), 2), :] = wide
    return [scratch[64 * i : 64 * i + 64, :] for i in range(len(planes))]


def left(shape):
    return lax.broadcasted_iota(jnp.int32, shape, 1) < 64


def pack(x):
    return jnp.where(left((16, 128)), x[:16], x[16:])


def unpack(t):
    other = turn(t, 64, 1)
    here = left((16, 128))
    return jnp.concatenate([jnp.where(here, t, other), jnp.where(here, other, t)], axis=0)


def coarse_slope(below, centre, above, coef):
    return 0.25 * (around(centre) + below + above - 6.0 * centre) + coef * cubic(centre)


def mix(row, nodes):
    return QUAD[row][0] * nodes[0] + QUAD[row][1] * nodes[1] + QUAD[row][2] * nodes[2]


def packets(spot, up, down, inners, outers):
    def put(to_inner, to_outer):
        for parts, outs in ((to_inner, inners), (to_outer, outers)):
            whole = jnp.concatenate(parts, axis=0)
            half = whole.shape[0] // 2
            outs[0][...] = whole[:half]
            outs[1][...] = whole[half:]

    @pl.when(spot[2] == 0)
    def _():
        put(up, down)

    @pl.when(spot[2] != 0)
    def _():
        put(down, up)


def sides(spot, inner, inner_rest, outer, outer_rest):
    a = jnp.concatenate([inner[...], inner_rest[...]], axis=0)
    b = jnp.concatenate([outer[...], outer_rest[...]], axis=0)
    low = jnp.full(a.shape, spot[2], jnp.int32) == 0
    return jnp.where(low, b, a), jnp.where(low, a, b)


def first_kernel(
    spot, initial, coeff, guess, inner, inner_rest, outer, outer_rest, keep, initial_out, coeff_out, guess_out, scratch
):
    for out, given in ((initial_out, initial), (coeff_out, coeff), (guess_out, guess)):
        out[...] = given[...]
    u = [guess[0], guess[1]]
    c = [coeff[0], coeff[1]]
    both = u[0] + u[1]
    total = around(both) - 5.0 * both + c[0] * cubic(u[0]) + c[1] * cubic(u[1])
    own, value, coef, start = squash([total, both, c[0] + c[1], initial[0] + initial[1]], scratch)
    value, coef, start = 0.125 * value, 0.125 * coef, 0.125 * start
    packets(spot, u + [c[1], pack(start)], u + [c[0], pack(start)], [inner, inner_rest], [outer, outer_rest])
    keep[0] = own
    keep[1] = value
    keep[2] = coef
    keep[3] = start


def own_k(own, value0, value0_sides, coef):
    slope = coarse_slope(value0_sides[0], value0, value0_sides[1], coef)
    return [(STEP / 8.0) * own[m] - (STEP * QUAD[m + 1][0]) * slope for m in (0, 1)]


def complete_first(
    spot, inner, inner_rest, outer, outer_rest, kept, initial, received, owned, beside, beyond, mine, keep, begin_out,
    scratch,
):
    below, above = sides(spot, inner, inner_rest, outer, outer_rest)
    begin = starting(spot, initial, received)
    own, value, coef, start = (kept[i] for i in range(4))
    low, high, value_low, value_high, value_begin = squash(
        [below[64:128, :], above[0:64, :], below[0:64, :] + below[64:128, :], above[0:64, :] + above[64:128, :],
         begin[0] + begin[1]],
        scratch,
    )
    value_low, value_high = 0.125 * value_low, 0.125 * value_high
    start_low, start_high = unpack(below[192:208, :]), unpack(above[192:208, :])
    start_slope = coarse_slope(start_low, start, start_high, coef)
    whole = own + low + high
    k = own_k([ROWSUM[1] * whole, ROWSUM[2] * whole], value, [value_low, value_high], coef)
    first = jnp.full((32, 128), spot[0], jnp.int32) == 0
    given = [pack(k[m - 1] + jnp.where(first, start + (STEP * QUAD[m][0]) * start_slope, 0.0)) for m in (2, 1)]
    given += [pack(coef), pack(0.125 * value_begin), pack(start)]
    mine[...] = given[0]
    odd = jnp.full((64, 128), spot[3], jnp.int32) == 1
    for i, part in enumerate(given):
        for out in (owned, beside, beyond):
            out[16 * i : 16 * i + 16, :] = part
    beside[80:144, :] = jnp.where(odd, begin[0], begin[1])
    beyond[80:144, :] = jnp.where(odd, begin[1], begin[0])
    for x in (0, 1):
        owned[80 + 64 * x : 144 + 64 * x, :] = begin[x]
        begin_out[x] = begin[x]
    for i, part in enumerate([k[0], k[1], start, start_slope, start_low, start_high, value_low, value_high]):
        keep[i] = part


def plane(spot, rows, owned, beside, beyond, sections, side, item, up=False):
    odd = spot[3]
    if item < SECTIONS:
        if side == 0:
            return sections[item, 0:16, :]
        at = jnp.where(odd == 1, side, 3 - side)
        return sections[item, pl.ds(pl.multiple_of(16 * at, 16), 16), :]
    row = rows[item]
    if side == 0:
        row += 64 if item >= EDGE and up else 0
        return owned[row : row + 16, :]
    near, far = beside[row : row + 16, :], beyond[row : row + 16, :]
    picked = jnp.full((16, 128), odd, jnp.int32) == (1 if side == 1 else 0)
    return jnp.where(picked, near, far)


def pack_kernel(items, rows):
    total = slots(items)

    def body(spot, owned, beside, beyond, sections, out):
        chip, core = spot[1], spot[2]

        def fill(own_core, away):
            slot = 0
            up = away > 0 or (away == 0 and own_core == 0)
            for side, least in shares(own_core, away):
                for item, reach in items:
                    if reach >= least:
                        part = plane(spot, rows, owned, beside, beyond, sections, side, item, up)
                        out[chip + away, 16 * slot : 16 * slot + 16, :] = part
                        slot += 1

        for own_core in (0, 1):
            for away in range(1 - CHIPS, CHIPS):
                there = jnp.logical_and(chip + away >= 0, chip + away < CHIPS)

                @pl.when(jnp.logical_and(core == own_core, there))
                def _():
                    fill(own_core, away)

    return body, total


def sweep(spot, items, rows, owned, beside, beyond, sections, windows, swapped, coefs, started, line, history):
    core = spot[2]
    place = 2 * spot[1] + core
    rank = {item: i for i, (item, _) in enumerate(items)}
    reach_of = dict(items)

    def fetch(item, w, whole=False):
        if w in (0, -BLOCK, BLOCK):
            side = {0: 0, -BLOCK: 1, BLOCK: 2}[w]
            return unpack(plane(spot, rows, owned, beside, beyond, sections, side, item))
        at = place + w
        if w > 0:
            outside, least = at >= BLOCK, [max(1, BLOCK - w - i) for i in (0, 1)]
        else:
            outside, least = at < 0, [max(1, BLOCK - 1 + w + i) for i in (0, 1)]
        before = jnp.where(core == 0, count(items, least[0]), count(items, least[1]))
        slot = rank[item] + jnp.where(outside, before, 0)
        source = windows if w % 2 == 0 else swapped
        found = source[(at & (BLOCK - 1)) >> 1, pl.ds(pl.multiple_of(16 * slot, 16), 16), :]
        return found if whole else unpack(found)

    if COEF in rank:
        for w in range(-7, 8):
            coefs[w + 7] = fetch(COEF, w)
    outermost = [fetch(INITIAL, w) if INITIAL in rank else jnp.zeros((32, 128), F32) for w in (-2, 2)]
    history[0] = outermost[0]
    history[1] = started[4]
    history[2] = started[2]
    history[3] = started[5]
    history[4] = outermost[1]
    for w in range(-8, 9):
        value = fetch(0, w)
        line[0, w + 8] = value
        if abs(w) <= 2:
            history[5 + w + 2] = value
    for k in range(1, SECTIONS):
        if k not in rank:
            continue
        old, new = (k - 1) % 2, k % 2
        for w in range(-reach_of[k], reach_of[k] + 1):
            centre = line[old, w + 8]
            slope = coarse_slope(line[old, w + 7], centre, line[old, w + 9], coefs[w + 7])
            value = centre + (STEP * QUAD[2][0]) * slope + fetch(k, w)
            line[new, w + 8] = value
            if abs(w) <= 2:
                history[5 * (k + 1) + w + 2] = value
    return fetch


def correct(spot, fetch, coefs, started, history, kept, values, nodes, below, above, coeff, begin, scratch):
    section = spot[0]
    s = [history[5 * section + i] for i in range(5)]
    slope = [coarse_slope(s[i], s[i + 1], s[i + 2], coefs[6 + i]) for i in range(3)]
    later = jnp.full((32, 128), section, jnp.int32) > 0
    edges = []
    for w, i in ((-1, 0), (1, 2)):
        for m, near in ((1, NEAR1), (2, NEAR2)):
            edges.append(fetch(near, w) + jnp.where(later, ROWSUM[m] * s[i + 1] + START[m] * slope[i], 0.0))
    coarse = [s[2]] + [s[2] + (STEP * QUAD[m][0]) * slope[1] + kept[m - 1] for m in (1, 2)]
    wide = spread([coarse[j] - values[j] for j in range(3)] + edges, scratch)
    fixed = [[nodes[j][x] + wide[j] for x in (0, 1)] for j in range(3)]
    rates = [[cubic(fixed[j][x]) for x in (0, 1)] for j in range(3)]
    fresh = []
    for m in (1, 2):
        sums = [mix(m, [fixed[j][x] for j in range(3)]) for x in (0, 1)]
        ends = [below[m - 1] + wide[2 + m], above[m - 1] + wide[4 + m]]
        fresh.append([])
        for x in (0, 1):
            change = around(sums[x]) - 6.0 * sums[x] + sums[1 - x] + ends[x]
            change = change + coeff[x] * mix(m, [rates[j][x] for j in range(3)])
            fresh[-1].append(begin[x] + STEP * change)
    return coarse[2], fresh


def starting(spot, initial, received):
    first = jnp.full((64, 128), spot[0], jnp.int32) == 0
    return [jnp.where(first, initial[x], received[x]) for x in (0, 1)]


def previous_end(section, fetch, coefs, history, starts, coeff, initial, earlier, scratch):
    before = jnp.maximum(section - 1, 0)
    s = [history[5 * before + i] for i in range(5)]
    value = [fetch(BEGIN, w) for w in range(-2, 3)]
    shift = []
    for i in range(3):
        two = history[5 * section + 1 + i]
        slope = coarse_slope(s[i], s[i + 1], s[i + 2], coefs[6 + i])
        slope = slope - coarse_slope(value[i], value[i + 1], value[i + 2], coefs[6 + i])
        one = 0.5 * (s[i + 1] + two) + (STEP * (QUAD[1][0] - 0.5 * QUAD[2][0])) * slope
        shift.append([s[i + 1] - value[i + 1], one - value[i + 1], two - value[i + 1]])
    wide = spread([mix(2, shift[0])] + shift[1] + [mix(2, shift[2])], scratch)
    fixed = [[starts[x] + wide[1 + j] for j in range(3)] for x in (1, 2)]
    sums = [ROWSUM[2] * starts[0] + wide[0], mix(2, fixed[0]), mix(2, fixed[1]), ROWSUM[2] * starts[3] + wide[4]]
    number = jnp.full((64, 128), section, jnp.int32)
    out = []
    for x in (0, 1):
        change = around(sums[x + 1]) - 6.0 * sums[x + 1] + sums[x] + sums[x + 2]
        change = change + coeff[x] * mix(2, [cubic(part) for part in fixed[x]])
        end = jnp.where(number == 1, initial[x], earlier[x]) + STEP * change
        out.append(jnp.where(number == 0, initial[x], end))
    return out


def finish_first(
    spot, owned, beside, beyond, sections, windows, swapped, started, kept, inner, inner_rest, outer, outer_rest,
    initial, coeff, guess, begin, earlier, middle_out, end_out, ends, begin_out, keep, owned_out, mine, coefs, line, history, scratch,
):
    fetch = sweep(
        spot, ITEMS[0], ROWS[0], owned, beside, beyond, sections, windows, swapped, coefs, started, line, history
    )
    below, above = sides(spot, inner, inner_rest, outer, outer_rest)
    section = spot[0]
    later = jnp.full((32, 128), section, jnp.int32) > 0
    s = [history[5 * section + i] for i in range(5)]
    slope = [coarse_slope(s[i], s[i + 1], s[i + 2], coefs[6 + i]) for i in range(3)]
    step = [s[i + 1] + (STEP * QUAD[1][0]) * slope[i] for i in range(3)]
    value = [started[6], kept[1], started[7]]
    coarse = []
    for i in range(3):
        if i == 1:
            one, two = step[1] + started[0], s[2] + (STEP * QUAD[2][0]) * slope[1] + started[1]
        else:
            one = fetch(NEAR1, i - 1) + jnp.where(later, step[i], 0.0)
            two = history[5 * section + 6 + i]
        coarse += [s[i + 1] - value[i], one - value[i], two - value[i]]
    wide = spread(coarse, scratch)
    u = [below[0:64, :], below[64:128, :], guess[0], guess[1], above[0:64, :], above[64:128, :]]
    c = [None, below[128:192, :], coeff[0], coeff[1], above[128:192, :], None]
    b = [None] + [None] * 4 + [None]
    b[2], b[3] = begin[0], begin[1]
    for x, w in ((1, -1), (4, 1)):
        b[x] = jnp.concatenate([fetch(EDGE + i, w, whole=True) for i in range(4)], axis=0)
    begin_next = previous_end(section, fetch, coefs, history, b[1:5], coeff, initial, earlier, scratch)
    for x in (0, 1):
        begin_out[x] = begin_next[x]
    fixed = [[u[x] + wide[3 * (x // 2) + j] for j in range(3)] for x in range(6)]
    nodes = [None] + [[b[x]] for x in range(1, 5)] + [None]
    rates = [None] + [[cubic(fixed[x][j]) for j in range(3)] for x in range(1, 5)] + [None]
    for m in (1, 2):
        sums = [mix(m, fixed[x]) for x in range(6)]
        for x in range(1, 5):
            change = around(sums[x]) - 6.0 * sums[x] + sums[x - 1] + sums[x + 1] + c[x] * mix(m, rates[x])
            nodes[x].append(b[x] + STEP * change)
    for x in (0, 1):
        middle_out[x] = nodes[x + 2][1]
        end_out[x] = nodes[x + 2][2]
    rates = [[cubic(nodes[x][j]) for j in range(3)] for x in (2, 3)]
    planes = []
    for m in (1, 2):
        sums = [mix(m, nodes[x]) for x in range(1, 5)]
        ends[m - 1] = sums[0]
        ends[m + 1] = sums[3]
        both = sums[1] + sums[2]
        planes.append(
            around(both) - 5.0 * both + sums[0] + sums[3] + c[2] * mix(m, rates[0]) + c[3] * mix(m, rates[1])
        )
    for j in range(3):
        planes.append(nodes[2][j] + nodes[3][j])
    small = squash(planes, scratch)
    values = [0.125 * small[2 + j] for j in range(3)]
    k = own_k(small[:2], values[0], [fetch(BEGIN, -1), fetch(BEGIN, 1)], kept[2])
    first = jnp.logical_not(later)
    ours = pack(k[1] + jnp.where(first, started[2] + (STEP * QUAD[2][0]) * started[3], 0.0))
    owned_out[0:16, :] = ours
    mine[...] = ours
    for m in (1, 2):
        near = QUAD[m][1] * k[0] + QUAD[m][2] * k[1] - mix(m, values)
        near = near + jnp.where(first, ROWSUM[m] * started[2] + START[m] * started[3], 0.0)
        owned_out[16 * m : 16 * m + 16, :] = pack(near)
    for i, part in enumerate(values + k):
        keep[i] = part


def finish_second(
    spot, owned, beside, beyond, sections, windows, swapped, started, kept, ends, coeff, begin_in, middle_in, end_in,
    begin, coefs, fresh_out, coarse_out, line, history, scratch,
):
    fetch = sweep(
        spot, ITEMS[1], ROWS[1], owned, beside, beyond, sections, windows, swapped, coefs, started, line, history
    )
    nodes = [[part[0], part[1]] for part in (begin_in, middle_in, end_in)]
    end, fresh = correct(
        spot, fetch, coefs, started, history, (kept[3], kept[4]), [kept[0], kept[1], kept[2]], nodes,
        [ends[0], ends[1]], [ends[2], ends[3]], [coeff[0], coeff[1]], [begin[0], begin[1]], scratch,
    )
    for m in (0, 1):
        for x in (0, 1):
            fresh_out[m, x] = fresh[m][x]
    coarse_out[...] = end[:, :64]


def run(body, args, outs, scratch=(), name=None, first=False, last=False):
    def placed(*refs):
        spot = [lax.axis_index(a) for a in ("tm", "chip", "core", "block")]
        body(spot[:3] + [spot[3] & 1], *refs)

    return pl.pallas_call(
        placed,
        out_shape=[jax.ShapeDtypeStruct(shape, F32) if last else pltpu.VMEM(shape, F32) for shape in outs],
        in_specs=[pl.BlockSpec(memory_space=pltpu.VMEM)] * len(args),
        out_specs=[pl.BlockSpec(memory_space=pltpu.VMEM)] * len(outs),
        scratch_shapes=[pltpu.VMEM(shape, F32) for shape in scratch],
        compiler_params=None if first else pltpu.CompilerParams(vmem_limit_bytes=16 << 20),
        name=name,
    )(*(a if first else pltpu.with_memory_space_constraint(a, pltpu.VMEM) for a in args))


class Links:
    call = staticmethod(run)

    @staticmethod
    def swap_block(x, row):
        n = lax.axis_size("block")
        pairs = [(i, i ^ 1 if row else (i + 2 * (i % 2) - 1) % n) for i in range(n)]
        return lax.ppermute(x, "block", pairs)

    @staticmethod
    def swap_inner(x):
        return lax.ppermute(x, "core", [(0, 1), (1, 0)])

    @staticmethod
    def swap_outer(x):
        n = lax.axis_size("block") * BLOCK
        return lax.ppermute(x, ("block", "chip", "core"), [(i, (i + 2 * (i % 2) - 1) % n) for i in range(n)])

    @staticmethod
    def onward(x, by):
        n = lax.axis_size("tm")
        return lax.ppermute(x, "tm", [(i, i + by) for i in range(n - by)])

    @staticmethod
    def sections(x):
        return lax.all_to_all(jnp.broadcast_to(x, (SECTIONS,) + x.shape), "tm", 0, 0)

    @staticmethod
    def block(x):
        return lax.all_to_all(x, "chip", 0, 0)

    @staticmethod
    def together(*values):
        return lax.optimization_barrier(values)

    @staticmethod
    def stack(*planes):
        return jnp.concatenate([p[:16] for p in planes], axis=0)


def iterate(links, initial, coeff, guess):
    coarse, slab = (32, 128), (2, 64, 128)
    work = [(2, 17) + coarse, (45,) + coarse]

    def windows(owned, beside, beyond, mine, iteration):
        sections = links.sections(links.stack(mine, beside, beyond))
        body, total = pack_kernel(ITEMS[iteration], ROWS[iteration])
        (parcels,) = links.call(
            body, (owned, beside, beyond, sections), [(CHIPS, 16 * total, 128)], name="hand_out"
        )
        parcels = links.block(parcels)
        return owned, beside, beyond, sections, parcels, links.swap_inner(parcels)

    sent = guess
    inner, inner_rest, outer, outer_rest, kept, initial, coeff, guess = links.call(
        first_kernel, (initial, coeff, guess),
        [(104, 128)] * 4 + [(4,) + coarse, slab, slab, slab], [(256, 128)], name="first", first=True,
    )
    outer, outer_rest, inner, inner_rest, received = links.together(
        links.swap_outer(outer), links.swap_outer(outer_rest), links.swap_inner(inner), links.swap_inner(inner_rest),
        links.onward(sent, 1),
    )
    owned, beside, beyond, mine, started, begin = links.call(
        complete_first, (inner, inner_rest, outer, outer_rest, kept, initial, received),
        [(208, 128), (144, 128), (144, 128), (16, 128), (8,) + coarse, slab], [(320, 128)], name="complete_first",
    )
    beside, beyond, earlier = links.swap_block(beside, True), links.swap_block(beyond, False), links.onward(sent, 2)
    middle, end, ends, begin_next, kept, owned, mine, coefs = links.call(
        finish_first,
        (*windows(owned, beside, beyond, mine, 0), started, kept, inner, inner_rest, outer, outer_rest, initial,
         coeff, guess, begin, earlier),
        [slab, slab, (4, 64, 128), slab, (5,) + coarse, (48, 128), (16, 128), (15,) + coarse],
        work + [(576, 128)],
        name="finish_first",
    )
    beside, beyond = links.swap_block(owned, True), links.swap_block(owned, False)
    fine, coarse_end = links.call(
        finish_second,
        (*windows(owned, beside, beyond, mine, 1), started, kept, ends, coeff, begin, middle, end, begin_next, coefs),
        [(2, 2, 64, 128), (32, 64)],
        work + [(448, 128)],
        name="finish_second",
        last=True,
    )
    return fine, coarse_end


def on_device(initial, coeff, guess):
    fine, coarse_end = iterate(Links, initial, coeff, guess[0])
    return fine[None], coarse_end[None, None]


def solution(mesh):
    split = Mesh(
        mesh.devices.reshape(mesh.shape["tm"], mesh.shape["space"] // BLOCK, CHIPS, 2), ("tm", "block", "chip", "core")
    )
    space = ("block", "chip", "core")
    return jax.shard_map(
        on_device,
        mesh=split,
        in_specs=(P(space, None, None), P(space, None, None), P("tm", space, None, None)),
        out_specs=(P("tm", None, space, None, None), P("tm", space, None, None)),
        check_vma=False,
    )
```

```python
import jax
import jax.numpy as jnp
from jax import lax
from jax.experimental import pallas as pl
from jax.experimental.pallas import tpu as pltpu
from jax.sharding import Mesh, PartitionSpec as P

STEP = 0.06
QUAD = ((0.0, 0.0, 0.0), (5.0 / 24.0, 1.0 / 3.0, -1.0 / 24.0), (1.0 / 6.0, 2.0 / 3.0, 1.0 / 6.0))
ROWSUM = tuple(sum(row) for row in QUAD)
START = tuple(STEP * (row[1] * QUAD[1][0] + row[2] * QUAD[2][0]) for row in QUAD)
SECTIONS = 8
BLOCK = 8
CHIPS = BLOCK // 2
F32 = jnp.float32

COEF, NEAR1, NEAR2, BEGIN, INITIAL, EDGE = 10, 11, 12, 13, 14, 15
ITEMS = (
    ((0, 8), (1, 7), (COEF, 7), (2, 6), (3, 5), (4, 4), (5, 3), (6, 2), (BEGIN, 2), (INITIAL, 2), (7, 1),
     (NEAR1, 1))
    + tuple((EDGE + i, 1) for i in range(4)),
    ((0, 8), (1, 7), (2, 6), (3, 5), (4, 4), (5, 3), (6, 2), (NEAR1, 1), (NEAR2, 1)),
)
ROWS = ({NEAR1: 16, COEF: 32, BEGIN: 48, INITIAL: 64, **{EDGE + i: 80 + 16 * i for i in range(4)}}, {NEAR1: 16, NEAR2: 32})


def count(items, distance):
    return sum(1 for _, reach in items if reach >= distance)


def shares(core, ahead):
    if ahead == 0:
        return (0, 1), (2 - core, BLOCK - 1)
    if ahead > 0:
        return (0, 2 * ahead - core), (2, BLOCK - 1 - 2 * ahead + core)
    return (0, -2 * ahead + core - 1), (1, BLOCK + 2 * ahead - core)


def slots(items):
    return max(sum(count(items, least) for _, least in shares(core, a)) for core in (0, 1) for a in range(-3, 4))


def turn(x, by, axis):
    return pltpu.roll(x, by % x.shape[axis], axis)


def around(x):
    return turn(x, 1, 0) + turn(x, -1, 0) + turn(x, 1, 1) + turn(x, -1, 1)


def cubic(u):
    return u - u * u * u


def dot(a, b):
    return jnp.dot(a, b, precision=lax.Precision.HIGHEST, preferred_element_type=F32)


def pair_lanes():
    z = lax.broadcasted_iota(jnp.int32, (128, 128), 0)
    c = lax.broadcasted_iota(jnp.int32, (128, 128), 1)
    return jnp.where((z >> 1) == (c & 63), 1.0, 0.0).astype(F32)


def spread_lanes():
    c = lax.broadcasted_iota(jnp.int32, (128, 128), 0)
    z = lax.broadcasted_iota(jnp.int32, (128, 128), 1)
    return jnp.where((z >> 1) == c, 1.0, 0.0).astype(F32)


def squash(planes, scratch):
    for i, plane in enumerate(planes):
        scratch[64 * i : 64 * i + 64, :] = plane
    both = scratch[pl.ds(0, 32 * len(planes), 2), :] + scratch[pl.ds(1, 32 * len(planes), 2), :]
    sums = dot(both, pair_lanes())
    return [sums[32 * i : 32 * i + 32] for i in range(len(planes))]


def spread(planes, scratch):
    wide = dot(jnp.concatenate(planes, axis=0), spread_lanes())
    scratch[pl.ds(0, 32 * len(planes), 2), :] = wide
    scratch[pl.ds(1, 32 * len(planes), 2), :] = wide
    return [scratch[64 * i : 64 * i + 64, :] for i in range(len(planes))]


def left(shape):
    return lax.broadcasted_iota(jnp.int32, shape, 1) < 64


def pack(x):
    return jnp.where(left((16, 128)), x[:16], x[16:])


def unpack(t):
    other = turn(t, 64, 1)
    here = left((16, 128))
    return jnp.concatenate([jnp.where(here, t, other), jnp.where(here, other, t)], axis=0)


def coarse_slope(below, centre, above, coef):
    return 0.25 * (around(centre) + below + above - 6.0 * centre) + coef * cubic(centre)


def mix(row, nodes):
    return QUAD[row][0] * nodes[0] + QUAD[row][1] * nodes[1] + QUAD[row][2] * nodes[2]


def packets(spot, up, down, inners, outers):
    def put(to_inner, to_outer):
        for parts, outs in ((to_inner, inners), (to_outer, outers)):
            whole = jnp.concatenate(parts, axis=0)
            half = whole.shape[0] // 2
            outs[0][...] = whole[:half]
            outs[1][...] = whole[half:]

    @pl.when(spot[2] == 0)
    def _():
        put(up, down)

    @pl.when(spot[2] != 0)
    def _():
        put(down, up)


def sides(spot, inners, outers):
    a = jnp.concatenate([part[...] for part in inners], axis=0)
    b = jnp.concatenate([part[...] for part in outers], axis=0)
    low = jnp.full(a.shape, spot[2], jnp.int32) == 0
    return jnp.where(low, b, a), jnp.where(low, a, b)


def first_kernel(
    spot, initial, coeff, guess, inner, inner_rest, outer, outer_rest, keep, initial_out, coeff_out, guess_out, scratch
):
    for out, given in ((initial_out, initial), (coeff_out, coeff), (guess_out, guess)):
        out[...] = given[...]
    u = [guess[0], guess[1]]
    c = [coeff[0], coeff[1]]
    both = u[0] + u[1]
    total = around(both) - 5.0 * both + c[0] * cubic(u[0]) + c[1] * cubic(u[1])
    own, value, coef, start = squash([total, both, c[0] + c[1], initial[0] + initial[1]], scratch)
    value, coef, start = 0.125 * value, 0.125 * coef, 0.125 * start
    small = [pack(value), pack(start)]
    packets(
        spot, [u[1]] + small + [u[0], c[1]], [u[0]] + small + [u[1], c[0]], [inner, inner_rest], [outer, outer_rest]
    )
    keep[0] = own
    keep[1] = value
    keep[2] = coef
    keep[3] = start


def own_k(own, value0, value0_sides, coef):
    slope = coarse_slope(value0_sides[0], value0, value0_sides[1], coef)
    return [(STEP / 8.0) * own[m] - (STEP * QUAD[m + 1][0]) * slope for m in (0, 1)]


def complete_first(
    spot, inner, outer, kept, initial, earlier, received, owned, beside, beyond, mine, keep, begin_out, earlier_out, scratch
):
    below, above = sides(spot, [inner], [outer])
    begin = starting(spot, initial, received)
    own, value, coef, start = (kept[i] for i in range(4))
    low, high, value_begin = squash([below[0:64, :], above[0:64, :], begin[0] + begin[1]], scratch)
    value_low, value_high = unpack(below[64:80, :]), unpack(above[64:80, :])
    start_low, start_high = unpack(below[80:96, :]), unpack(above[80:96, :])
    start_slope = coarse_slope(start_low, start, start_high, coef)
    whole = own + low + high
    k = own_k([ROWSUM[1] * whole, ROWSUM[2] * whole], value, [value_low, value_high], coef)
    first = jnp.full((32, 128), spot[0], jnp.int32) == 0
    given = [pack(k[m - 1] + jnp.where(first, start + (STEP * QUAD[m][0]) * start_slope, 0.0)) for m in (2, 1)]
    given += [pack(coef), pack(0.125 * value_begin), pack(start)]
    mine[...] = given[0]
    odd = jnp.full((64, 128), spot[3], jnp.int32) == 1
    for i, part in enumerate(given):
        for out in (owned, beside, beyond):
            out[16 * i : 16 * i + 16, :] = part
    beside[80:144, :] = jnp.where(odd, begin[0], begin[1])
    beyond[80:144, :] = jnp.where(odd, begin[1], begin[0])
    for x in (0, 1):
        owned[80 + 64 * x : 144 + 64 * x, :] = begin[x]
        begin_out[x] = begin[x]
        earlier_out[x] = jnp.where(jnp.full((64, 128), spot[0], jnp.int32) == 1, initial[x], earlier[x])
    for i, part in enumerate([k[0], k[1], start, start_slope, start_low, start_high, value_low, value_high]):
        keep[i] = part


def plane(spot, rows, owned, beside, beyond, sections, side, item, up=False):
    odd = spot[3]
    if item < SECTIONS:
        if side == 0:
            return sections[item, 0:16, :]
        at = jnp.where(odd == 1, side, 3 - side)
        return sections[item, pl.ds(pl.multiple_of(16 * at, 16), 16), :]
    row = rows[item]
    if side == 0:
        row += 64 if item >= EDGE and up else 0
        return owned[row : row + 16, :]
    near, far = beside[row : row + 16, :], beyond[row : row + 16, :]
    picked = jnp.full((16, 128), odd, jnp.int32) == (1 if side == 1 else 0)
    return jnp.where(picked, near, far)


def pack_kernel(items, rows):
    total = slots(items)

    def body(spot, owned, beside, beyond, sections, out):
        chip, core = spot[1], spot[2]

        def fill(own_core, away):
            slot = 0
            up = away > 0 or (away == 0 and own_core == 0)
            for side, least in shares(own_core, away):
                for item, reach in items:
                    if reach >= least:
                        part = plane(spot, rows, owned, beside, beyond, sections, side, item, up)
                        out[chip + away, 16 * slot : 16 * slot + 16, :] = part
                        slot += 1

        for own_core in (0, 1):
            for away in range(1 - CHIPS, CHIPS):
                there = jnp.logical_and(chip + away >= 0, chip + away < CHIPS)

                @pl.when(jnp.logical_and(core == own_core, there))
                def _():
                    fill(own_core, away)

    return body, total


def sweep(spot, items, rows, owned, beside, beyond, sections, windows, swapped, coefs, started, line, history):
    core = spot[2]
    place = 2 * spot[1] + core
    rank = {item: i for i, (item, _) in enumerate(items)}
    reach_of = dict(items)

    def fetch(item, w, whole=False):
        if w in (0, -BLOCK, BLOCK):
            side = {0: 0, -BLOCK: 1, BLOCK: 2}[w]
            return unpack(plane(spot, rows, owned, beside, beyond, sections, side, item))
        at = place + w
        if w > 0:
            outside, least = at >= BLOCK, [max(1, BLOCK - w - i) for i in (0, 1)]
        else:
            outside, least = at < 0, [max(1, BLOCK - 1 + w + i) for i in (0, 1)]
        before = jnp.where(core == 0, count(items, least[0]), count(items, least[1]))
        slot = rank[item] + jnp.where(outside, before, 0)
        source = windows if w % 2 == 0 else swapped
        found = source[(at & (BLOCK - 1)) >> 1, pl.ds(pl.multiple_of(16 * slot, 16), 16), :]
        return found if whole else unpack(found)

    if COEF in rank:
        for w in range(-7, 8):
            coefs[w + 7] = fetch(COEF, w)
    outermost = [fetch(INITIAL, w) if INITIAL in rank else jnp.zeros((32, 128), F32) for w in (-2, 2)]
    history[0] = outermost[0]
    history[1] = started[4]
    history[2] = started[2]
    history[3] = started[5]
    history[4] = outermost[1]
    for w in range(-8, 9):
        value = fetch(0, w)
        line[0, w + 8] = value
        if abs(w) <= 2:
            history[5 + w + 2] = value
    for k in range(1, SECTIONS):
        if k not in rank:
            continue
        old, new = (k - 1) % 2, k % 2
        for w in range(-reach_of[k], reach_of[k] + 1):
            centre = line[old, w + 8]
            slope = coarse_slope(line[old, w + 7], centre, line[old, w + 9], coefs[w + 7])
            value = centre + (STEP * QUAD[2][0]) * slope + fetch(k, w)
            line[new, w + 8] = value
            if abs(w) <= 2:
                history[5 * (k + 1) + w + 2] = value
    return fetch


def correct(spot, fetch, coefs, started, history, kept, values, nodes, below, above, coeff, begin, scratch):
    section = spot[0]
    s = [history[5 * section + i] for i in range(5)]
    slope = [coarse_slope(s[i], s[i + 1], s[i + 2], coefs[6 + i]) for i in range(3)]
    later = jnp.full((32, 128), section, jnp.int32) > 0
    edges = []
    for w, i in ((-1, 0), (1, 2)):
        for m, near in ((1, NEAR1), (2, NEAR2)):
            edges.append(fetch(near, w) + jnp.where(later, ROWSUM[m] * s[i + 1] + START[m] * slope[i], 0.0))
    coarse = [s[2]] + [s[2] + (STEP * QUAD[m][0]) * slope[1] + kept[m - 1] for m in (1, 2)]
    wide = spread([coarse[j] - values[j] for j in range(3)] + edges, scratch)
    fixed = [[nodes[j][x] + wide[j] for x in (0, 1)] for j in range(3)]
    rates = [[cubic(fixed[j][x]) for x in (0, 1)] for j in range(3)]
    fresh = []
    for m in (1, 2):
        sums = [mix(m, [fixed[j][x] for j in range(3)]) for x in (0, 1)]
        ends = [below[m - 1] + wide[2 + m], above[m - 1] + wide[4 + m]]
        fresh.append([])
        for x in (0, 1):
            change = around(sums[x]) - 6.0 * sums[x] + sums[1 - x] + ends[x]
            change = change + coeff[x] * mix(m, [rates[j][x] for j in range(3)])
            fresh[-1].append(begin[x] + STEP * change)
    return coarse[2], fresh


def starting(spot, initial, received):
    first = jnp.full((64, 128), spot[0], jnp.int32) == 0
    return [jnp.where(first, initial[x], received[x]) for x in (0, 1)]


def previous_end(section, fetch, coefs, history, starts, coeff, initial, earlier, scratch):
    before = jnp.maximum(section - 1, 0)
    s = [history[5 * before + i] for i in range(5)]
    value = [fetch(BEGIN, w) for w in range(-2, 3)]
    shift = []
    for i in range(3):
        two = history[5 * section + 1 + i]
        slope = coarse_slope(s[i], s[i + 1], s[i + 2], coefs[6 + i])
        slope = slope - coarse_slope(value[i], value[i + 1], value[i + 2], coefs[6 + i])
        one = 0.5 * (s[i + 1] + two) + (STEP * (QUAD[1][0] - 0.5 * QUAD[2][0])) * slope
        shift.append([s[i + 1] - value[i + 1], one - value[i + 1], two - value[i + 1]])
    wide = spread([mix(2, shift[0])] + shift[1] + [mix(2, shift[2])], scratch)
    fixed = [[starts[x] + wide[1 + j] for j in range(3)] for x in (1, 2)]
    sums = [ROWSUM[2] * starts[0] + wide[0], mix(2, fixed[0]), mix(2, fixed[1]), ROWSUM[2] * starts[3] + wide[4]]
    first = jnp.full((64, 128), section, jnp.int32) == 0
    out = []
    for x in (0, 1):
        change = around(sums[x + 1]) - 6.0 * sums[x + 1] + sums[x] + sums[x + 2]
        change = change + coeff[x] * mix(2, [cubic(part) for part in fixed[x]])
        out.append(jnp.where(first, initial[x], earlier[x] + STEP * change))
    return out


def finish_first(
    spot, owned, beside, beyond, sections, windows, swapped, started, kept, inner, inner_rest, outer, outer_rest,
    initial, coeff, guess, begin, earlier, middle_out, end_out, ends, begin_out, keep, owned_out, mine, coefs, line, history, scratch,
):
    fetch = sweep(
        spot, ITEMS[0], ROWS[0], owned, beside, beyond, sections, windows, swapped, coefs, started, line, history
    )
    below, above = sides(spot, [inner, inner_rest], [outer, outer_rest])
    section = spot[0]
    later = jnp.full((32, 128), section, jnp.int32) > 0
    s = [history[5 * section + i] for i in range(5)]
    slope = [coarse_slope(s[i], s[i + 1], s[i + 2], coefs[6 + i]) for i in range(3)]
    step = [s[i + 1] + (STEP * QUAD[1][0]) * slope[i] for i in range(3)]
    value = [started[6], kept[1], started[7]]
    coarse = []
    for i in range(3):
        if i == 1:
            one, two = step[1] + started[0], s[2] + (STEP * QUAD[2][0]) * slope[1] + started[1]
        else:
            one = fetch(NEAR1, i - 1) + jnp.where(later, step[i], 0.0)
            two = history[5 * section + 6 + i]
        coarse += [s[i + 1] - value[i], one - value[i], two - value[i]]
    wide = spread(coarse, scratch)
    u = [below[96:160, :], below[0:64, :], guess[0], guess[1], above[0:64, :], above[96:160, :]]
    c = [None, below[160:224, :], coeff[0], coeff[1], above[160:224, :], None]
    b = [None] + [None] * 4 + [None]
    b[2], b[3] = begin[0], begin[1]
    for x, w in ((1, -1), (4, 1)):
        b[x] = jnp.concatenate([fetch(EDGE + i, w, whole=True) for i in range(4)], axis=0)
    begin_next = previous_end(section, fetch, coefs, history, b[1:5], coeff, initial, earlier, scratch)
    for x in (0, 1):
        begin_out[x] = begin_next[x]
    fixed = [[u[x] + wide[3 * (x // 2) + j] for j in range(3)] for x in range(6)]
    nodes = [None] + [[b[x]] for x in range(1, 5)] + [None]
    rates = [None] + [[cubic(fixed[x][j]) for j in range(3)] for x in range(1, 5)] + [None]
    for m in (1, 2):
        sums = [mix(m, fixed[x]) for x in range(6)]
        for x in range(1, 5):
            change = around(sums[x]) - 6.0 * sums[x] + sums[x - 1] + sums[x + 1] + c[x] * mix(m, rates[x])
            nodes[x].append(b[x] + STEP * change)
    for x in (0, 1):
        middle_out[x] = nodes[x + 2][1]
        end_out[x] = nodes[x + 2][2]
    rates = [[cubic(nodes[x][j]) for j in range(3)] for x in (2, 3)]
    planes = []
    for m in (1, 2):
        sums = [mix(m, nodes[x]) for x in range(1, 5)]
        ends[m - 1] = sums[0]
        ends[m + 1] = sums[3]
        both = sums[1] + sums[2]
        planes.append(
            around(both) - 5.0 * both + sums[0] + sums[3] + c[2] * mix(m, rates[0]) + c[3] * mix(m, rates[1])
        )
    for j in range(3):
        planes.append(nodes[2][j] + nodes[3][j])
    small = squash(planes, scratch)
    values = [0.125 * small[2 + j] for j in range(3)]
    k = own_k(small[:2], values[0], [fetch(BEGIN, -1), fetch(BEGIN, 1)], kept[2])
    first = jnp.logical_not(later)
    ours = pack(k[1] + jnp.where(first, started[2] + (STEP * QUAD[2][0]) * started[3], 0.0))
    owned_out[0:16, :] = ours
    mine[...] = ours
    for m in (1, 2):
        near = QUAD[m][1] * k[0] + QUAD[m][2] * k[1] - mix(m, values)
        near = near + jnp.where(first, ROWSUM[m] * started[2] + START[m] * started[3], 0.0)
        owned_out[16 * m : 16 * m + 16, :] = pack(near)
    for i, part in enumerate(values + k):
        keep[i] = part


def finish_second(
    spot, owned, beside, beyond, sections, windows, swapped, started, kept, ends, coeff, begin_in, middle_in, end_in,
    begin, coefs, fresh_out, coarse_out, line, history, scratch,
):
    fetch = sweep(
        spot, ITEMS[1], ROWS[1], owned, beside, beyond, sections, windows, swapped, coefs, started, line, history
    )
    nodes = [[part[0], part[1]] for part in (begin_in, middle_in, end_in)]
    end, fresh = correct(
        spot, fetch, coefs, started, history, (kept[3], kept[4]), [kept[0], kept[1], kept[2]], nodes,
        [ends[0], ends[1]], [ends[2], ends[3]], [coeff[0], coeff[1]], [begin[0], begin[1]], scratch,
    )
    for m in (0, 1):
        for x in (0, 1):
            fresh_out[m, x] = fresh[m][x]
    coarse_out[...] = end[:, :64]


def run(body, args, outs, scratch=(), name=None, first=False, last=False):
    def placed(*refs):
        spot = [lax.axis_index(a) for a in ("tm", "chip", "core", "block")]
        body(spot[:3] + [spot[3] & 1], *refs)

    return pl.pallas_call(
        placed,
        out_shape=[jax.ShapeDtypeStruct(shape, F32) if last else pltpu.VMEM(shape, F32) for shape in outs],
        in_specs=[pl.BlockSpec(memory_space=pltpu.VMEM)] * len(args),
        out_specs=[pl.BlockSpec(memory_space=pltpu.VMEM)] * len(outs),
        scratch_shapes=[pltpu.VMEM(shape, F32) for shape in scratch],
        compiler_params=None if first else pltpu.CompilerParams(vmem_limit_bytes=16 << 20),
        name=name,
    )(*(a if first else pltpu.with_memory_space_constraint(a, pltpu.VMEM) for a in args))


class Links:
    call = staticmethod(run)

    @staticmethod
    def swap_block(x, row):
        n = lax.axis_size("block")
        pairs = [(i, i ^ 1 if row else (i + 2 * (i % 2) - 1) % n) for i in range(n)]
        return lax.ppermute(x, "block", pairs)

    @staticmethod
    def swap_inner(x):
        return lax.ppermute(x, "core", [(0, 1), (1, 0)])

    @staticmethod
    def swap_outer(x):
        n = lax.axis_size("block") * BLOCK
        return lax.ppermute(x, ("block", "chip", "core"), [(i, (i + 2 * (i % 2) - 1) % n) for i in range(n)])

    @staticmethod
    def onward(x, by):
        n = lax.axis_size("tm")
        return lax.ppermute(x, "tm", [(i, i + by) for i in range(n - by)])

    @staticmethod
    def sections(x):
        return lax.all_to_all(jnp.broadcast_to(x, (SECTIONS,) + x.shape), "tm", 0, 0)

    @staticmethod
    def block(x):
        return lax.all_to_all(x, "chip", 0, 0)

    @staticmethod
    def together(*values):
        return lax.optimization_barrier(values)

    @staticmethod
    def stack(*planes):
        return jnp.concatenate([p[:16] for p in planes], axis=0)


def iterate(links, initial, coeff, guess):
    coarse, slab = (32, 128), (2, 64, 128)
    work = [(2, 17) + coarse, (45,) + coarse]

    def windows(owned, beside, beyond, mine, iteration):
        sections = links.sections(links.stack(mine, beside, beyond))
        body, total = pack_kernel(ITEMS[iteration], ROWS[iteration])
        (parcels,) = links.call(
            body, (owned, beside, beyond, sections), [(CHIPS, 16 * total, 128)], name="hand_out"
        )
        parcels = links.block(parcels)
        return owned, beside, beyond, sections, parcels, links.swap_inner(parcels)

    sent = guess
    inner, inner_rest, outer, outer_rest, kept, initial, coeff, guess = links.call(
        first_kernel, (initial, coeff, guess),
        [(112, 128)] * 4 + [(4,) + coarse, slab, slab, slab], [(256, 128)], name="first", first=True,
    )
    earlier, received, outer, outer_rest, inner = links.together(
        links.onward(sent, 2), links.onward(sent, 1), links.swap_outer(outer), links.swap_outer(outer_rest),
        links.swap_inner(inner),
    )
    inner_rest = links.swap_inner(inner_rest)
    owned, beside, beyond, mine, started, begin, earlier = links.call(
        complete_first, (inner, outer, kept, initial, earlier, received),
        [(208, 128), (144, 128), (144, 128), (16, 128), (8,) + coarse, slab, slab], [(192, 128)], name="complete_first",
    )
    beside, beyond = links.swap_block(beside, True), links.swap_block(beyond, False)
    middle, end, ends, begin_next, kept, owned, mine, coefs = links.call(
        finish_first,
        (*windows(owned, beside, beyond, mine, 0), started, kept, inner, inner_rest, outer, outer_rest, initial,
         coeff, guess, begin, earlier),
        [slab, slab, (4, 64, 128), slab, (5,) + coarse, (48, 128), (16, 128), (15,) + coarse],
        work + [(576, 128)],
        name="finish_first",
    )
    beside, beyond = links.swap_block(owned, True), links.swap_block(owned, False)
    fine, coarse_end = links.call(
        finish_second,
        (*windows(owned, beside, beyond, mine, 1), started, kept, ends, coeff, begin, middle, end, begin_next, coefs),
        [(2, 2, 64, 128), (32, 64)],
        work + [(448, 128)],
        name="finish_second",
        last=True,
    )
    return fine, coarse_end


def on_device(initial, coeff, guess):
    fine, coarse_end = iterate(Links, initial, coeff, guess[0])
    return fine[None], coarse_end[None, None]


def solution(mesh):
    split = Mesh(
        mesh.devices.reshape(mesh.shape["tm"], mesh.shape["space"] // BLOCK, CHIPS, 2), ("tm", "block", "chip", "core")
    )
    space = ("block", "chip", "core")
    return jax.shard_map(
        on_device,
        mesh=split,
        in_specs=(P(space, None, None), P(space, None, None), P("tm", space, None, None)),
        out_specs=(P("tm", None, space, None, None), P("tm", space, None, None)),
        check_vma=False,
    )
```

```python
import jax
import jax.numpy as jnp
from jax import lax
from jax.experimental import pallas as pl
from jax.experimental.pallas import tpu as pltpu
from jax.sharding import Mesh, PartitionSpec as P

STEP = 0.06
QUAD = ((0.0, 0.0, 0.0), (5.0 / 24.0, 1.0 / 3.0, -1.0 / 24.0), (1.0 / 6.0, 2.0 / 3.0, 1.0 / 6.0))
ROWSUM = tuple(sum(row) for row in QUAD)
START = tuple(STEP * (row[1] * QUAD[1][0] + row[2] * QUAD[2][0]) for row in QUAD)
SECTIONS = 8
BLOCK = 8
CHIPS = BLOCK // 2
F32 = jnp.float32

COEF, NEAR1, NEAR2, BEGIN, INITIAL, EDGE = 10, 11, 12, 13, 14, 15
ITEMS = (
    ((0, 8), (1, 7), (COEF, 7), (2, 6), (3, 5), (4, 4), (5, 3), (6, 2), (BEGIN, 2), (INITIAL, 2), (7, 1),
     (NEAR1, 1))
    + tuple((EDGE + i, 1) for i in range(4)),
    ((0, 8), (1, 7), (2, 6), (3, 5), (4, 4), (5, 3), (6, 2), (NEAR1, 1), (NEAR2, 1)),
)
ROWS = ({NEAR1: 16, COEF: 32, BEGIN: 48, INITIAL: 64, **{EDGE + i: 80 + 16 * i for i in range(4)}}, {NEAR1: 16, NEAR2: 32})


def count(items, distance):
    return sum(1 for _, reach in items if reach >= distance)


def shares(core, ahead):
    if ahead == 0:
        return (0, 1), (2 - core, BLOCK - 1)
    if ahead > 0:
        return (0, 2 * ahead - core), (2, BLOCK - 1 - 2 * ahead + core)
    return (0, -2 * ahead + core - 1), (1, BLOCK + 2 * ahead - core)


def slots(items):
    return max(sum(count(items, least) for _, least in shares(core, a)) for core in (0, 1) for a in range(-3, 4))


def turn(x, by, axis):
    return pltpu.roll(x, by % x.shape[axis], axis)


def around(x):
    return turn(x, 1, 0) + turn(x, -1, 0) + turn(x, 1, 1) + turn(x, -1, 1)


def cubic(u):
    return u - u * u * u


def dot(a, b):
    return jnp.dot(a, b, precision=lax.Precision.HIGHEST, preferred_element_type=F32)


def pair_lanes():
    z = lax.broadcasted_iota(jnp.int32, (128, 128), 0)
    c = lax.broadcasted_iota(jnp.int32, (128, 128), 1)
    return jnp.where((z >> 1) == (c & 63), 1.0, 0.0).astype(F32)


def spread_lanes():
    c = lax.broadcasted_iota(jnp.int32, (128, 128), 0)
    z = lax.broadcasted_iota(jnp.int32, (128, 128), 1)
    return jnp.where((z >> 1) == c, 1.0, 0.0).astype(F32)


def squash(planes, scratch):
    for i, plane in enumerate(planes):
        scratch[64 * i : 64 * i + 64, :] = plane
    both = scratch[pl.ds(0, 32 * len(planes), 2), :] + scratch[pl.ds(1, 32 * len(planes), 2), :]
    sums = dot(both, pair_lanes())
    return [sums[32 * i : 32 * i + 32] for i in range(len(planes))]


def spread(planes, scratch):
    wide = dot(jnp.concatenate(planes, axis=0), spread_lanes())
    scratch[pl.ds(0, 32 * len(planes), 2), :] = wide
    scratch[pl.ds(1, 32 * len(planes), 2), :] = wide
    return [scratch[64 * i : 64 * i + 64, :] for i in range(len(planes))]


def left(shape):
    return lax.broadcasted_iota(jnp.int32, shape, 1) < 64


def pack(x):
    return jnp.where(left((16, 128)), x[:16], x[16:])


def unpack(t):
    other = turn(t, 64, 1)
    here = left((16, 128))
    return jnp.concatenate([jnp.where(here, t, other), jnp.where(here, other, t)], axis=0)


def coarse_slope(below, centre, above, coef):
    return 0.25 * (around(centre) + below + above - 6.0 * centre) + coef * cubic(centre)


def mix(row, nodes):
    return QUAD[row][0] * nodes[0] + QUAD[row][1] * nodes[1] + QUAD[row][2] * nodes[2]


def packets(spot, up, down, inners, outers):
    def put(to_inner, to_outer):
        for parts, outs in ((to_inner, inners), (to_outer, outers)):
            whole = jnp.concatenate(parts, axis=0)
            half = whole.shape[0] // 2
            outs[0][...] = whole[:half]
            outs[1][...] = whole[half:]

    @pl.when(spot[2] == 0)
    def _():
        put(up, down)

    @pl.when(spot[2] != 0)
    def _():
        put(down, up)


def sides(spot, inner, inner_rest, outer, outer_rest):
    a = jnp.concatenate([inner[...], inner_rest[...]], axis=0)
    b = jnp.concatenate([outer[...], outer_rest[...]], axis=0)
    low = jnp.full(a.shape, spot[2], jnp.int32) == 0
    return jnp.where(low, b, a), jnp.where(low, a, b)


def first_kernel(
    spot, initial, coeff, guess, inner, inner_rest, outer, outer_rest, keep, initial_out, coeff_out, guess_out, scratch
):
    for out, given in ((initial_out, initial), (coeff_out, coeff), (guess_out, guess)):
        out[...] = given[...]
    u = [guess[0], guess[1]]
    c = [coeff[0], coeff[1]]
    both = u[0] + u[1]
    total = around(both) - 5.0 * both + c[0] * cubic(u[0]) + c[1] * cubic(u[1])
    own, value, coef, start = squash([total, both, c[0] + c[1], initial[0] + initial[1]], scratch)
    value, coef, start = 0.125 * value, 0.125 * coef, 0.125 * start
    packets(spot, u + [c[1], pack(start)], u + [c[0], pack(start)], [inner, inner_rest], [outer, outer_rest])
    keep[0] = own
    keep[1] = value
    keep[2] = coef
    keep[3] = start


def own_k(own, value0, value0_sides, coef):
    slope = coarse_slope(value0_sides[0], value0, value0_sides[1], coef)
    return [(STEP / 8.0) * own[m] - (STEP * QUAD[m + 1][0]) * slope for m in (0, 1)]


def complete_first(
    spot, inner, inner_rest, outer, outer_rest, kept, initial, received, owned, beside, beyond, mine, keep, begin_out,
    scratch,
):
    below, above = sides(spot, inner, inner_rest, outer, outer_rest)
    begin = starting(spot, initial, received)
    own, value, coef, start = (kept[i] for i in range(4))
    low, high, value_low, value_high, value_begin = squash(
        [below[64:128, :], above[0:64, :], below[0:64, :] + below[64:128, :], above[0:64, :] + above[64:128, :],
         begin[0] + begin[1]],
        scratch,
    )
    value_low, value_high = 0.125 * value_low, 0.125 * value_high
    start_low, start_high = unpack(below[192:208, :]), unpack(above[192:208, :])
    start_slope = coarse_slope(start_low, start, start_high, coef)
    whole = own + low + high
    k = own_k([ROWSUM[1] * whole, ROWSUM[2] * whole], value, [value_low, value_high], coef)
    first = jnp.full((32, 128), spot[0], jnp.int32) == 0
    given = [pack(k[m - 1] + jnp.where(first, start + (STEP * QUAD[m][0]) * start_slope, 0.0)) for m in (2, 1)]
    given += [pack(coef), pack(0.125 * value_begin), pack(start)]
    mine[...] = given[0]
    odd = jnp.full((64, 128), spot[3], jnp.int32) == 1
    for i, part in enumerate(given):
        for out in (owned, beside, beyond):
            out[16 * i : 16 * i + 16, :] = part
    beside[80:144, :] = jnp.where(odd, begin[0], begin[1])
    beyond[80:144, :] = jnp.where(odd, begin[1], begin[0])
    for x in (0, 1):
        owned[80 + 64 * x : 144 + 64 * x, :] = begin[x]
        begin_out[x] = begin[x]
    for i, part in enumerate([k[0], k[1], start, start_slope, start_low, start_high, value_low, value_high]):
        keep[i] = part


def plane(spot, rows, owned, beside, beyond, sections, side, item, up=False):
    odd = spot[3]
    if item < SECTIONS:
        if side == 0:
            return sections[item, 0:16, :]
        at = jnp.where(odd == 1, side, 3 - side)
        return sections[item, pl.ds(pl.multiple_of(16 * at, 16), 16), :]
    row = rows[item]
    if side == 0:
        row += 64 if item >= EDGE and up else 0
        return owned[row : row + 16, :]
    near, far = beside[row : row + 16, :], beyond[row : row + 16, :]
    picked = jnp.full((16, 128), odd, jnp.int32) == (1 if side == 1 else 0)
    return jnp.where(picked, near, far)


def pack_kernel(items, rows):
    total = slots(items)

    def body(spot, owned, beside, beyond, sections, out):
        chip, core = spot[1], spot[2]

        def fill(own_core, away):
            slot = 0
            up = away > 0 or (away == 0 and own_core == 0)
            for side, least in shares(own_core, away):
                for item, reach in items:
                    if reach >= least:
                        part = plane(spot, rows, owned, beside, beyond, sections, side, item, up)
                        out[chip + away, 16 * slot : 16 * slot + 16, :] = part
                        slot += 1

        for own_core in (0, 1):
            for away in range(1 - CHIPS, CHIPS):
                there = jnp.logical_and(chip + away >= 0, chip + away < CHIPS)

                @pl.when(jnp.logical_and(core == own_core, there))
                def _():
                    fill(own_core, away)

    return body, total


def sweep(spot, items, rows, owned, beside, beyond, sections, windows, swapped, coefs, started, line, history):
    core = spot[2]
    place = 2 * spot[1] + core
    rank = {item: i for i, (item, _) in enumerate(items)}
    reach_of = dict(items)

    def fetch(item, w, whole=False):
        if w in (0, -BLOCK, BLOCK):
            side = {0: 0, -BLOCK: 1, BLOCK: 2}[w]
            return unpack(plane(spot, rows, owned, beside, beyond, sections, side, item))
        at = place + w
        if w > 0:
            outside, least = at >= BLOCK, [max(1, BLOCK - w - i) for i in (0, 1)]
        else:
            outside, least = at < 0, [max(1, BLOCK - 1 + w + i) for i in (0, 1)]
        before = jnp.where(core == 0, count(items, least[0]), count(items, least[1]))
        slot = rank[item] + jnp.where(outside, before, 0)
        source = windows if w % 2 == 0 else swapped
        found = source[(at & (BLOCK - 1)) >> 1, pl.ds(pl.multiple_of(16 * slot, 16), 16), :]
        return found if whole else unpack(found)

    if COEF in rank:
        for w in range(-7, 8):
            coefs[w + 7] = fetch(COEF, w)
    outermost = [fetch(INITIAL, w) if INITIAL in rank else jnp.zeros((32, 128), F32) for w in (-2, 2)]
    history[0] = outermost[0]
    history[1] = started[4]
    history[2] = started[2]
    history[3] = started[5]
    history[4] = outermost[1]
    for w in range(-8, 9):
        value = fetch(0, w)
        line[0, w + 8] = value
        if abs(w) <= 2:
            history[5 + w + 2] = value
    for k in range(1, SECTIONS):
        if k not in rank:
            continue
        old, new = (k - 1) % 2, k % 2
        for w in range(-reach_of[k], reach_of[k] + 1):
            centre = line[old, w + 8]
            slope = coarse_slope(line[old, w + 7], centre, line[old, w + 9], coefs[w + 7])
            value = centre + (STEP * QUAD[2][0]) * slope + fetch(k, w)
            line[new, w + 8] = value
            if abs(w) <= 2:
                history[5 * (k + 1) + w + 2] = value
    return fetch


def correct(spot, fetch, coefs, started, history, kept, values, nodes, below, above, coeff, begin, scratch):
    section = spot[0]
    s = [history[5 * section + i] for i in range(5)]
    slope = [coarse_slope(s[i], s[i + 1], s[i + 2], coefs[6 + i]) for i in range(3)]
    later = jnp.full((32, 128), section, jnp.int32) > 0
    edges = []
    for w, i in ((-1, 0), (1, 2)):
        for m, near in ((1, NEAR1), (2, NEAR2)):
            edges.append(fetch(near, w) + jnp.where(later, ROWSUM[m] * s[i + 1] + START[m] * slope[i], 0.0))
    coarse = [s[2]] + [s[2] + (STEP * QUAD[m][0]) * slope[1] + kept[m - 1] for m in (1, 2)]
    wide = spread([coarse[j] - values[j] for j in range(3)] + edges, scratch)
    fixed = [[nodes[j][x] + wide[j] for x in (0, 1)] for j in range(3)]
    rates = [[cubic(fixed[j][x]) for x in (0, 1)] for j in range(3)]
    fresh = []
    for m in (1, 2):
        sums = [mix(m, [fixed[j][x] for j in range(3)]) for x in (0, 1)]
        ends = [below[m - 1] + wide[2 + m], above[m - 1] + wide[4 + m]]
        fresh.append([])
        for x in (0, 1):
            change = around(sums[x]) - 6.0 * sums[x] + sums[1 - x] + ends[x]
            change = change + coeff[x] * mix(m, [rates[j][x] for j in range(3)])
            fresh[-1].append(begin[x] + STEP * change)
    return coarse[2], fresh


def starting(spot, initial, received):
    first = jnp.full((64, 128), spot[0], jnp.int32) == 0
    return [jnp.where(first, initial[x], received[x]) for x in (0, 1)]


def previous_end(section, fetch, coefs, history, starts, coeff, initial, earlier, scratch):
    before = jnp.maximum(section - 1, 0)
    s = [history[5 * before + i] for i in range(5)]
    value = [fetch(BEGIN, w) for w in range(-2, 3)]
    shift = []
    for i in range(3):
        two = history[5 * section + 1 + i]
        slope = coarse_slope(s[i], s[i + 1], s[i + 2], coefs[6 + i])
        slope = slope - coarse_slope(value[i], value[i + 1], value[i + 2], coefs[6 + i])
        one = 0.5 * (s[i + 1] + two) + (STEP * (QUAD[1][0] - 0.5 * QUAD[2][0])) * slope
        shift.append([s[i + 1] - value[i + 1], one - value[i + 1], two - value[i + 1]])
    wide = spread([mix(2, shift[0])] + shift[1] + [mix(2, shift[2])], scratch)
    fixed = [[starts[x] + wide[1 + j] for j in range(3)] for x in (1, 2)]
    sums = [ROWSUM[2] * starts[0] + wide[0], mix(2, fixed[0]), mix(2, fixed[1]), ROWSUM[2] * starts[3] + wide[4]]
    number = jnp.full((64, 128), section, jnp.int32)
    out = []
    for x in (0, 1):
        change = around(sums[x + 1]) - 6.0 * sums[x + 1] + sums[x] + sums[x + 2]
        change = change + coeff[x] * mix(2, [cubic(part) for part in fixed[x]])
        end = jnp.where(number == 1, initial[x], earlier[x]) + STEP * change
        out.append(jnp.where(number == 0, initial[x], end))
    return out


def finish_first(
    spot, owned, beside, beyond, sections, windows, swapped, started, kept, inner, inner_rest, outer, outer_rest,
    initial, coeff, guess, begin, earlier, middle_out, end_out, ends, begin_out, keep, owned_out, mine, coefs, line, history, scratch,
):
    fetch = sweep(
        spot, ITEMS[0], ROWS[0], owned, beside, beyond, sections, windows, swapped, coefs, started, line, history
    )
    below, above = sides(spot, inner, inner_rest, outer, outer_rest)
    section = spot[0]
    later = jnp.full((32, 128), section, jnp.int32) > 0
    s = [history[5 * section + i] for i in range(5)]
    slope = [coarse_slope(s[i], s[i + 1], s[i + 2], coefs[6 + i]) for i in range(3)]
    step = [s[i + 1] + (STEP * QUAD[1][0]) * slope[i] for i in range(3)]
    value = [started[6], kept[1], started[7]]
    coarse = []
    for i in range(3):
        if i == 1:
            one, two = step[1] + started[0], s[2] + (STEP * QUAD[2][0]) * slope[1] + started[1]
        else:
            one = fetch(NEAR1, i - 1) + jnp.where(later, step[i], 0.0)
            two = history[5 * section + 6 + i]
        coarse += [s[i + 1] - value[i], one - value[i], two - value[i]]
    wide = spread(coarse, scratch)
    u = [below[0:64, :], below[64:128, :], guess[0], guess[1], above[0:64, :], above[64:128, :]]
    c = [None, below[128:192, :], coeff[0], coeff[1], above[128:192, :], None]
    b = [None] + [None] * 4 + [None]
    b[2], b[3] = begin[0], begin[1]
    for x, w in ((1, -1), (4, 1)):
        b[x] = jnp.concatenate([fetch(EDGE + i, w, whole=True) for i in range(4)], axis=0)
    begin_next = previous_end(section, fetch, coefs, history, b[1:5], coeff, initial, earlier, scratch)
    for x in (0, 1):
        begin_out[x] = begin_next[x]
    fixed = [[u[x] + wide[3 * (x // 2) + j] for j in range(3)] for x in range(6)]
    nodes = [None] + [[b[x]] for x in range(1, 5)] + [None]
    rates = [None] + [[cubic(fixed[x][j]) for j in range(3)] for x in range(1, 5)] + [None]
    for m in (1, 2):
        sums = [mix(m, fixed[x]) for x in range(6)]
        for x in range(1, 5):
            change = around(sums[x]) - 6.0 * sums[x] + sums[x - 1] + sums[x + 1] + c[x] * mix(m, rates[x])
            nodes[x].append(b[x] + STEP * change)
    for x in (0, 1):
        middle_out[x] = nodes[x + 2][1]
        end_out[x] = nodes[x + 2][2]
    rates = [[cubic(nodes[x][j]) for j in range(3)] for x in (2, 3)]
    planes = []
    for m in (1, 2):
        sums = [mix(m, nodes[x]) for x in range(1, 5)]
        ends[m - 1] = sums[0]
        ends[m + 1] = sums[3]
        both = sums[1] + sums[2]
        planes.append(
            around(both) - 5.0 * both + sums[0] + sums[3] + c[2] * mix(m, rates[0]) + c[3] * mix(m, rates[1])
        )
    for j in range(3):
        planes.append(nodes[2][j] + nodes[3][j])
    small = squash(planes, scratch)
    values = [0.125 * small[2 + j] for j in range(3)]
    k = own_k(small[:2], values[0], [fetch(BEGIN, -1), fetch(BEGIN, 1)], kept[2])
    first = jnp.logical_not(later)
    ours = pack(k[1] + jnp.where(first, started[2] + (STEP * QUAD[2][0]) * started[3], 0.0))
    owned_out[0:16, :] = ours
    mine[...] = ours
    for m in (1, 2):
        near = QUAD[m][1] * k[0] + QUAD[m][2] * k[1] - mix(m, values)
        near = near + jnp.where(first, ROWSUM[m] * started[2] + START[m] * started[3], 0.0)
        owned_out[16 * m : 16 * m + 16, :] = pack(near)
    for i, part in enumerate(values + k):
        keep[i] = part


def finish_second(
    spot, owned, beside, beyond, sections, windows, swapped, started, kept, ends, coeff, begin_in, middle_in, end_in,
    begin, coefs, fresh_out, coarse_out, line, history, scratch,
):
    fetch = sweep(
        spot, ITEMS[1], ROWS[1], owned, beside, beyond, sections, windows, swapped, coefs, started, line, history
    )
    nodes = [[part[0], part[1]] for part in (begin_in, middle_in, end_in)]
    end, fresh = correct(
        spot, fetch, coefs, started, history, (kept[3], kept[4]), [kept[0], kept[1], kept[2]], nodes,
        [ends[0], ends[1]], [ends[2], ends[3]], [coeff[0], coeff[1]], [begin[0], begin[1]], scratch,
    )
    for m in (0, 1):
        for x in (0, 1):
            fresh_out[m, x] = fresh[m][x]
    coarse_out[...] = end[:, :64]


def run(body, args, outs, scratch=(), name=None, first=False, last=False):
    def placed(*refs):
        spot = [lax.axis_index(a) for a in ("tm", "chip", "core", "block")]
        body(spot[:3] + [spot[3] & 1], *refs)

    return pl.pallas_call(
        placed,
        out_shape=[jax.ShapeDtypeStruct(shape, F32) if last else pltpu.VMEM(shape, F32) for shape in outs],
        in_specs=[pl.BlockSpec(memory_space=pltpu.VMEM)] * len(args),
        out_specs=[pl.BlockSpec(memory_space=pltpu.VMEM)] * len(outs),
        scratch_shapes=[pltpu.VMEM(shape, F32) for shape in scratch],
        compiler_params=None if first else pltpu.CompilerParams(vmem_limit_bytes=16 << 20),
        name=name,
    )(*(a if first else pltpu.with_memory_space_constraint(a, pltpu.VMEM) for a in args))


class Links:
    call = staticmethod(run)

    @staticmethod
    def swap_block(x, row):
        n = lax.axis_size("block")
        pairs = [(i, i ^ 1 if row else (i + 2 * (i % 2) - 1) % n) for i in range(n)]
        return lax.ppermute(x, "block", pairs)

    @staticmethod
    def swap_inner(x):
        return lax.ppermute(x, "core", [(0, 1), (1, 0)])

    @staticmethod
    def swap_outer(x):
        n = lax.axis_size("block") * BLOCK
        return lax.ppermute(x, ("block", "chip", "core"), [(i, (i + 2 * (i % 2) - 1) % n) for i in range(n)])

    @staticmethod
    def onward(x, by):
        n = lax.axis_size("tm")
        return lax.ppermute(x, "tm", [(i, i + by) for i in range(n - by)])

    @staticmethod
    def sections(x):
        return lax.all_to_all(jnp.broadcast_to(x, (SECTIONS,) + x.shape), "tm", 0, 0)

    @staticmethod
    def block(x):
        return lax.all_to_all(x, "chip", 0, 0)

    @staticmethod
    def together(*values):
        return lax.optimization_barrier(values)

    @staticmethod
    def stack(*planes):
        return jnp.concatenate([p[:16] for p in planes], axis=0)


def iterate(links, initial, coeff, guess):
    coarse, slab = (32, 128), (2, 64, 128)
    work = [(2, 17) + coarse, (45,) + coarse]

    def windows(owned, beside, beyond, mine, iteration):
        sections = links.sections(links.stack(mine, beside, beyond))
        body, total = pack_kernel(ITEMS[iteration], ROWS[iteration])
        (parcels,) = links.call(
            body, (owned, beside, beyond, sections), [(CHIPS, 16 * total, 128)], name="hand_out"
        )
        parcels = links.block(parcels)
        return owned, beside, beyond, sections, parcels, links.swap_inner(parcels)

    sent = guess
    inner, inner_rest, outer, outer_rest, kept, initial, coeff, guess = links.call(
        first_kernel, (initial, coeff, guess),
        [(104, 128)] * 4 + [(4,) + coarse, slab, slab, slab], [(256, 128)], name="first", first=True,
    )
    outer, outer_rest, inner, inner_rest, received = links.together(
        links.swap_outer(outer), links.swap_outer(outer_rest), links.swap_inner(inner), links.swap_inner(inner_rest),
        links.onward(sent, 1),
    )
    owned, beside, beyond, mine, started, begin = links.call(
        complete_first, (inner, inner_rest, outer, outer_rest, kept, initial, received),
        [(208, 128), (144, 128), (144, 128), (16, 128), (8,) + coarse, slab], [(320, 128)], name="complete_first",
    )
    beyond, beside, earlier = links.together(
        links.swap_block(beyond, False), links.swap_block(beside, True), links.onward(sent, 2)
    )
    middle, end, ends, begin_next, kept, owned, mine, coefs = links.call(
        finish_first,
        (*windows(owned, beside, beyond, mine, 0), started, kept, inner, inner_rest, outer, outer_rest, initial,
         coeff, guess, begin, earlier),
        [slab, slab, (4, 64, 128), slab, (5,) + coarse, (48, 128), (16, 128), (15,) + coarse],
        work + [(576, 128)],
        name="finish_first",
    )
    beside, beyond = links.swap_block(owned, True), links.swap_block(owned, False)
    fine, coarse_end = links.call(
        finish_second,
        (*windows(owned, beside, beyond, mine, 1), started, kept, ends, coeff, begin, middle, end, begin_next, coefs),
        [(2, 2, 64, 128), (32, 64)],
        work + [(448, 128)],
        name="finish_second",
        last=True,
    )
    return fine, coarse_end


def on_device(initial, coeff, guess):
    fine, coarse_end = iterate(Links, initial, coeff, guess[0])
    return fine[None], coarse_end[None, None]


def solution(mesh):
    split = Mesh(
        mesh.devices.reshape(mesh.shape["tm"], mesh.shape["space"] // BLOCK, CHIPS, 2), ("tm", "block", "chip", "core")
    )
    space = ("block", "chip", "core")
    return jax.shard_map(
        on_device,
        mesh=split,
        in_specs=(P(space, None, None), P(space, None, None), P("tm", space, None, None)),
        out_specs=(P("tm", None, space, None, None), P("tm", space, None, None)),
        check_vma=False,
    )
```

```python
import jax
import jax.numpy as jnp
from jax import lax
from jax.experimental import pallas as pl
from jax.experimental.pallas import tpu as pltpu
from jax.sharding import Mesh, PartitionSpec as P

STEP = 0.06
QUAD = ((0.0, 0.0, 0.0), (5.0 / 24.0, 1.0 / 3.0, -1.0 / 24.0), (1.0 / 6.0, 2.0 / 3.0, 1.0 / 6.0))
ROWSUM = tuple(sum(row) for row in QUAD)
START = tuple(STEP * (row[1] * QUAD[1][0] + row[2] * QUAD[2][0]) for row in QUAD)
SECTIONS = 8
BLOCK = 8
CHIPS = BLOCK // 2
F32 = jnp.float32

COEF, NEAR1, NEAR2, BEGIN, INITIAL, EDGE = 10, 11, 12, 13, 14, 15
ITEMS = (
    ((0, 8), (1, 7), (COEF, 7), (2, 6), (3, 5), (4, 4), (5, 3), (6, 2), (BEGIN, 2), (INITIAL, 2), (7, 1),
     (NEAR1, 1))
    + tuple((EDGE + i, 1) for i in range(4)),
    ((0, 8), (1, 7), (2, 6), (3, 5), (4, 4), (5, 3), (6, 2), (NEAR1, 1), (NEAR2, 1)),
)
ROWS = ({NEAR1: 16, COEF: 32, BEGIN: 48, INITIAL: 64, **{EDGE + i: 80 + 16 * i for i in range(4)}}, {NEAR1: 16, NEAR2: 32})


def count(items, distance):
    return sum(1 for _, reach in items if reach >= distance)


def shares(core, ahead):
    if ahead == 0:
        return (0, 1), (2 - core, BLOCK - 1)
    if ahead > 0:
        return (0, 2 * ahead - core), (2, BLOCK - 1 - 2 * ahead + core)
    return (0, -2 * ahead + core - 1), (1, BLOCK + 2 * ahead - core)


def slots(items):
    return max(sum(count(items, least) for _, least in shares(core, a)) for core in (0, 1) for a in range(-3, 4))


def turn(x, by, axis):
    return pltpu.roll(x, by % x.shape[axis], axis)


def around(x):
    return turn(x, 1, 0) + turn(x, -1, 0) + turn(x, 1, 1) + turn(x, -1, 1)


def cubic(u):
    return u - u * u * u


def dot(a, b):
    return jnp.dot(a, b, precision=lax.Precision.HIGHEST, preferred_element_type=F32)


def pair_lanes():
    z = lax.broadcasted_iota(jnp.int32, (128, 128), 0)
    c = lax.broadcasted_iota(jnp.int32, (128, 128), 1)
    return jnp.where((z >> 1) == (c & 63), 1.0, 0.0).astype(F32)


def spread_lanes():
    c = lax.broadcasted_iota(jnp.int32, (128, 128), 0)
    z = lax.broadcasted_iota(jnp.int32, (128, 128), 1)
    return jnp.where((z >> 1) == c, 1.0, 0.0).astype(F32)


def squash(planes, scratch):
    for i, plane in enumerate(planes):
        scratch[64 * i : 64 * i + 64, :] = plane
    both = scratch[pl.ds(0, 32 * len(planes), 2), :] + scratch[pl.ds(1, 32 * len(planes), 2), :]
    sums = dot(both, pair_lanes())
    return [sums[32 * i : 32 * i + 32] for i in range(len(planes))]


def spread(planes, scratch):
    wide = dot(jnp.concatenate(planes, axis=0), spread_lanes())
    scratch[pl.ds(0, 32 * len(planes), 2), :] = wide
    scratch[pl.ds(1, 32 * len(planes), 2), :] = wide
    return [scratch[64 * i : 64 * i + 64, :] for i in range(len(planes))]


def left(shape):
    return lax.broadcasted_iota(jnp.int32, shape, 1) < 64


def pack(x):
    return jnp.where(left((16, 128)), x[:16], x[16:])


def unpack(t):
    other = turn(t, 64, 1)
    here = left((16, 128))
    return jnp.concatenate([jnp.where(here, t, other), jnp.where(here, other, t)], axis=0)


def coarse_slope(below, centre, above, coef):
    return 0.25 * (around(centre) + below + above - 6.0 * centre) + coef * cubic(centre)


def mix(row, nodes):
    return QUAD[row][0] * nodes[0] + QUAD[row][1] * nodes[1] + QUAD[row][2] * nodes[2]


def packets(spot, up, down, inners, outers):
    def put(to_inner, to_outer):
        for parts, outs in ((to_inner, inners), (to_outer, outers)):
            whole = jnp.concatenate(parts, axis=0)
            half = whole.shape[0] // 2
            outs[0][...] = whole[:half]
            outs[1][...] = whole[half:]

    @pl.when(spot[2] == 0)
    def _():
        put(up, down)

    @pl.when(spot[2] != 0)
    def _():
        put(down, up)


def sides(spot, inner, inner_rest, outer, outer_rest):
    a = jnp.concatenate([inner[...], inner_rest[...]], axis=0)
    b = jnp.concatenate([outer[...], outer_rest[...]], axis=0)
    low = jnp.full(a.shape, spot[2], jnp.int32) == 0
    return jnp.where(low, b, a), jnp.where(low, a, b)


def first_kernel(
    spot, initial, coeff, guess, inner, inner_rest, outer, outer_rest, keep, initial_out, coeff_out, guess_out, scratch
):
    for out, given in ((initial_out, initial), (coeff_out, coeff), (guess_out, guess)):
        out[...] = given[...]
    u = [guess[0], guess[1]]
    c = [coeff[0], coeff[1]]
    both = u[0] + u[1]
    total = around(both) - 5.0 * both + c[0] * cubic(u[0]) + c[1] * cubic(u[1])
    own, value, coef, start = squash([total, both, c[0] + c[1], initial[0] + initial[1]], scratch)
    value, coef, start = 0.125 * value, 0.125 * coef, 0.125 * start
    packets(spot, u + [c[1], pack(start)], u + [c[0], pack(start)], [inner, inner_rest], [outer, outer_rest])
    keep[0] = own
    keep[1] = value
    keep[2] = coef
    keep[3] = start


def own_k(own, value0, value0_sides, coef):
    slope = coarse_slope(value0_sides[0], value0, value0_sides[1], coef)
    return [(STEP / 8.0) * own[m] - (STEP * QUAD[m + 1][0]) * slope for m in (0, 1)]


def complete_first(
    spot, inner, inner_rest, outer, outer_rest, kept, initial, received, owned, beside, beyond, mine, keep, begin_out,
    scratch,
):
    below, above = sides(spot, inner, inner_rest, outer, outer_rest)
    begin = starting(spot, initial, received)
    own, value, coef, start = (kept[i] for i in range(4))
    low, high, value_low, value_high, value_begin = squash(
        [below[64:128, :], above[0:64, :], below[0:64, :] + below[64:128, :], above[0:64, :] + above[64:128, :],
         begin[0] + begin[1]],
        scratch,
    )
    value_low, value_high = 0.125 * value_low, 0.125 * value_high
    start_low, start_high = unpack(below[192:208, :]), unpack(above[192:208, :])
    start_slope = coarse_slope(start_low, start, start_high, coef)
    whole = own + low + high
    k = own_k([ROWSUM[1] * whole, ROWSUM[2] * whole], value, [value_low, value_high], coef)
    first = jnp.full((32, 128), spot[0], jnp.int32) == 0
    given = [pack(k[m - 1] + jnp.where(first, start + (STEP * QUAD[m][0]) * start_slope, 0.0)) for m in (2, 1)]
    given += [pack(coef), pack(0.125 * value_begin), pack(start)]
    mine[...] = given[0]
    odd = jnp.full((64, 128), spot[3], jnp.int32) == 1
    for i, part in enumerate(given):
        for out in (owned, beside, beyond):
            out[16 * i : 16 * i + 16, :] = part
    beside[80:144, :] = jnp.where(odd, begin[0], begin[1])
    beyond[80:144, :] = jnp.where(odd, begin[1], begin[0])
    for x in (0, 1):
        owned[80 + 64 * x : 144 + 64 * x, :] = begin[x]
        begin_out[x] = begin[x]
    for i, part in enumerate([k[0], k[1], start, start_slope, start_low, start_high, value_low, value_high]):
        keep[i] = part


def plane(spot, rows, owned, beside, beyond, sections, side, item, up=False):
    odd = spot[3]
    if item < SECTIONS:
        if side == 0:
            return sections[item, 0:16, :]
        at = jnp.where(odd == 1, side, 3 - side)
        return sections[item, pl.ds(pl.multiple_of(16 * at, 16), 16), :]
    row = rows[item]
    if side == 0:
        row += 64 if item >= EDGE and up else 0
        return owned[row : row + 16, :]
    near, far = beside[row : row + 16, :], beyond[row : row + 16, :]
    picked = jnp.full((16, 128), odd, jnp.int32) == (1 if side == 1 else 0)
    return jnp.where(picked, near, far)


def pack_kernel(items, rows):
    total = slots(items)

    def body(spot, owned, beside, beyond, sections, out):
        chip, core = spot[1], spot[2]

        def fill(own_core, away):
            slot = 0
            up = away > 0 or (away == 0 and own_core == 0)
            for side, least in shares(own_core, away):
                for item, reach in items:
                    if reach >= least:
                        part = plane(spot, rows, owned, beside, beyond, sections, side, item, up)
                        out[chip + away, 16 * slot : 16 * slot + 16, :] = part
                        slot += 1

        for own_core in (0, 1):
            for away in range(1 - CHIPS, CHIPS):
                there = jnp.logical_and(chip + away >= 0, chip + away < CHIPS)

                @pl.when(jnp.logical_and(core == own_core, there))
                def _():
                    fill(own_core, away)

    return body, total


def sweep(spot, items, rows, owned, beside, beyond, sections, windows, swapped, coefs, started, line, history):
    core = spot[2]
    place = 2 * spot[1] + core
    rank = {item: i for i, (item, _) in enumerate(items)}
    reach_of = dict(items)

    def fetch(item, w, whole=False):
        if w in (0, -BLOCK, BLOCK):
            side = {0: 0, -BLOCK: 1, BLOCK: 2}[w]
            return unpack(plane(spot, rows, owned, beside, beyond, sections, side, item))
        at = place + w
        if w > 0:
            outside, least = at >= BLOCK, [max(1, BLOCK - w - i) for i in (0, 1)]
        else:
            outside, least = at < 0, [max(1, BLOCK - 1 + w + i) for i in (0, 1)]
        before = jnp.where(core == 0, count(items, least[0]), count(items, least[1]))
        slot = rank[item] + jnp.where(outside, before, 0)
        source = windows if w % 2 == 0 else swapped
        found = source[(at & (BLOCK - 1)) >> 1, pl.ds(pl.multiple_of(16 * slot, 16), 16), :]
        return found if whole else unpack(found)

    if COEF in rank:
        for w in range(-7, 8):
            coefs[w + 7] = fetch(COEF, w)
    outermost = [fetch(INITIAL, w) if INITIAL in rank else jnp.zeros((32, 128), F32) for w in (-2, 2)]
    history[0] = outermost[0]
    history[1] = started[4]
    history[2] = started[2]
    history[3] = started[5]
    history[4] = outermost[1]
    for w in range(-8, 9):
        value = fetch(0, w)
        line[0, w + 8] = value
        if abs(w) <= 2:
            history[5 + w + 2] = value
    for k in range(1, SECTIONS):
        if k not in rank:
            continue
        old, new = (k - 1) % 2, k % 2
        for w in range(-reach_of[k], reach_of[k] + 1):
            centre = line[old, w + 8]
            slope = coarse_slope(line[old, w + 7], centre, line[old, w + 9], coefs[w + 7])
            value = centre + (STEP * QUAD[2][0]) * slope + fetch(k, w)
            line[new, w + 8] = value
            if abs(w) <= 2:
                history[5 * (k + 1) + w + 2] = value
    return fetch


def correct(spot, fetch, coefs, started, history, kept, values, nodes, below, above, coeff, begin, scratch):
    section = spot[0]
    s = [history[5 * section + i] for i in range(5)]
    slope = [coarse_slope(s[i], s[i + 1], s[i + 2], coefs[6 + i]) for i in range(3)]
    later = jnp.full((32, 128), section, jnp.int32) > 0
    edges = []
    for w, i in ((-1, 0), (1, 2)):
        for m, near in ((1, NEAR1), (2, NEAR2)):
            edges.append(fetch(near, w) + jnp.where(later, ROWSUM[m] * s[i + 1] + START[m] * slope[i], 0.0))
    coarse = [s[2]] + [s[2] + (STEP * QUAD[m][0]) * slope[1] + kept[m - 1] for m in (1, 2)]
    wide = spread([coarse[j] - values[j] for j in range(3)] + edges, scratch)
    fixed = [[nodes[j][x] + wide[j] for x in (0, 1)] for j in range(3)]
    rates = [[cubic(fixed[j][x]) for x in (0, 1)] for j in range(3)]
    fresh = []
    for m in (1, 2):
        sums = [mix(m, [fixed[j][x] for j in range(3)]) for x in (0, 1)]
        ends = [below[m - 1] + wide[2 + m], above[m - 1] + wide[4 + m]]
        fresh.append([])
        for x in (0, 1):
            change = around(sums[x]) - 6.0 * sums[x] + sums[1 - x] + ends[x]
            change = change + coeff[x] * mix(m, [rates[j][x] for j in range(3)])
            fresh[-1].append(begin[x] + STEP * change)
    return coarse[2], fresh


def starting(spot, initial, received):
    first = jnp.full((64, 128), spot[0], jnp.int32) == 0
    return [jnp.where(first, initial[x], received[x]) for x in (0, 1)]


def previous_end(section, fetch, coefs, history, starts, coeff, initial, earlier, scratch):
    before = jnp.maximum(section - 1, 0)
    s = [history[5 * before + i] for i in range(5)]
    value = [fetch(BEGIN, w) for w in range(-2, 3)]
    shift = []
    for i in range(3):
        two = history[5 * section + 1 + i]
        slope = coarse_slope(s[i], s[i + 1], s[i + 2], coefs[6 + i])
        slope = slope - coarse_slope(value[i], value[i + 1], value[i + 2], coefs[6 + i])
        one = 0.5 * (s[i + 1] + two) + (STEP * (QUAD[1][0] - 0.5 * QUAD[2][0])) * slope
        shift.append([s[i + 1] - value[i + 1], one - value[i + 1], two - value[i + 1]])
    wide = spread([mix(2, shift[0])] + shift[1] + [mix(2, shift[2])], scratch)
    fixed = [[starts[x] + wide[1 + j] for j in range(3)] for x in (1, 2)]
    sums = [ROWSUM[2] * starts[0] + wide[0], mix(2, fixed[0]), mix(2, fixed[1]), ROWSUM[2] * starts[3] + wide[4]]
    number = jnp.full((64, 128), section, jnp.int32)
    out = []
    for x in (0, 1):
        change = around(sums[x + 1]) - 6.0 * sums[x + 1] + sums[x] + sums[x + 2]
        change = change + coeff[x] * mix(2, [cubic(part) for part in fixed[x]])
        end = jnp.where(number == 1, initial[x], earlier[x]) + STEP * change
        out.append(jnp.where(number == 0, initial[x], end))
    return out


def finish_first(
    spot, owned, beside, beyond, sections, windows, swapped, started, kept, inner, inner_rest, outer, outer_rest,
    initial, coeff, guess, begin, earlier, middle_out, end_out, ends, begin_out, keep, owned_out, mine, coefs, line, history, scratch,
):
    fetch = sweep(
        spot, ITEMS[0], ROWS[0], owned, beside, beyond, sections, windows, swapped, coefs, started, line, history
    )
    below, above = sides(spot, inner, inner_rest, outer, outer_rest)
    section = spot[0]
    later = jnp.full((32, 128), section, jnp.int32) > 0
    s = [history[5 * section + i] for i in range(5)]
    slope = [coarse_slope(s[i], s[i + 1], s[i + 2], coefs[6 + i]) for i in range(3)]
    step = [s[i + 1] + (STEP * QUAD[1][0]) * slope[i] for i in range(3)]
    value = [started[6], kept[1], started[7]]
    coarse = []
    for i in range(3):
        if i == 1:
            one, two = step[1] + started[0], s[2] + (STEP * QUAD[2][0]) * slope[1] + started[1]
        else:
            one = fetch(NEAR1, i - 1) + jnp.where(later, step[i], 0.0)
            two = history[5 * section + 6 + i]
        coarse += [s[i + 1] - value[i], one - value[i], two - value[i]]
    wide = spread(coarse, scratch)
    u = [below[0:64, :], below[64:128, :], guess[0], guess[1], above[0:64, :], above[64:128, :]]
    c = [None, below[128:192, :], coeff[0], coeff[1], above[128:192, :], None]
    b = [None] + [None] * 4 + [None]
    b[2], b[3] = begin[0], begin[1]
    for x, w in ((1, -1), (4, 1)):
        b[x] = jnp.concatenate([fetch(EDGE + i, w, whole=True) for i in range(4)], axis=0)
    begin_next = previous_end(section, fetch, coefs, history, b[1:5], coeff, initial, earlier, scratch)
    for x in (0, 1):
        begin_out[x] = begin_next[x]
    fixed = [[u[x] + wide[3 * (x // 2) + j] for j in range(3)] for x in range(6)]
    nodes = [None] + [[b[x]] for x in range(1, 5)] + [None]
    rates = [None] + [[cubic(fixed[x][j]) for j in range(3)] for x in range(1, 5)] + [None]
    for m in (1, 2):
        sums = [mix(m, fixed[x]) for x in range(6)]
        for x in range(1, 5):
            change = around(sums[x]) - 6.0 * sums[x] + sums[x - 1] + sums[x + 1] + c[x] * mix(m, rates[x])
            nodes[x].append(b[x] + STEP * change)
    for x in (0, 1):
        middle_out[x] = nodes[x + 2][1]
        end_out[x] = nodes[x + 2][2]
    rates = [[cubic(nodes[x][j]) for j in range(3)] for x in (2, 3)]
    planes = []
    for m in (1, 2):
        sums = [mix(m, nodes[x]) for x in range(1, 5)]
        ends[m - 1] = sums[0]
        ends[m + 1] = sums[3]
        both = sums[1] + sums[2]
        planes.append(
            around(both) - 5.0 * both + sums[0] + sums[3] + c[2] * mix(m, rates[0]) + c[3] * mix(m, rates[1])
        )
    for j in range(3):
        planes.append(nodes[2][j] + nodes[3][j])
    small = squash(planes, scratch)
    values = [0.125 * small[2 + j] for j in range(3)]
    k = own_k(small[:2], values[0], [fetch(BEGIN, -1), fetch(BEGIN, 1)], kept[2])
    first = jnp.logical_not(later)
    ours = pack(k[1] + jnp.where(first, started[2] + (STEP * QUAD[2][0]) * started[3], 0.0))
    owned_out[0:16, :] = ours
    mine[...] = ours
    for m in (1, 2):
        near = QUAD[m][1] * k[0] + QUAD[m][2] * k[1] - mix(m, values)
        near = near + jnp.where(first, ROWSUM[m] * started[2] + START[m] * started[3], 0.0)
        owned_out[16 * m : 16 * m + 16, :] = pack(near)
    for i, part in enumerate(values + k):
        keep[i] = part


def finish_second(
    spot, owned, beside, beyond, sections, windows, swapped, started, kept, ends, coeff, begin_in, middle_in, end_in,
    begin, coefs, fresh_out, coarse_out, line, history, scratch,
):
    fetch = sweep(
        spot, ITEMS[1], ROWS[1], owned, beside, beyond, sections, windows, swapped, coefs, started, line, history
    )
    nodes = [[part[0], part[1]] for part in (begin_in, middle_in, end_in)]
    end, fresh = correct(
        spot, fetch, coefs, started, history, (kept[3], kept[4]), [kept[0], kept[1], kept[2]], nodes,
        [ends[0], ends[1]], [ends[2], ends[3]], [coeff[0], coeff[1]], [begin[0], begin[1]], scratch,
    )
    for m in (0, 1):
        for x in (0, 1):
            fresh_out[m, x] = fresh[m][x]
    coarse_out[...] = end[:, :64]


def run(body, args, outs, scratch=(), name=None, first=False, last=False):
    def placed(*refs):
        spot = [lax.axis_index(a) for a in ("tm", "chip", "core", "block")]
        body(spot[:3] + [spot[3] & 1], *refs)

    return pl.pallas_call(
        placed,
        out_shape=[jax.ShapeDtypeStruct(shape, F32) if last else pltpu.VMEM(shape, F32) for shape in outs],
        in_specs=[pl.BlockSpec(memory_space=pltpu.VMEM)] * len(args),
        out_specs=[pl.BlockSpec(memory_space=pltpu.VMEM)] * len(outs),
        scratch_shapes=[pltpu.VMEM(shape, F32) for shape in scratch],
        compiler_params=None if first else pltpu.CompilerParams(vmem_limit_bytes=16 << 20),
        name=name,
    )(*(a if first else pltpu.with_memory_space_constraint(a, pltpu.VMEM) for a in args))


class Links:
    call = staticmethod(run)

    @staticmethod
    def swap_block(x, row):
        n = lax.axis_size("block")
        pairs = [(i, i ^ 1 if row else (i + 2 * (i % 2) - 1) % n) for i in range(n)]
        return lax.ppermute(x, "block", pairs)

    @staticmethod
    def swap_inner(x):
        return lax.ppermute(x, "core", [(0, 1), (1, 0)])

    @staticmethod
    def swap_outer(x):
        n = lax.axis_size("block") * BLOCK
        return lax.ppermute(x, ("block", "chip", "core"), [(i, (i + 2 * (i % 2) - 1) % n) for i in range(n)])

    @staticmethod
    def onward(x, by):
        n = lax.axis_size("tm")
        return lax.ppermute(x, "tm", [(i, i + by) for i in range(n - by)])

    @staticmethod
    def sections(x):
        return lax.all_to_all(jnp.broadcast_to(x, (SECTIONS,) + x.shape), "tm", 0, 0)

    @staticmethod
    def block(x):
        return lax.all_to_all(x, "chip", 0, 0)

    @staticmethod
    def together(*values):
        return lax.optimization_barrier(values)

    @staticmethod
    def stack(*planes):
        return jnp.concatenate([p[:16] for p in planes], axis=0)


def iterate(links, initial, coeff, guess):
    coarse, slab = (32, 128), (2, 64, 128)
    work = [(2, 17) + coarse, (45,) + coarse]

    def windows(owned, beside, beyond, mine, iteration):
        sections = links.sections(links.stack(mine, beside, beyond))
        body, total = pack_kernel(ITEMS[iteration], ROWS[iteration])
        (parcels,) = links.call(
            body, (owned, beside, beyond, sections), [(CHIPS, 16 * total, 128)], name="hand_out"
        )
        parcels = links.block(parcels)
        return owned, beside, beyond, sections, parcels, links.swap_inner(parcels)

    sent = guess
    inner, inner_rest, outer, outer_rest, kept, initial, coeff, guess = links.call(
        first_kernel, (initial, coeff, guess),
        [(104, 128)] * 4 + [(4,) + coarse, slab, slab, slab], [(256, 128)], name="first", first=True,
    )
    outer, outer_rest, inner, inner_rest, received = links.together(
        links.swap_outer(outer), links.swap_outer(outer_rest), links.swap_inner(inner), links.swap_inner(inner_rest),
        links.onward(sent, 1),
    )
    owned, beside, beyond, mine, started, begin = links.call(
        complete_first, (inner, inner_rest, outer, outer_rest, kept, initial, received),
        [(208, 128), (144, 128), (144, 128), (16, 128), (8,) + coarse, slab], [(320, 128)], name="complete_first",
    )
    beside, beyond, earlier = links.together(
        links.swap_block(beside, True), links.swap_block(beyond, False), links.onward(sent, 2)
    )
    middle, end, ends, begin_next, kept, owned, mine, coefs = links.call(
        finish_first,
        (*windows(owned, beside, beyond, mine, 0), started, kept, inner, inner_rest, outer, outer_rest, initial,
         coeff, guess, begin, earlier),
        [slab, slab, (4, 64, 128), slab, (5,) + coarse, (48, 128), (16, 128), (15,) + coarse],
        work + [(576, 128)],
        name="finish_first",
    )
    beyond, beside = links.together(links.swap_block(owned, False), links.swap_block(owned, True))
    fine, coarse_end = links.call(
        finish_second,
        (*windows(owned, beside, beyond, mine, 1), started, kept, ends, coeff, begin, middle, end, begin_next, coefs),
        [(2, 2, 64, 128), (32, 64)],
        work + [(448, 128)],
        name="finish_second",
        last=True,
    )
    return fine, coarse_end


def on_device(initial, coeff, guess):
    fine, coarse_end = iterate(Links, initial, coeff, guess[0])
    return fine[None], coarse_end[None, None]


def solution(mesh):
    split = Mesh(
        mesh.devices.reshape(mesh.shape["tm"], mesh.shape["space"] // BLOCK, CHIPS, 2), ("tm", "block", "chip", "core")
    )
    space = ("block", "chip", "core")
    return jax.shard_map(
        on_device,
        mesh=split,
        in_specs=(P(space, None, None), P(space, None, None), P("tm", space, None, None)),
        out_specs=(P("tm", None, space, None, None), P("tm", space, None, None)),
        check_vma=False,
    )
```

```python
import jax
import jax.numpy as jnp
from jax import lax
from jax.experimental import pallas as pl
from jax.experimental.pallas import tpu as pltpu
from jax.sharding import Mesh, PartitionSpec as P

STEP = 0.06
QUAD = ((0.0, 0.0, 0.0), (5.0 / 24.0, 1.0 / 3.0, -1.0 / 24.0), (1.0 / 6.0, 2.0 / 3.0, 1.0 / 6.0))
ROWSUM = tuple(sum(row) for row in QUAD)
START = tuple(STEP * (row[1] * QUAD[1][0] + row[2] * QUAD[2][0]) for row in QUAD)
SECTIONS = 8
BLOCK = 8
CHIPS = BLOCK // 2
F32 = jnp.float32

COEF, NEAR1, NEAR2, BEGIN, INITIAL, EDGE = 10, 11, 12, 13, 14, 15
ITEMS = (
    ((0, 8), (1, 7), (COEF, 7), (2, 6), (3, 5), (4, 4), (5, 3), (6, 2), (BEGIN, 2), (INITIAL, 2), (7, 1),
     (NEAR1, 1))
    + tuple((EDGE + i, 1) for i in range(4)),
    ((0, 8), (1, 7), (2, 6), (3, 5), (4, 4), (5, 3), (6, 2), (NEAR1, 1), (NEAR2, 1)),
)
ROWS = ({NEAR1: 16, COEF: 32, BEGIN: 48, INITIAL: 64, **{EDGE + i: 80 + 16 * i for i in range(4)}}, {NEAR1: 16, NEAR2: 32})


def count(items, distance):
    return sum(1 for _, reach in items if reach >= distance)


def shares(core, ahead):
    if ahead == 0:
        return (0, 1), (2 - core, BLOCK - 1)
    if ahead > 0:
        return (0, 2 * ahead - core), (2, BLOCK - 1 - 2 * ahead + core)
    return (0, -2 * ahead + core - 1), (1, BLOCK + 2 * ahead - core)


def slots(items):
    return max(sum(count(items, least) for _, least in shares(core, a)) for core in (0, 1) for a in range(-3, 4))


def turn(x, by, axis):
    return pltpu.roll(x, by % x.shape[axis], axis)


def around(x):
    return turn(x, 1, 0) + turn(x, -1, 0) + turn(x, 1, 1) + turn(x, -1, 1)


def cubic(u):
    return u - u * u * u


def dot(a, b):
    return jnp.dot(a, b, precision=lax.Precision.HIGHEST, preferred_element_type=F32)


def pair_lanes():
    z = lax.broadcasted_iota(jnp.int32, (128, 128), 0)
    c = lax.broadcasted_iota(jnp.int32, (128, 128), 1)
    return jnp.where((z >> 1) == (c & 63), 1.0, 0.0).astype(F32)


def spread_lanes():
    c = lax.broadcasted_iota(jnp.int32, (128, 128), 0)
    z = lax.broadcasted_iota(jnp.int32, (128, 128), 1)
    return jnp.where((z >> 1) == c, 1.0, 0.0).astype(F32)


def squash(planes, scratch):
    for i, plane in enumerate(planes):
        scratch[64 * i : 64 * i + 64, :] = plane
    both = scratch[pl.ds(0, 32 * len(planes), 2), :] + scratch[pl.ds(1, 32 * len(planes), 2), :]
    sums = dot(both, pair_lanes())
    return [sums[32 * i : 32 * i + 32] for i in range(len(planes))]


def spread(planes, scratch):
    wide = dot(jnp.concatenate(planes, axis=0), spread_lanes())
    scratch[pl.ds(0, 32 * len(planes), 2), :] = wide
    scratch[pl.ds(1, 32 * len(planes), 2), :] = wide
    return [scratch[64 * i : 64 * i + 64, :] for i in range(len(planes))]


def left(shape):
    return lax.broadcasted_iota(jnp.int32, shape, 1) < 64


def pack(x):
    return jnp.where(left((16, 128)), x[:16], x[16:])


def unpack(t):
    other = turn(t, 64, 1)
    here = left((16, 128))
    return jnp.concatenate([jnp.where(here, t, other), jnp.where(here, other, t)], axis=0)


def coarse_slope(below, centre, above, coef):
    return 0.25 * (around(centre) + below + above - 6.0 * centre) + coef * cubic(centre)


def mix(row, nodes):
    return QUAD[row][0] * nodes[0] + QUAD[row][1] * nodes[1] + QUAD[row][2] * nodes[2]


def packets(spot, up, down, inners, outers):
    def put(to_inner, to_outer):
        for parts, outs in ((to_inner, inners), (to_outer, outers)):
            whole = jnp.concatenate(parts, axis=0)
            half = whole.shape[0] // 2
            outs[0][...] = whole[:half]
            outs[1][...] = whole[half:]

    @pl.when(spot[2] == 0)
    def _():
        put(up, down)

    @pl.when(spot[2] != 0)
    def _():
        put(down, up)


def sides(spot, inners, outers):
    a = jnp.concatenate([part[...] for part in inners], axis=0)
    b = jnp.concatenate([part[...] for part in outers], axis=0)
    low = jnp.full(a.shape, spot[2], jnp.int32) == 0
    return jnp.where(low, b, a), jnp.where(low, a, b)


def first_kernel(
    spot, initial, coeff, guess, inner, inner_rest, outer, outer_rest, keep, initial_out, coeff_out, guess_out, scratch
):
    for out, given in ((initial_out, initial), (coeff_out, coeff), (guess_out, guess)):
        out[...] = given[...]
    u = [guess[0], guess[1]]
    c = [coeff[0], coeff[1]]
    both = u[0] + u[1]
    total = around(both) - 5.0 * both + c[0] * cubic(u[0]) + c[1] * cubic(u[1])
    own, value, coef, start = squash([total, both, c[0] + c[1], initial[0] + initial[1]], scratch)
    value, coef, start = 0.125 * value, 0.125 * coef, 0.125 * start
    small = [pack(value), pack(start)]
    packets(
        spot, [u[1]] + small + [u[0], c[1]], [u[0]] + small + [u[1], c[0]], [inner, inner_rest], [outer, outer_rest]
    )
    keep[0] = own
    keep[1] = value
    keep[2] = coef
    keep[3] = start


def own_k(own, value0, value0_sides, coef):
    slope = coarse_slope(value0_sides[0], value0, value0_sides[1], coef)
    return [(STEP / 8.0) * own[m] - (STEP * QUAD[m + 1][0]) * slope for m in (0, 1)]


def complete_first(
    spot, inner, outer, kept, initial, earlier, received, owned, beside, beyond, mine, keep, begin_out, earlier_out, scratch
):
    below, above = sides(spot, [inner], [outer])
    begin = starting(spot, initial, received)
    own, value, coef, start = (kept[i] for i in range(4))
    low, high, value_begin = squash([below[0:64, :], above[0:64, :], begin[0] + begin[1]], scratch)
    value_low, value_high = unpack(below[64:80, :]), unpack(above[64:80, :])
    start_low, start_high = unpack(below[80:96, :]), unpack(above[80:96, :])
    start_slope = coarse_slope(start_low, start, start_high, coef)
    whole = own + low + high
    k = own_k([ROWSUM[1] * whole, ROWSUM[2] * whole], value, [value_low, value_high], coef)
    first = jnp.full((32, 128), spot[0], jnp.int32) == 0
    given = [pack(k[m - 1] + jnp.where(first, start + (STEP * QUAD[m][0]) * start_slope, 0.0)) for m in (2, 1)]
    given += [pack(coef), pack(0.125 * value_begin), pack(start)]
    mine[...] = given[0]
    odd = jnp.full((64, 128), spot[3], jnp.int32) == 1
    for i, part in enumerate(given):
        for out in (owned, beside, beyond):
            out[16 * i : 16 * i + 16, :] = part
    beside[80:144, :] = jnp.where(odd, begin[0], begin[1])
    beyond[80:144, :] = jnp.where(odd, begin[1], begin[0])
    for x in (0, 1):
        owned[80 + 64 * x : 144 + 64 * x, :] = begin[x]
        begin_out[x] = begin[x]
        earlier_out[x] = jnp.where(jnp.full((64, 128), spot[0], jnp.int32) == 1, initial[x], earlier[x])
    for i, part in enumerate([k[0], k[1], start, start_slope, start_low, start_high, value_low, value_high]):
        keep[i] = part


def plane(spot, rows, owned, beside, beyond, sections, side, item, up=False):
    odd = spot[3]
    if item < SECTIONS:
        if side == 0:
            return sections[item, 0:16, :]
        at = jnp.where(odd == 1, side, 3 - side)
        return sections[item, pl.ds(pl.multiple_of(16 * at, 16), 16), :]
    row = rows[item]
    if side == 0:
        row += 64 if item >= EDGE and up else 0
        return owned[row : row + 16, :]
    near, far = beside[row : row + 16, :], beyond[row : row + 16, :]
    picked = jnp.full((16, 128), odd, jnp.int32) == (1 if side == 1 else 0)
    return jnp.where(picked, near, far)


def pack_kernel(items, rows):
    total = slots(items)

    def body(spot, owned, beside, beyond, sections, out):
        chip, core = spot[1], spot[2]

        def fill(own_core, away):
            slot = 0
            up = away > 0 or (away == 0 and own_core == 0)
            for side, least in shares(own_core, away):
                for item, reach in items:
                    if reach >= least:
                        part = plane(spot, rows, owned, beside, beyond, sections, side, item, up)
                        out[chip + away, 16 * slot : 16 * slot + 16, :] = part
                        slot += 1

        for own_core in (0, 1):
            for away in range(1 - CHIPS, CHIPS):
                there = jnp.logical_and(chip + away >= 0, chip + away < CHIPS)

                @pl.when(jnp.logical_and(core == own_core, there))
                def _():
                    fill(own_core, away)

    return body, total


def sweep(spot, items, rows, owned, beside, beyond, sections, windows, swapped, coefs, started, line, history):
    core = spot[2]
    place = 2 * spot[1] + core
    rank = {item: i for i, (item, _) in enumerate(items)}
    reach_of = dict(items)

    def fetch(item, w, whole=False):
        if w in (0, -BLOCK, BLOCK):
            side = {0: 0, -BLOCK: 1, BLOCK: 2}[w]
            return unpack(plane(spot, rows, owned, beside, beyond, sections, side, item))
        at = place + w
        if w > 0:
            outside, least = at >= BLOCK, [max(1, BLOCK - w - i) for i in (0, 1)]
        else:
            outside, least = at < 0, [max(1, BLOCK - 1 + w + i) for i in (0, 1)]
        before = jnp.where(core == 0, count(items, least[0]), count(items, least[1]))
        slot = rank[item] + jnp.where(outside, before, 0)
        source = windows if w % 2 == 0 else swapped
        found = source[(at & (BLOCK - 1)) >> 1, pl.ds(pl.multiple_of(16 * slot, 16), 16), :]
        return found if whole else unpack(found)

    if COEF in rank:
        for w in range(-7, 8):
            coefs[w + 7] = fetch(COEF, w)
    outermost = [fetch(INITIAL, w) if INITIAL in rank else jnp.zeros((32, 128), F32) for w in (-2, 2)]
    history[0] = outermost[0]
    history[1] = started[4]
    history[2] = started[2]
    history[3] = started[5]
    history[4] = outermost[1]
    for w in range(-8, 9):
        value = fetch(0, w)
        line[0, w + 8] = value
        if abs(w) <= 2:
            history[5 + w + 2] = value
    for k in range(1, SECTIONS):
        if k not in rank:
            continue
        old, new = (k - 1) % 2, k % 2
        for w in range(-reach_of[k], reach_of[k] + 1):
            centre = line[old, w + 8]
            slope = coarse_slope(line[old, w + 7], centre, line[old, w + 9], coefs[w + 7])
            value = centre + (STEP * QUAD[2][0]) * slope + fetch(k, w)
            line[new, w + 8] = value
            if abs(w) <= 2:
                history[5 * (k + 1) + w + 2] = value
    return fetch


def correct(spot, fetch, coefs, started, history, kept, values, nodes, below, above, coeff, begin, scratch):
    section = spot[0]
    s = [history[5 * section + i] for i in range(5)]
    slope = [coarse_slope(s[i], s[i + 1], s[i + 2], coefs[6 + i]) for i in range(3)]
    later = jnp.full((32, 128), section, jnp.int32) > 0
    edges = []
    for w, i in ((-1, 0), (1, 2)):
        for m, near in ((1, NEAR1), (2, NEAR2)):
            edges.append(fetch(near, w) + jnp.where(later, ROWSUM[m] * s[i + 1] + START[m] * slope[i], 0.0))
    coarse = [s[2]] + [s[2] + (STEP * QUAD[m][0]) * slope[1] + kept[m - 1] for m in (1, 2)]
    wide = spread([coarse[j] - values[j] for j in range(3)] + edges, scratch)
    fixed = [[nodes[j][x] + wide[j] for x in (0, 1)] for j in range(3)]
    rates = [[cubic(fixed[j][x]) for x in (0, 1)] for j in range(3)]
    fresh = []
    for m in (1, 2):
        sums = [mix(m, [fixed[j][x] for j in range(3)]) for x in (0, 1)]
        ends = [below[m - 1] + wide[2 + m], above[m - 1] + wide[4 + m]]
        fresh.append([])
        for x in (0, 1):
            change = around(sums[x]) - 6.0 * sums[x] + sums[1 - x] + ends[x]
            change = change + coeff[x] * mix(m, [rates[j][x] for j in range(3)])
            fresh[-1].append(begin[x] + STEP * change)
    return coarse[2], fresh


def starting(spot, initial, received):
    first = jnp.full((64, 128), spot[0], jnp.int32) == 0
    return [jnp.where(first, initial[x], received[x]) for x in (0, 1)]


def previous_end(section, fetch, coefs, history, starts, coeff, initial, earlier, scratch):
    before = jnp.maximum(section - 1, 0)
    s = [history[5 * before + i] for i in range(5)]
    value = [fetch(BEGIN, w) for w in range(-2, 3)]
    shift = []
    for i in range(3):
        two = history[5 * section + 1 + i]
        slope = coarse_slope(s[i], s[i + 1], s[i + 2], coefs[6 + i])
        slope = slope - coarse_slope(value[i], value[i + 1], value[i + 2], coefs[6 + i])
        one = 0.5 * (s[i + 1] + two) + (STEP * (QUAD[1][0] - 0.5 * QUAD[2][0])) * slope
        shift.append([s[i + 1] - value[i + 1], one - value[i + 1], two - value[i + 1]])
    wide = spread([mix(2, shift[0])] + shift[1] + [mix(2, shift[2])], scratch)
    fixed = [[starts[x] + wide[1 + j] for j in range(3)] for x in (1, 2)]
    sums = [ROWSUM[2] * starts[0] + wide[0], mix(2, fixed[0]), mix(2, fixed[1]), ROWSUM[2] * starts[3] + wide[4]]
    first = jnp.full((64, 128), section, jnp.int32) == 0
    out = []
    for x in (0, 1):
        change = around(sums[x + 1]) - 6.0 * sums[x + 1] + sums[x] + sums[x + 2]
        change = change + coeff[x] * mix(2, [cubic(part) for part in fixed[x]])
        out.append(jnp.where(first, initial[x], earlier[x] + STEP * change))
    return out


def finish_first(
    spot, owned, beside, beyond, sections, windows, swapped, started, kept, inner, inner_rest, outer, outer_rest,
    initial, coeff, guess, begin, earlier, middle_out, end_out, ends, begin_out, keep, owned_out, mine, coefs, line, history, scratch,
):
    fetch = sweep(
        spot, ITEMS[0], ROWS[0], owned, beside, beyond, sections, windows, swapped, coefs, started, line, history
    )
    below, above = sides(spot, [inner, inner_rest], [outer, outer_rest])
    section = spot[0]
    later = jnp.full((32, 128), section, jnp.int32) > 0
    s = [history[5 * section + i] for i in range(5)]
    slope = [coarse_slope(s[i], s[i + 1], s[i + 2], coefs[6 + i]) for i in range(3)]
    step = [s[i + 1] + (STEP * QUAD[1][0]) * slope[i] for i in range(3)]
    value = [started[6], kept[1], started[7]]
    coarse = []
    for i in range(3):
        if i == 1:
            one, two = step[1] + started[0], s[2] + (STEP * QUAD[2][0]) * slope[1] + started[1]
        else:
            one = fetch(NEAR1, i - 1) + jnp.where(later, step[i], 0.0)
            two = history[5 * section + 6 + i]
        coarse += [s[i + 1] - value[i], one - value[i], two - value[i]]
    wide = spread(coarse, scratch)
    u = [below[96:160, :], below[0:64, :], guess[0], guess[1], above[0:64, :], above[96:160, :]]
    c = [None, below[160:224, :], coeff[0], coeff[1], above[160:224, :], None]
    b = [None] + [None] * 4 + [None]
    b[2], b[3] = begin[0], begin[1]
    for x, w in ((1, -1), (4, 1)):
        b[x] = jnp.concatenate([fetch(EDGE + i, w, whole=True) for i in range(4)], axis=0)
    begin_next = previous_end(section, fetch, coefs, history, b[1:5], coeff, initial, earlier, scratch)
    for x in (0, 1):
        begin_out[x] = begin_next[x]
    fixed = [[u[x] + wide[3 * (x // 2) + j] for j in range(3)] for x in range(6)]
    nodes = [None] + [[b[x]] for x in range(1, 5)] + [None]
    rates = [None] + [[cubic(fixed[x][j]) for j in range(3)] for x in range(1, 5)] + [None]
    for m in (1, 2):
        sums = [mix(m, fixed[x]) for x in range(6)]
        for x in range(1, 5):
            change = around(sums[x]) - 6.0 * sums[x] + sums[x - 1] + sums[x + 1] + c[x] * mix(m, rates[x])
            nodes[x].append(b[x] + STEP * change)
    for x in (0, 1):
        middle_out[x] = nodes[x + 2][1]
        end_out[x] = nodes[x + 2][2]
    rates = [[cubic(nodes[x][j]) for j in range(3)] for x in (2, 3)]
    planes = []
    for m in (1, 2):
        sums = [mix(m, nodes[x]) for x in range(1, 5)]
        ends[m - 1] = sums[0]
        ends[m + 1] = sums[3]
        both = sums[1] + sums[2]
        planes.append(
            around(both) - 5.0 * both + sums[0] + sums[3] + c[2] * mix(m, rates[0]) + c[3] * mix(m, rates[1])
        )
    for j in range(3):
        planes.append(nodes[2][j] + nodes[3][j])
    small = squash(planes, scratch)
    values = [0.125 * small[2 + j] for j in range(3)]
    k = own_k(small[:2], values[0], [fetch(BEGIN, -1), fetch(BEGIN, 1)], kept[2])
    first = jnp.logical_not(later)
    ours = pack(k[1] + jnp.where(first, started[2] + (STEP * QUAD[2][0]) * started[3], 0.0))
    owned_out[0:16, :] = ours
    mine[...] = ours
    for m in (1, 2):
        near = QUAD[m][1] * k[0] + QUAD[m][2] * k[1] - mix(m, values)
        near = near + jnp.where(first, ROWSUM[m] * started[2] + START[m] * started[3], 0.0)
        owned_out[16 * m : 16 * m + 16, :] = pack(near)
    for i, part in enumerate(values + k):
        keep[i] = part


def finish_second(
    spot, owned, beside, beyond, sections, windows, swapped, started, kept, ends, coeff, begin_in, middle_in, end_in,
    begin, coefs, fresh_out, coarse_out, line, history, scratch,
):
    fetch = sweep(
        spot, ITEMS[1], ROWS[1], owned, beside, beyond, sections, windows, swapped, coefs, started, line, history
    )
    nodes = [[part[0], part[1]] for part in (begin_in, middle_in, end_in)]
    end, fresh = correct(
        spot, fetch, coefs, started, history, (kept[3], kept[4]), [kept[0], kept[1], kept[2]], nodes,
        [ends[0], ends[1]], [ends[2], ends[3]], [coeff[0], coeff[1]], [begin[0], begin[1]], scratch,
    )
    for m in (0, 1):
        for x in (0, 1):
            fresh_out[m, x] = fresh[m][x]
    coarse_out[...] = end[:, :64]


def run(body, args, outs, scratch=(), name=None, first=False, last=False):
    def placed(*refs):
        spot = [lax.axis_index(a) for a in ("tm", "chip", "core", "block")]
        body(spot[:3] + [spot[3] & 1], *refs)

    return pl.pallas_call(
        placed,
        out_shape=[jax.ShapeDtypeStruct(shape, F32) if last else pltpu.VMEM(shape, F32) for shape in outs],
        in_specs=[pl.BlockSpec(memory_space=pltpu.VMEM)] * len(args),
        out_specs=[pl.BlockSpec(memory_space=pltpu.VMEM)] * len(outs),
        scratch_shapes=[pltpu.VMEM(shape, F32) for shape in scratch],
        compiler_params=None if first else pltpu.CompilerParams(vmem_limit_bytes=16 << 20),
        name=name,
    )(*(a if first else pltpu.with_memory_space_constraint(a, pltpu.VMEM) for a in args))


class Links:
    call = staticmethod(run)

    @staticmethod
    def swap_block(x, row):
        n = lax.axis_size("block")
        pairs = [(i, i ^ 1 if row else (i + 2 * (i % 2) - 1) % n) for i in range(n)]
        return lax.ppermute(x, "block", pairs)

    @staticmethod
    def swap_inner(x):
        return lax.ppermute(x, "core", [(0, 1), (1, 0)])

    @staticmethod
    def swap_outer(x):
        n = lax.axis_size("block") * BLOCK
        return lax.ppermute(x, ("block", "chip", "core"), [(i, (i + 2 * (i % 2) - 1) % n) for i in range(n)])

    @staticmethod
    def onward(x, by):
        n = lax.axis_size("tm")
        return lax.ppermute(x, "tm", [(i, i + by) for i in range(n - by)])

    @staticmethod
    def sections(x):
        return lax.all_to_all(jnp.broadcast_to(x, (SECTIONS,) + x.shape), "tm", 0, 0)

    @staticmethod
    def block(x):
        return lax.all_to_all(x, "chip", 0, 0)

    @staticmethod
    def together(*values):
        return lax.optimization_barrier(values)

    @staticmethod
    def stack(*planes):
        return jnp.concatenate([p[:16] for p in planes], axis=0)


def iterate(links, initial, coeff, guess):
    coarse, slab = (32, 128), (2, 64, 128)
    work = [(2, 17) + coarse, (45,) + coarse]

    def windows(owned, beside, beyond, mine, iteration):
        sections = links.sections(links.stack(mine, beside, beyond))
        body, total = pack_kernel(ITEMS[iteration], ROWS[iteration])
        (parcels,) = links.call(
            body, (owned, beside, beyond, sections), [(CHIPS, 16 * total, 128)], name="hand_out"
        )
        parcels = links.block(parcels)
        return owned, beside, beyond, sections, parcels, links.swap_inner(parcels)

    sent = guess
    inner, inner_rest, outer, outer_rest, kept, initial, coeff, guess = links.call(
        first_kernel, (initial, coeff, guess),
        [(112, 128)] * 4 + [(4,) + coarse, slab, slab, slab], [(256, 128)], name="first", first=True,
    )
    earlier, received, outer, outer_rest, inner, inner_rest = links.together(
        links.onward(sent, 2), links.onward(sent, 1), links.swap_outer(outer), links.swap_outer(outer_rest),
        links.swap_inner(inner), links.swap_inner(inner_rest),
    )
    owned, beside, beyond, mine, started, begin, earlier = links.call(
        complete_first, (inner, outer, kept, initial, earlier, received),
        [(208, 128), (144, 128), (144, 128), (16, 128), (8,) + coarse, slab, slab], [(192, 128)], name="complete_first",
    )
    beside, beyond = links.swap_block(beside, True), links.swap_block(beyond, False)
    middle, end, ends, begin_next, kept, owned, mine, coefs = links.call(
        finish_first,
        (*windows(owned, beside, beyond, mine, 0), started, kept, inner, inner_rest, outer, outer_rest, initial,
         coeff, guess, begin, earlier),
        [slab, slab, (4, 64, 128), slab, (5,) + coarse, (48, 128), (16, 128), (15,) + coarse],
        work + [(576, 128)],
        name="finish_first",
    )
    beyond, beside = links.together(links.swap_block(owned, False), links.swap_block(owned, True))
    fine, coarse_end = links.call(
        finish_second,
        (*windows(owned, beside, beyond, mine, 1), started, kept, ends, coeff, begin, middle, end, begin_next, coefs),
        [(2, 2, 64, 128), (32, 64)],
        work + [(448, 128)],
        name="finish_second",
        last=True,
    )
    return fine, coarse_end


def on_device(initial, coeff, guess):
    fine, coarse_end = iterate(Links, initial, coeff, guess[0])
    return fine[None], coarse_end[None, None]


def solution(mesh):
    split = Mesh(
        mesh.devices.reshape(mesh.shape["tm"], mesh.shape["space"] // BLOCK, CHIPS, 2), ("tm", "block", "chip", "core")
    )
    space = ("block", "chip", "core")
    return jax.shard_map(
        on_device,
        mesh=split,
        in_specs=(P(space, None, None), P(space, None, None), P("tm", space, None, None)),
        out_specs=(P("tm", None, space, None, None), P("tm", space, None, None)),
        check_vma=False,
    )
```

```python
import jax
import jax.numpy as jnp
from jax import lax
from jax.experimental import pallas as pl
from jax.experimental.pallas import tpu as pltpu
from jax.sharding import Mesh, PartitionSpec as P

STEP = 0.06
QUAD = ((0.0, 0.0, 0.0), (5.0 / 24.0, 1.0 / 3.0, -1.0 / 24.0), (1.0 / 6.0, 2.0 / 3.0, 1.0 / 6.0))
ROWSUM = tuple(sum(row) for row in QUAD)
START = tuple(STEP * (row[1] * QUAD[1][0] + row[2] * QUAD[2][0]) for row in QUAD)
SECTIONS = 8
BLOCK = 8
CHIPS = BLOCK // 2
F32 = jnp.float32

COEF, NEAR1, NEAR2, BEGIN, INITIAL, EDGE = 10, 11, 12, 13, 14, 15
ITEMS = (
    ((0, 8), (1, 7), (COEF, 7), (2, 6), (3, 5), (4, 4), (5, 3), (6, 2), (BEGIN, 2), (INITIAL, 2), (7, 1),
     (NEAR1, 1))
    + tuple((EDGE + i, 1) for i in range(4)),
    ((0, 8), (1, 7), (2, 6), (3, 5), (4, 4), (5, 3), (6, 2), (NEAR1, 1), (NEAR2, 1)),
)
ROWS = ({NEAR1: 16, COEF: 32, BEGIN: 48, INITIAL: 64, **{EDGE + i: 80 + 16 * i for i in range(4)}}, {NEAR1: 16, NEAR2: 32})


def count(items, distance):
    return sum(1 for _, reach in items if reach >= distance)


def shares(core, ahead):
    if ahead == 0:
        return (0, 1), (2 - core, BLOCK - 1)
    if ahead > 0:
        return (0, 2 * ahead - core), (2, BLOCK - 1 - 2 * ahead + core)
    return (0, -2 * ahead + core - 1), (1, BLOCK + 2 * ahead - core)


def slots(items):
    return max(sum(count(items, least) for _, least in shares(core, a)) for core in (0, 1) for a in range(-3, 4))


def turn(x, by, axis):
    return pltpu.roll(x, by % x.shape[axis], axis)


def around(x):
    return turn(x, 1, 0) + turn(x, -1, 0) + turn(x, 1, 1) + turn(x, -1, 1)


def cubic(u):
    return u - u * u * u


def dot(a, b):
    b = b.astype(jnp.bfloat16)
    total, rest = None, a
    for _ in range(3):
        part = rest.astype(jnp.bfloat16)
        rest = rest - part.astype(F32)
        product = jnp.dot(part, b, preferred_element_type=F32)
        total = product if total is None else total + product
    return total


def pair_lanes():
    z = lax.broadcasted_iota(jnp.int32, (128, 128), 0)
    c = lax.broadcasted_iota(jnp.int32, (128, 128), 1)
    return jnp.where((z >> 1) == (c & 63), 1.0, 0.0).astype(F32)


def spread_lanes():
    c = lax.broadcasted_iota(jnp.int32, (128, 128), 0)
    z = lax.broadcasted_iota(jnp.int32, (128, 128), 1)
    return jnp.where((z >> 1) == c, 1.0, 0.0).astype(F32)


def squash(planes, scratch):
    for i, plane in enumerate(planes):
        scratch[64 * i : 64 * i + 64, :] = plane
    both = scratch[pl.ds(0, 32 * len(planes), 2), :] + scratch[pl.ds(1, 32 * len(planes), 2), :]
    sums = dot(both, pair_lanes())
    return [sums[32 * i : 32 * i + 32] for i in range(len(planes))]


def spread(planes, scratch):
    wide = dot(jnp.concatenate(planes, axis=0), spread_lanes())
    scratch[pl.ds(0, 32 * len(planes), 2), :] = wide
    scratch[pl.ds(1, 32 * len(planes), 2), :] = wide
    return [scratch[64 * i : 64 * i + 64, :] for i in range(len(planes))]


def left(shape):
    return lax.broadcasted_iota(jnp.int32, shape, 1) < 64


def pack(x):
    return jnp.where(left((16, 128)), x[:16], x[16:])


def unpack(t):
    other = turn(t, 64, 1)
    here = left((16, 128))
    return jnp.concatenate([jnp.where(here, t, other), jnp.where(here, other, t)], axis=0)


def coarse_slope(below, centre, above, coef):
    return 0.25 * (around(centre) + below + above - 6.0 * centre) + coef * cubic(centre)


def mix(row, nodes):
    return QUAD[row][0] * nodes[0] + QUAD[row][1] * nodes[1] + QUAD[row][2] * nodes[2]


def packets(spot, up, down, inners, outers):
    def put(to_inner, to_outer):
        for parts, outs in ((to_inner, inners), (to_outer, outers)):
            whole = jnp.concatenate(parts, axis=0)
            half = whole.shape[0] // 2
            outs[0][...] = whole[:half]
            outs[1][...] = whole[half:]

    @pl.when(spot[2] == 0)
    def _():
        put(up, down)

    @pl.when(spot[2] != 0)
    def _():
        put(down, up)


def sides(spot, inner, inner_rest, outer, outer_rest):
    a = jnp.concatenate([inner[...], inner_rest[...]], axis=0)
    b = jnp.concatenate([outer[...], outer_rest[...]], axis=0)
    low = jnp.full(a.shape, spot[2], jnp.int32) == 0
    return jnp.where(low, b, a), jnp.where(low, a, b)


def first_kernel(
    spot, initial, coeff, guess, inner, inner_rest, outer, outer_rest, keep, initial_out, coeff_out, guess_out, scratch
):
    for out, given in ((initial_out, initial), (coeff_out, coeff), (guess_out, guess)):
        out[...] = given[...]
    u = [guess[0], guess[1]]
    c = [coeff[0], coeff[1]]
    both = u[0] + u[1]
    total = around(both) - 5.0 * both + c[0] * cubic(u[0]) + c[1] * cubic(u[1])
    own, value, coef, start = squash([total, both, c[0] + c[1], initial[0] + initial[1]], scratch)
    value, coef, start = 0.125 * value, 0.125 * coef, 0.125 * start
    packets(spot, u + [c[1], pack(start)], u + [c[0], pack(start)], [inner, inner_rest], [outer, outer_rest])
    keep[0] = own
    keep[1] = value
    keep[2] = coef
    keep[3] = start


def own_k(own, value0, value0_sides, coef):
    slope = coarse_slope(value0_sides[0], value0, value0_sides[1], coef)
    return [(STEP / 8.0) * own[m] - (STEP * QUAD[m + 1][0]) * slope for m in (0, 1)]


def complete_first(
    spot, inner, inner_rest, outer, outer_rest, kept, initial, received, owned, beside, beyond, mine, keep, begin_out,
    scratch,
):
    below, above = sides(spot, inner, inner_rest, outer, outer_rest)
    begin = starting(spot, initial, received)
    own, value, coef, start = (kept[i] for i in range(4))
    low, high, value_low, value_high, value_begin = squash(
        [below[64:128, :], above[0:64, :], below[0:64, :] + below[64:128, :], above[0:64, :] + above[64:128, :],
         begin[0] + begin[1]],
        scratch,
    )
    value_low, value_high = 0.125 * value_low, 0.125 * value_high
    start_low, start_high = unpack(below[192:208, :]), unpack(above[192:208, :])
    start_slope = coarse_slope(start_low, start, start_high, coef)
    whole = own + low + high
    k = own_k([ROWSUM[1] * whole, ROWSUM[2] * whole], value, [value_low, value_high], coef)
    first = jnp.full((32, 128), spot[0], jnp.int32) == 0
    given = [pack(k[m - 1] + jnp.where(first, start + (STEP * QUAD[m][0]) * start_slope, 0.0)) for m in (2, 1)]
    given += [pack(coef), pack(0.125 * value_begin), pack(start)]
    mine[...] = given[0]
    odd = jnp.full((64, 128), spot[3], jnp.int32) == 1
    for i, part in enumerate(given):
        for out in (owned, beside, beyond):
            out[16 * i : 16 * i + 16, :] = part
    beside[80:144, :] = jnp.where(odd, begin[0], begin[1])
    beyond[80:144, :] = jnp.where(odd, begin[1], begin[0])
    for x in (0, 1):
        owned[80 + 64 * x : 144 + 64 * x, :] = begin[x]
        begin_out[x] = begin[x]
    for i, part in enumerate([k[0], k[1], start, start_slope, start_low, start_high, value_low, value_high]):
        keep[i] = part


def plane(spot, rows, owned, beside, beyond, sections, side, item, up=False):
    odd = spot[3]
    if item < SECTIONS:
        if side == 0:
            return sections[item, 0:16, :]
        at = jnp.where(odd == 1, side, 3 - side)
        return sections[item, pl.ds(pl.multiple_of(16 * at, 16), 16), :]
    row = rows[item]
    if side == 0:
        row += 64 if item >= EDGE and up else 0
        return owned[row : row + 16, :]
    near, far = beside[row : row + 16, :], beyond[row : row + 16, :]
    picked = jnp.full((16, 128), odd, jnp.int32) == (1 if side == 1 else 0)
    return jnp.where(picked, near, far)


def pack_kernel(items, rows):
    total = slots(items)

    def body(spot, owned, beside, beyond, sections, out):
        chip, core = spot[1], spot[2]

        def fill(own_core, away):
            slot = 0
            up = away > 0 or (away == 0 and own_core == 0)
            for side, least in shares(own_core, away):
                for item, reach in items:
                    if reach >= least:
                        part = plane(spot, rows, owned, beside, beyond, sections, side, item, up)
                        out[chip + away, 16 * slot : 16 * slot + 16, :] = part
                        slot += 1

        for own_core in (0, 1):
            for away in range(1 - CHIPS, CHIPS):
                there = jnp.logical_and(chip + away >= 0, chip + away < CHIPS)

                @pl.when(jnp.logical_and(core == own_core, there))
                def _():
                    fill(own_core, away)

    return body, total


def sweep(spot, items, rows, owned, beside, beyond, sections, windows, swapped, coefs, started, line, history):
    core = spot[2]
    place = 2 * spot[1] + core
    rank = {item: i for i, (item, _) in enumerate(items)}
    reach_of = dict(items)

    def fetch(item, w, whole=False):
        if w in (0, -BLOCK, BLOCK):
            side = {0: 0, -BLOCK: 1, BLOCK: 2}[w]
            return unpack(plane(spot, rows, owned, beside, beyond, sections, side, item))
        at = place + w
        if w > 0:
            outside, least = at >= BLOCK, [max(1, BLOCK - w - i) for i in (0, 1)]
        else:
            outside, least = at < 0, [max(1, BLOCK - 1 + w + i) for i in (0, 1)]
        before = jnp.where(core == 0, count(items, least[0]), count(items, least[1]))
        slot = rank[item] + jnp.where(outside, before, 0)
        source = windows if w % 2 == 0 else swapped
        found = source[(at & (BLOCK - 1)) >> 1, pl.ds(pl.multiple_of(16 * slot, 16), 16), :]
        return found if whole else unpack(found)

    if COEF in rank:
        for w in range(-7, 8):
            coefs[w + 7] = fetch(COEF, w)
    outermost = [fetch(INITIAL, w) if INITIAL in rank else jnp.zeros((32, 128), F32) for w in (-2, 2)]
    history[0] = outermost[0]
    history[1] = started[4]
    history[2] = started[2]
    history[3] = started[5]
    history[4] = outermost[1]
    for w in range(-8, 9):
        value = fetch(0, w)
        line[0, w + 8] = value
        if abs(w) <= 2:
            history[5 + w + 2] = value
    for k in range(1, SECTIONS):
        if k not in rank:
            continue
        old, new = (k - 1) % 2, k % 2
        for w in range(-reach_of[k], reach_of[k] + 1):
            centre = line[old, w + 8]
            slope = coarse_slope(line[old, w + 7], centre, line[old, w + 9], coefs[w + 7])
            value = centre + (STEP * QUAD[2][0]) * slope + fetch(k, w)
            line[new, w + 8] = value
            if abs(w) <= 2:
                history[5 * (k + 1) + w + 2] = value
    return fetch


def correct(spot, fetch, coefs, started, history, kept, values, nodes, below, above, coeff, begin, scratch):
    section = spot[0]
    s = [history[5 * section + i] for i in range(5)]
    slope = [coarse_slope(s[i], s[i + 1], s[i + 2], coefs[6 + i]) for i in range(3)]
    later = jnp.full((32, 128), section, jnp.int32) > 0
    edges = []
    for w, i in ((-1, 0), (1, 2)):
        for m, near in ((1, NEAR1), (2, NEAR2)):
            edges.append(fetch(near, w) + jnp.where(later, ROWSUM[m] * s[i + 1] + START[m] * slope[i], 0.0))
    coarse = [s[2]] + [s[2] + (STEP * QUAD[m][0]) * slope[1] + kept[m - 1] for m in (1, 2)]
    wide = spread([coarse[j] - values[j] for j in range(3)] + edges, scratch)
    fixed = [[nodes[j][x] + wide[j] for x in (0, 1)] for j in range(3)]
    rates = [[cubic(fixed[j][x]) for x in (0, 1)] for j in range(3)]
    fresh = []
    for m in (1, 2):
        sums = [mix(m, [fixed[j][x] for j in range(3)]) for x in (0, 1)]
        ends = [below[m - 1] + wide[2 + m], above[m - 1] + wide[4 + m]]
        fresh.append([])
        for x in (0, 1):
            change = around(sums[x]) - 6.0 * sums[x] + sums[1 - x] + ends[x]
            change = change + coeff[x] * mix(m, [rates[j][x] for j in range(3)])
            fresh[-1].append(begin[x] + STEP * change)
    return coarse[2], fresh


def starting(spot, initial, received):
    first = jnp.full((64, 128), spot[0], jnp.int32) == 0
    return [jnp.where(first, initial[x], received[x]) for x in (0, 1)]


def previous_end(section, fetch, coefs, history, starts, coeff, initial, earlier, scratch):
    before = jnp.maximum(section - 1, 0)
    s = [history[5 * before + i] for i in range(5)]
    value = [fetch(BEGIN, w) for w in range(-2, 3)]
    shift = []
    for i in range(3):
        two = history[5 * section + 1 + i]
        slope = coarse_slope(s[i], s[i + 1], s[i + 2], coefs[6 + i])
        slope = slope - coarse_slope(value[i], value[i + 1], value[i + 2], coefs[6 + i])
        one = 0.5 * (s[i + 1] + two) + (STEP * (QUAD[1][0] - 0.5 * QUAD[2][0])) * slope
        shift.append([s[i + 1] - value[i + 1], one - value[i + 1], two - value[i + 1]])
    wide = spread([mix(2, shift[0])] + shift[1] + [mix(2, shift[2])], scratch)
    fixed = [[starts[x] + wide[1 + j] for j in range(3)] for x in (1, 2)]
    sums = [ROWSUM[2] * starts[0] + wide[0], mix(2, fixed[0]), mix(2, fixed[1]), ROWSUM[2] * starts[3] + wide[4]]
    number = jnp.full((64, 128), section, jnp.int32)
    out = []
    for x in (0, 1):
        change = around(sums[x + 1]) - 6.0 * sums[x + 1] + sums[x] + sums[x + 2]
        change = change + coeff[x] * mix(2, [cubic(part) for part in fixed[x]])
        end = jnp.where(number == 1, initial[x], earlier[x]) + STEP * change
        out.append(jnp.where(number == 0, initial[x], end))
    return out


def finish_first(
    spot, owned, beside, beyond, sections, windows, swapped, started, kept, inner, inner_rest, outer, outer_rest,
    initial, coeff, guess, begin, earlier, middle_out, end_out, ends, begin_out, keep, owned_out, mine, coefs, line, history, scratch,
):
    fetch = sweep(
        spot, ITEMS[0], ROWS[0], owned, beside, beyond, sections, windows, swapped, coefs, started, line, history
    )
    below, above = sides(spot, inner, inner_rest, outer, outer_rest)
    section = spot[0]
    later = jnp.full((32, 128), section, jnp.int32) > 0
    s = [history[5 * section + i] for i in range(5)]
    slope = [coarse_slope(s[i], s[i + 1], s[i + 2], coefs[6 + i]) for i in range(3)]
    step = [s[i + 1] + (STEP * QUAD[1][0]) * slope[i] for i in range(3)]
    value = [started[6], kept[1], started[7]]
    coarse = []
    for i in range(3):
        if i == 1:
            one, two = step[1] + started[0], s[2] + (STEP * QUAD[2][0]) * slope[1] + started[1]
        else:
            one = fetch(NEAR1, i - 1) + jnp.where(later, step[i], 0.0)
            two = history[5 * section + 6 + i]
        coarse += [s[i + 1] - value[i], one - value[i], two - value[i]]
    wide = spread(coarse, scratch)
    u = [below[0:64, :], below[64:128, :], guess[0], guess[1], above[0:64, :], above[64:128, :]]
    c = [None, below[128:192, :], coeff[0], coeff[1], above[128:192, :], None]
    b = [None] + [None] * 4 + [None]
    b[2], b[3] = begin[0], begin[1]
    for x, w in ((1, -1), (4, 1)):
        b[x] = jnp.concatenate([fetch(EDGE + i, w, whole=True) for i in range(4)], axis=0)
    begin_next = previous_end(section, fetch, coefs, history, b[1:5], coeff, initial, earlier, scratch)
    for x in (0, 1):
        begin_out[x] = begin_next[x]
    fixed = [[u[x] + wide[3 * (x // 2) + j] for j in range(3)] for x in range(6)]
    nodes = [None] + [[b[x]] for x in range(1, 5)] + [None]
    rates = [None] + [[cubic(fixed[x][j]) for j in range(3)] for x in range(1, 5)] + [None]
    for m in (1, 2):
        sums = [mix(m, fixed[x]) for x in range(6)]
        for x in range(1, 5):
            change = around(sums[x]) - 6.0 * sums[x] + sums[x - 1] + sums[x + 1] + c[x] * mix(m, rates[x])
            nodes[x].append(b[x] + STEP * change)
    for x in (0, 1):
        middle_out[x] = nodes[x + 2][1]
        end_out[x] = nodes[x + 2][2]
    rates = [[cubic(nodes[x][j]) for j in range(3)] for x in (2, 3)]
    planes = []
    for m in (1, 2):
        sums = [mix(m, nodes[x]) for x in range(1, 5)]
        ends[m - 1] = sums[0]
        ends[m + 1] = sums[3]
        both = sums[1] + sums[2]
        planes.append(
            around(both) - 5.0 * both + sums[0] + sums[3] + c[2] * mix(m, rates[0]) + c[3] * mix(m, rates[1])
        )
    for j in range(3):
        planes.append(nodes[2][j] + nodes[3][j])
    small = squash(planes, scratch)
    values = [0.125 * small[2 + j] for j in range(3)]
    k = own_k(small[:2], values[0], [fetch(BEGIN, -1), fetch(BEGIN, 1)], kept[2])
    first = jnp.logical_not(later)
    ours = pack(k[1] + jnp.where(first, started[2] + (STEP * QUAD[2][0]) * started[3], 0.0))
    owned_out[0:16, :] = ours
    mine[...] = ours
    for m in (1, 2):
        near = QUAD[m][1] * k[0] + QUAD[m][2] * k[1] - mix(m, values)
        near = near + jnp.where(first, ROWSUM[m] * started[2] + START[m] * started[3], 0.0)
        owned_out[16 * m : 16 * m + 16, :] = pack(near)
    for i, part in enumerate(values + k):
        keep[i] = part


def finish_second(
    spot, owned, beside, beyond, sections, windows, swapped, started, kept, ends, coeff, begin_in, middle_in, end_in,
    begin, coefs, fresh_out, coarse_out, line, history, scratch,
):
    fetch = sweep(
        spot, ITEMS[1], ROWS[1], owned, beside, beyond, sections, windows, swapped, coefs, started, line, history
    )
    nodes = [[part[0], part[1]] for part in (begin_in, middle_in, end_in)]
    end, fresh = correct(
        spot, fetch, coefs, started, history, (kept[3], kept[4]), [kept[0], kept[1], kept[2]], nodes,
        [ends[0], ends[1]], [ends[2], ends[3]], [coeff[0], coeff[1]], [begin[0], begin[1]], scratch,
    )
    for m in (0, 1):
        for x in (0, 1):
            fresh_out[m, x] = fresh[m][x]
    coarse_out[...] = end[:, :64]


def run(body, args, outs, scratch=(), name=None, first=False, last=False):
    def placed(*refs):
        spot = [lax.axis_index(a) for a in ("tm", "chip", "core", "block")]
        body(spot[:3] + [spot[3] & 1], *refs)

    return pl.pallas_call(
        placed,
        out_shape=[jax.ShapeDtypeStruct(shape, F32) if last else pltpu.VMEM(shape, F32) for shape in outs],
        in_specs=[pl.BlockSpec(memory_space=pltpu.VMEM)] * len(args),
        out_specs=[pl.BlockSpec(memory_space=pltpu.VMEM)] * len(outs),
        scratch_shapes=[pltpu.VMEM(shape, F32) for shape in scratch],
        compiler_params=None if first else pltpu.CompilerParams(vmem_limit_bytes=16 << 20),
        name=name,
    )(*(a if first else pltpu.with_memory_space_constraint(a, pltpu.VMEM) for a in args))


class Links:
    call = staticmethod(run)

    @staticmethod
    def swap_block(x, row):
        n = lax.axis_size("block")
        pairs = [(i, i ^ 1 if row else (i + 2 * (i % 2) - 1) % n) for i in range(n)]
        return lax.ppermute(x, "block", pairs)

    @staticmethod
    def swap_inner(x):
        return lax.ppermute(x, "core", [(0, 1), (1, 0)])

    @staticmethod
    def swap_outer(x):
        n = lax.axis_size("block") * BLOCK
        return lax.ppermute(x, ("block", "chip", "core"), [(i, (i + 2 * (i % 2) - 1) % n) for i in range(n)])

    @staticmethod
    def onward(x, by):
        n = lax.axis_size("tm")
        return lax.ppermute(x, "tm", [(i, i + by) for i in range(n - by)])

    @staticmethod
    def sections(x):
        return lax.all_to_all(jnp.broadcast_to(x, (SECTIONS,) + x.shape), "tm", 0, 0)

    @staticmethod
    def block(x):
        return lax.all_to_all(x, "chip", 0, 0)

    @staticmethod
    def together(*values):
        return lax.optimization_barrier(values)

    @staticmethod
    def stack(*planes):
        return jnp.concatenate([p[:16] for p in planes], axis=0)


def iterate(links, initial, coeff, guess):
    coarse, slab = (32, 128), (2, 64, 128)
    work = [(2, 17) + coarse, (45,) + coarse]

    def windows(owned, beside, beyond, mine, iteration):
        sections = links.sections(links.stack(mine, beside, beyond))
        body, total = pack_kernel(ITEMS[iteration], ROWS[iteration])
        (parcels,) = links.call(
            body, (owned, beside, beyond, sections), [(CHIPS, 16 * total, 128)], name="hand_out"
        )
        parcels = links.block(parcels)
        return owned, beside, beyond, sections, parcels, links.swap_inner(parcels)

    sent = guess
    inner, inner_rest, outer, outer_rest, kept, initial, coeff, guess = links.call(
        first_kernel, (initial, coeff, guess),
        [(104, 128)] * 4 + [(4,) + coarse, slab, slab, slab], [(256, 128)], name="first", first=True,
    )
    outer, outer_rest, inner, inner_rest, received = links.together(
        links.swap_outer(outer), links.swap_outer(outer_rest), links.swap_inner(inner), links.swap_inner(inner_rest),
        links.onward(sent, 1),
    )
    owned, beside, beyond, mine, started, begin = links.call(
        complete_first, (inner, inner_rest, outer, outer_rest, kept, initial, received),
        [(208, 128), (144, 128), (144, 128), (16, 128), (8,) + coarse, slab], [(320, 128)], name="complete_first",
    )
    beside, beyond, earlier = links.together(
        links.swap_block(beside, True), links.swap_block(beyond, False), links.onward(sent, 2)
    )
    middle, end, ends, begin_next, kept, owned, mine, coefs = links.call(
        finish_first,
        (*windows(owned, beside, beyond, mine, 0), started, kept, inner, inner_rest, outer, outer_rest, initial,
         coeff, guess, begin, earlier),
        [slab, slab, (4, 64, 128), slab, (5,) + coarse, (48, 128), (16, 128), (15,) + coarse],
        work + [(576, 128)],
        name="finish_first",
    )
    beyond, beside = links.together(links.swap_block(owned, False), links.swap_block(owned, True))
    fine, coarse_end = links.call(
        finish_second,
        (*windows(owned, beside, beyond, mine, 1), started, kept, ends, coeff, begin, middle, end, begin_next, coefs),
        [(2, 2, 64, 128), (32, 64)],
        work + [(448, 128)],
        name="finish_second",
        last=True,
    )
    return fine, coarse_end


def on_device(initial, coeff, guess):
    fine, coarse_end = iterate(Links, initial, coeff, guess[0])
    return fine[None], coarse_end[None, None]


def solution(mesh):
    split = Mesh(
        mesh.devices.reshape(mesh.shape["tm"], mesh.shape["space"] // BLOCK, CHIPS, 2), ("tm", "block", "chip", "core")
    )
    space = ("block", "chip", "core")
    return jax.shard_map(
        on_device,
        mesh=split,
        in_specs=(P(space, None, None), P(space, None, None), P("tm", space, None, None)),
        out_specs=(P("tm", None, space, None, None), P("tm", space, None, None)),
        check_vma=False,
    )
```

```python
import jax
import jax.numpy as jnp
from jax import lax
from jax.experimental import pallas as pl
from jax.experimental.pallas import tpu as pltpu
from jax.sharding import Mesh, PartitionSpec as P

STEP = 0.06
QUAD = ((0.0, 0.0, 0.0), (5.0 / 24.0, 1.0 / 3.0, -1.0 / 24.0), (1.0 / 6.0, 2.0 / 3.0, 1.0 / 6.0))
ROWSUM = tuple(sum(row) for row in QUAD)
START = tuple(STEP * (row[1] * QUAD[1][0] + row[2] * QUAD[2][0]) for row in QUAD)
SECTIONS = 8
BLOCK = 8
CHIPS = BLOCK // 2
F32 = jnp.float32

COEF, NEAR1, NEAR2, BEGIN, INITIAL, EDGE = 10, 11, 12, 13, 14, 15
ITEMS = (
    ((0, 8), (1, 7), (COEF, 7), (2, 6), (3, 5), (4, 4), (5, 3), (6, 2), (BEGIN, 2), (INITIAL, 2), (7, 1),
     (NEAR1, 1))
    + tuple((EDGE + i, 1) for i in range(4)),
    ((0, 8), (1, 7), (2, 6), (3, 5), (4, 4), (5, 3), (6, 2), (NEAR1, 1), (NEAR2, 1)),
)
ROWS = ({NEAR1: 16, COEF: 32, BEGIN: 48, INITIAL: 64, **{EDGE + i: 80 + 16 * i for i in range(4)}}, {NEAR1: 16, NEAR2: 32})


def count(items, distance):
    return sum(1 for _, reach in items if reach >= distance)


def shares(core, ahead):
    if ahead == 0:
        return (0, 1), (2 - core, BLOCK - 1)
    if ahead > 0:
        return (0, 2 * ahead - core), (2, BLOCK - 1 - 2 * ahead + core)
    return (0, -2 * ahead + core - 1), (1, BLOCK + 2 * ahead - core)


def slots(items):
    return max(sum(count(items, least) for _, least in shares(core, a)) for core in (0, 1) for a in range(-3, 4))


def turn(x, by, axis):
    return pltpu.roll(x, by % x.shape[axis], axis)


def around(x):
    return turn(x, 1, 0) + turn(x, -1, 0) + turn(x, 1, 1) + turn(x, -1, 1)


def cubic(u):
    return u - u * u * u


def dot(a, b):
    b = b.astype(jnp.bfloat16)
    total, rest = None, a
    for _ in range(3):
        part = rest.astype(jnp.bfloat16)
        rest = rest - part.astype(F32)
        product = jnp.dot(part, b, preferred_element_type=F32)
        total = product if total is None else total + product
    return total


def pair_lanes():
    z = lax.broadcasted_iota(jnp.int32, (128, 128), 0)
    c = lax.broadcasted_iota(jnp.int32, (128, 128), 1)
    return jnp.where((z >> 1) == (c & 63), 1.0, 0.0).astype(F32)


def spread_lanes():
    c = lax.broadcasted_iota(jnp.int32, (128, 128), 0)
    z = lax.broadcasted_iota(jnp.int32, (128, 128), 1)
    return jnp.where((z >> 1) == c, 1.0, 0.0).astype(F32)


def squash(planes, scratch):
    for i, plane in enumerate(planes):
        scratch[64 * i : 64 * i + 64, :] = plane
    both = scratch[pl.ds(0, 32 * len(planes), 2), :] + scratch[pl.ds(1, 32 * len(planes), 2), :]
    sums = dot(both, pair_lanes())
    return [sums[32 * i : 32 * i + 32] for i in range(len(planes))]


def spread(planes, scratch):
    wide = dot(jnp.concatenate(planes, axis=0), spread_lanes())
    scratch[pl.ds(0, 32 * len(planes), 2), :] = wide
    scratch[pl.ds(1, 32 * len(planes), 2), :] = wide
    return [scratch[64 * i : 64 * i + 64, :] for i in range(len(planes))]


def left(shape):
    return lax.broadcasted_iota(jnp.int32, shape, 1) < 64


def pack(x):
    return jnp.where(left((16, 128)), x[:16], x[16:])


def unpack(t):
    other = turn(t, 64, 1)
    here = left((16, 128))
    return jnp.concatenate([jnp.where(here, t, other), jnp.where(here, other, t)], axis=0)


def coarse_slope(below, centre, above, coef):
    return 0.25 * (around(centre) + below + above - 6.0 * centre) + coef * cubic(centre)


def mix(row, nodes):
    return QUAD[row][0] * nodes[0] + QUAD[row][1] * nodes[1] + QUAD[row][2] * nodes[2]


def packets(spot, up, down, inners, outers):
    def put(to_inner, to_outer):
        for parts, outs in ((to_inner, inners), (to_outer, outers)):
            whole = jnp.concatenate(parts, axis=0)
            half = whole.shape[0] // 2
            outs[0][...] = whole[:half]
            outs[1][...] = whole[half:]

    @pl.when(spot[2] == 0)
    def _():
        put(up, down)

    @pl.when(spot[2] != 0)
    def _():
        put(down, up)


def sides(spot, inner, inner_rest, outer, outer_rest):
    a = jnp.concatenate([inner[...], inner_rest[...]], axis=0)
    b = jnp.concatenate([outer[...], outer_rest[...]], axis=0)
    low = jnp.full(a.shape, spot[2], jnp.int32) == 0
    return jnp.where(low, b, a), jnp.where(low, a, b)


def first_kernel(
    spot, initial, coeff, guess, inner, inner_rest, outer, outer_rest, keep, initial_out, coeff_out, guess_out, scratch
):
    for out, given in ((initial_out, initial), (coeff_out, coeff), (guess_out, guess)):
        out[...] = given[...]
    u = [guess[0], guess[1]]
    c = [coeff[0], coeff[1]]
    both = u[0] + u[1]
    total = around(both) - 5.0 * both + c[0] * cubic(u[0]) + c[1] * cubic(u[1])
    own, value, coef, start = squash([total, both, c[0] + c[1], initial[0] + initial[1]], scratch)
    value, coef, start = 0.125 * value, 0.125 * coef, 0.125 * start
    packets(spot, u + [c[1], pack(start)], u + [c[0], pack(start)], [inner, inner_rest], [outer, outer_rest])
    keep[0] = own
    keep[1] = value
    keep[2] = coef
    keep[3] = start


def own_k(own, value0, value0_sides, coef):
    slope = coarse_slope(value0_sides[0], value0, value0_sides[1], coef)
    return [(STEP / 8.0) * own[m] - (STEP * QUAD[m + 1][0]) * slope for m in (0, 1)]


def complete_first(
    spot, inner, inner_rest, outer, outer_rest, kept, initial, received, owned, beside, beyond, mine, keep, begin_out,
    scratch,
):
    below, above = sides(spot, inner, inner_rest, outer, outer_rest)
    begin = starting(spot, initial, received)
    own, value, coef, start = (kept[i] for i in range(4))
    low, high, value_low, value_high, value_begin = squash(
        [below[64:128, :], above[0:64, :], below[0:64, :] + below[64:128, :], above[0:64, :] + above[64:128, :],
         begin[0] + begin[1]],
        scratch,
    )
    value_low, value_high = 0.125 * value_low, 0.125 * value_high
    start_low, start_high = unpack(below[192:208, :]), unpack(above[192:208, :])
    start_slope = coarse_slope(start_low, start, start_high, coef)
    whole = own + low + high
    k = own_k([ROWSUM[1] * whole, ROWSUM[2] * whole], value, [value_low, value_high], coef)
    first = jnp.full((32, 128), spot[0], jnp.int32) == 0
    given = [pack(k[m - 1] + jnp.where(first, start + (STEP * QUAD[m][0]) * start_slope, 0.0)) for m in (2, 1)]
    given += [pack(coef), pack(0.125 * value_begin), pack(start)]
    mine[...] = given[0]
    odd = jnp.full((64, 128), spot[3], jnp.int32) == 1
    for i, part in enumerate(given):
        for out in (owned, beside, beyond):
            out[16 * i : 16 * i + 16, :] = part
    beside[80:144, :] = jnp.where(odd, begin[0], begin[1])
    beyond[80:144, :] = jnp.where(odd, begin[1], begin[0])
    for x in (0, 1):
        owned[80 + 64 * x : 144 + 64 * x, :] = begin[x]
        begin_out[x] = begin[x]
    for i, part in enumerate([k[0], k[1], start, start_slope, start_low, start_high, value_low, value_high]):
        keep[i] = part


def plane(spot, rows, owned, beside, beyond, sections, side, item, up=False):
    odd = spot[3]
    if item < SECTIONS:
        if side == 0:
            return sections[item, 0:16, :]
        at = jnp.where(odd == 1, side, 3 - side)
        return sections[item, pl.ds(pl.multiple_of(16 * at, 16), 16), :]
    row = rows[item]
    if side == 0:
        row += 64 if item >= EDGE and up else 0
        return owned[row : row + 16, :]
    near, far = beside[row : row + 16, :], beyond[row : row + 16, :]
    picked = jnp.full((16, 128), odd, jnp.int32) == (1 if side == 1 else 0)
    return jnp.where(picked, near, far)


def pack_kernel(items, rows):
    total = slots(items)

    def body(spot, owned, beside, beyond, sections, out):
        chip, core = spot[1], spot[2]

        def fill(own_core, away):
            slot = 0
            up = away > 0 or (away == 0 and own_core == 0)
            for side, least in shares(own_core, away):
                for item, reach in items:
                    if reach >= least:
                        part = plane(spot, rows, owned, beside, beyond, sections, side, item, up)
                        out[chip + away, 16 * slot : 16 * slot + 16, :] = part
                        slot += 1

        for own_core in (0, 1):
            for away in range(1 - CHIPS, CHIPS):
                there = jnp.logical_and(chip + away >= 0, chip + away < CHIPS)

                @pl.when(jnp.logical_and(core == own_core, there))
                def _():
                    fill(own_core, away)

    return body, total


def sweep(spot, items, rows, owned, beside, beyond, sections, windows, swapped, coefs, started, line, history):
    core = spot[2]
    place = 2 * spot[1] + core
    rank = {item: i for i, (item, _) in enumerate(items)}
    reach_of = dict(items)

    def fetch(item, w, whole=False):
        if w in (0, -BLOCK, BLOCK):
            side = {0: 0, -BLOCK: 1, BLOCK: 2}[w]
            return unpack(plane(spot, rows, owned, beside, beyond, sections, side, item))
        at = place + w
        if w > 0:
            outside, least = at >= BLOCK, [max(1, BLOCK - w - i) for i in (0, 1)]
        else:
            outside, least = at < 0, [max(1, BLOCK - 1 + w + i) for i in (0, 1)]
        before = jnp.where(core == 0, count(items, least[0]), count(items, least[1]))
        slot = rank[item] + jnp.where(outside, before, 0)
        source = windows if w % 2 == 0 else swapped
        found = source[(at & (BLOCK - 1)) >> 1, pl.ds(pl.multiple_of(16 * slot, 16), 16), :]
        return found if whole else unpack(found)

    if COEF in rank:
        for w in range(-7, 8):
            coefs[w + 7] = fetch(COEF, w)
    outermost = [fetch(INITIAL, w) if INITIAL in rank else jnp.zeros((32, 128), F32) for w in (-2, 2)]
    history[0] = outermost[0]
    history[1] = started[4]
    history[2] = started[2]
    history[3] = started[5]
    history[4] = outermost[1]
    for w in range(-8, 9):
        value = fetch(0, w)
        line[0, w + 8] = value
        if abs(w) <= 2:
            history[5 + w + 2] = value
    for k in range(1, SECTIONS):
        if k not in rank:
            continue
        old, new = (k - 1) % 2, k % 2
        for w in range(-reach_of[k], reach_of[k] + 1):
            centre = line[old, w + 8]
            slope = coarse_slope(line[old, w + 7], centre, line[old, w + 9], coefs[w + 7])
            value = centre + (STEP * QUAD[2][0]) * slope + fetch(k, w)
            line[new, w + 8] = value
            if abs(w) <= 2:
                history[5 * (k + 1) + w + 2] = value
    return fetch


def correct(spot, fetch, coefs, started, history, kept, values, nodes, below, above, coeff, begin, scratch):
    section = spot[0]
    s = [history[5 * section + i] for i in range(5)]
    slope = [coarse_slope(s[i], s[i + 1], s[i + 2], coefs[6 + i]) for i in range(3)]
    later = jnp.full((32, 128), section, jnp.int32) > 0
    edges = []
    for w, i in ((-1, 0), (1, 2)):
        for m, near in ((1, NEAR1), (2, NEAR2)):
            edges.append(fetch(near, w) + jnp.where(later, ROWSUM[m] * s[i + 1] + START[m] * slope[i], 0.0))
    coarse = [s[2]] + [s[2] + (STEP * QUAD[m][0]) * slope[1] + kept[m - 1] for m in (1, 2)]
    wide = spread([coarse[j] - values[j] for j in range(3)] + edges, scratch)
    fixed = [[nodes[j][x] + wide[j] for x in (0, 1)] for j in range(3)]
    rates = [[cubic(fixed[j][x]) for x in (0, 1)] for j in range(3)]
    fresh = []
    for m in (1, 2):
        sums = [mix(m, [fixed[j][x] for j in range(3)]) for x in (0, 1)]
        ends = [below[m - 1] + wide[2 + m], above[m - 1] + wide[4 + m]]
        fresh.append([])
        for x in (0, 1):
            change = around(sums[x]) - 6.0 * sums[x] + sums[1 - x] + ends[x]
            change = change + coeff[x] * mix(m, [rates[j][x] for j in range(3)])
            fresh[-1].append(begin[x] + STEP * change)
    return coarse[2], fresh


def starting(spot, initial, received):
    first = jnp.full((64, 128), spot[0], jnp.int32) == 0
    return [jnp.where(first, initial[x], received[x]) for x in (0, 1)]


def previous_end(section, fetch, coefs, history, starts, coeff, initial, earlier, scratch):
    before = jnp.maximum(section - 1, 0)
    s = [history[5 * before + i] for i in range(5)]
    value = [fetch(BEGIN, w) for w in range(-2, 3)]
    shift = []
    for i in range(3):
        two = history[5 * section + 1 + i]
        slope = coarse_slope(s[i], s[i + 1], s[i + 2], coefs[6 + i])
        slope = slope - coarse_slope(value[i], value[i + 1], value[i + 2], coefs[6 + i])
        one = 0.5 * (s[i + 1] + two) + (STEP * (QUAD[1][0] - 0.5 * QUAD[2][0])) * slope
        shift.append([s[i + 1] - value[i + 1], one - value[i + 1], two - value[i + 1]])
    wide = spread([mix(2, shift[0])] + shift[1] + [mix(2, shift[2])], scratch)
    fixed = [[starts[x] + wide[1 + j] for j in range(3)] for x in (1, 2)]
    sums = [ROWSUM[2] * starts[0] + wide[0], mix(2, fixed[0]), mix(2, fixed[1]), ROWSUM[2] * starts[3] + wide[4]]
    number = jnp.full((64, 128), section, jnp.int32)
    out = []
    for x in (0, 1):
        change = around(sums[x + 1]) - 6.0 * sums[x + 1] + sums[x] + sums[x + 2]
        change = change + coeff[x] * mix(2, [cubic(part) for part in fixed[x]])
        end = jnp.where(number == 1, initial[x], earlier[x]) + STEP * change
        out.append(jnp.where(number == 0, initial[x], end))
    return out


def finish_first(
    spot, owned, beside, beyond, sections, windows, swapped, started, kept, inner, inner_rest, outer, outer_rest,
    initial, coeff, guess, begin, earlier, middle_out, end_out, ends, begin_out, keep, owned_out, mine, coefs, line, history, scratch,
):
    fetch = sweep(
        spot, ITEMS[0], ROWS[0], owned, beside, beyond, sections, windows, swapped, coefs, started, line, history
    )
    below, above = sides(spot, inner, inner_rest, outer, outer_rest)
    section = spot[0]
    later = jnp.full((32, 128), section, jnp.int32) > 0
    s = [history[5 * section + i] for i in range(5)]
    slope = [coarse_slope(s[i], s[i + 1], s[i + 2], coefs[6 + i]) for i in range(3)]
    step = [s[i + 1] + (STEP * QUAD[1][0]) * slope[i] for i in range(3)]
    value = [started[6], kept[1], started[7]]
    coarse = []
    for i in range(3):
        if i == 1:
            one, two = step[1] + started[0], s[2] + (STEP * QUAD[2][0]) * slope[1] + started[1]
        else:
            one = fetch(NEAR1, i - 1) + jnp.where(later, step[i], 0.0)
            two = history[5 * section + 6 + i]
        coarse += [s[i + 1] - value[i], one - value[i], two - value[i]]
    wide = spread(coarse, scratch)
    u = [below[0:64, :], below[64:128, :], guess[0], guess[1], above[0:64, :], above[64:128, :]]
    c = [None, below[128:192, :], coeff[0], coeff[1], above[128:192, :], None]
    b = [None] + [None] * 4 + [None]
    b[2], b[3] = begin[0], begin[1]
    for x, w in ((1, -1), (4, 1)):
        b[x] = jnp.concatenate([fetch(EDGE + i, w, whole=True) for i in range(4)], axis=0)
    begin_next = previous_end(section, fetch, coefs, history, b[1:5], coeff, initial, earlier, scratch)
    for x in (0, 1):
        begin_out[x] = begin_next[x]
    fixed = [[u[x] + wide[3 * (x // 2) + j] for j in range(3)] for x in range(6)]
    nodes = [None] + [[b[x]] for x in range(1, 5)] + [None]
    rates = [None] + [[cubic(fixed[x][j]) for j in range(3)] for x in range(1, 5)] + [None]
    for m in (1, 2):
        sums = [mix(m, fixed[x]) for x in range(6)]
        for x in range(1, 5):
            change = around(sums[x]) - 6.0 * sums[x] + sums[x - 1] + sums[x + 1] + c[x] * mix(m, rates[x])
            nodes[x].append(b[x] + STEP * change)
    for x in (0, 1):
        middle_out[x] = nodes[x + 2][1]
        end_out[x] = nodes[x + 2][2]
    rates = [[cubic(nodes[x][j]) for j in range(3)] for x in (2, 3)]
    planes = []
    for m in (1, 2):
        sums = [mix(m, nodes[x]) for x in range(1, 5)]
        ends[m - 1] = sums[0]
        ends[m + 1] = sums[3]
        both = sums[1] + sums[2]
        planes.append(
            around(both) - 5.0 * both + sums[0] + sums[3] + c[2] * mix(m, rates[0]) + c[3] * mix(m, rates[1])
        )
    for j in range(3):
        planes.append(nodes[2][j] + nodes[3][j])
    small = squash(planes, scratch)
    values = [0.125 * small[2 + j] for j in range(3)]
    k = own_k(small[:2], values[0], [fetch(BEGIN, -1), fetch(BEGIN, 1)], kept[2])
    first = jnp.logical_not(later)
    ours = pack(k[1] + jnp.where(first, started[2] + (STEP * QUAD[2][0]) * started[3], 0.0))
    owned_out[0:16, :] = ours
    mine[...] = ours
    for m in (1, 2):
        near = QUAD[m][1] * k[0] + QUAD[m][2] * k[1] - mix(m, values)
        near = near + jnp.where(first, ROWSUM[m] * started[2] + START[m] * started[3], 0.0)
        owned_out[16 * m : 16 * m + 16, :] = pack(near)
    for i, part in enumerate(values + k):
        keep[i] = part


def finish_second(
    spot, owned, beside, beyond, sections, windows, swapped, started, kept, ends, coeff, begin_in, middle_in, end_in,
    begin, coefs, fresh_out, coarse_out, line, history, scratch,
):
    fetch = sweep(
        spot, ITEMS[1], ROWS[1], owned, beside, beyond, sections, windows, swapped, coefs, started, line, history
    )
    nodes = [[part[0], part[1]] for part in (begin_in, middle_in, end_in)]
    end, fresh = correct(
        spot, fetch, coefs, started, history, (kept[3], kept[4]), [kept[0], kept[1], kept[2]], nodes,
        [ends[0], ends[1]], [ends[2], ends[3]], [coeff[0], coeff[1]], [begin[0], begin[1]], scratch,
    )
    for m in (0, 1):
        for x in (0, 1):
            fresh_out[m, x] = fresh[m][x]
    coarse_out[...] = end[:, :64]


def run(body, args, outs, scratch=(), name=None, first=False, last=False):
    def placed(*refs):
        spot = [lax.axis_index(a) for a in ("tm", "chip", "core", "block")]
        body(spot[:3] + [spot[3] & 1], *refs)

    return pl.pallas_call(
        placed,
        out_shape=[jax.ShapeDtypeStruct(shape, F32) if last else pltpu.VMEM(shape, F32) for shape in outs],
        in_specs=[pl.BlockSpec(memory_space=pltpu.VMEM)] * len(args),
        out_specs=[pl.BlockSpec(memory_space=pltpu.VMEM)] * len(outs),
        scratch_shapes=[pltpu.VMEM(shape, F32) for shape in scratch],
        compiler_params=None if first else pltpu.CompilerParams(vmem_limit_bytes=16 << 20),
        name=name,
    )(*(a if first else pltpu.with_memory_space_constraint(a, pltpu.VMEM) for a in args))


class Links:
    call = staticmethod(run)

    @staticmethod
    def swap_block(x, row):
        n = lax.axis_size("block")
        pairs = [(i, i ^ 1 if row else (i + 2 * (i % 2) - 1) % n) for i in range(n)]
        return lax.ppermute(x, "block", pairs)

    @staticmethod
    def swap_inner(x):
        return lax.ppermute(x, "core", [(0, 1), (1, 0)])

    @staticmethod
    def swap_outer(x):
        n = lax.axis_size("block") * BLOCK
        return lax.ppermute(x, ("block", "chip", "core"), [(i, (i + 2 * (i % 2) - 1) % n) for i in range(n)])

    @staticmethod
    def onward(x, by):
        n = lax.axis_size("tm")
        return lax.ppermute(x, "tm", [(i, i + by) for i in range(n - by)])

    @staticmethod
    def sections(x):
        return lax.all_to_all(jnp.broadcast_to(x, (SECTIONS,) + x.shape), "tm", 0, 0)

    @staticmethod
    def block(x):
        return lax.all_to_all(x, "chip", 0, 0)

    @staticmethod
    def together(*values):
        return lax.optimization_barrier(values)

    @staticmethod
    def stack(*planes):
        return jnp.concatenate([p[:16] for p in planes], axis=0)


def iterate(links, initial, coeff, guess):
    coarse, slab = (32, 128), (2, 64, 128)
    work = [(2, 17) + coarse, (45,) + coarse]

    def windows(owned, beside, beyond, mine, iteration):
        sections = links.sections(links.stack(mine, beside, beyond))
        body, total = pack_kernel(ITEMS[iteration], ROWS[iteration])
        (parcels,) = links.call(
            body, (owned, beside, beyond, sections), [(CHIPS, 16 * total, 128)], name="hand_out"
        )
        parcels = links.block(parcels)
        return owned, beside, beyond, sections, parcels, links.swap_inner(parcels)

    sent = guess
    inner, inner_rest, outer, outer_rest, kept, initial, coeff, guess = links.call(
        first_kernel, (initial, coeff, guess),
        [(104, 128)] * 4 + [(4,) + coarse, slab, slab, slab], [(256, 128)], name="first", first=True,
    )
    inner, inner_rest, outer, outer_rest, received = links.together(
        links.swap_inner(inner), links.swap_inner(inner_rest), links.swap_outer(outer), links.swap_outer(outer_rest),
        links.onward(sent, 1),
    )
    owned, beside, beyond, mine, started, begin = links.call(
        complete_first, (inner, inner_rest, outer, outer_rest, kept, initial, received),
        [(208, 128), (144, 128), (144, 128), (16, 128), (8,) + coarse, slab], [(320, 128)], name="complete_first",
    )
    beside, beyond, earlier = links.together(
        links.swap_block(beside, True), links.swap_block(beyond, False), links.onward(sent, 2)
    )
    middle, end, ends, begin_next, kept, owned, mine, coefs = links.call(
        finish_first,
        (*windows(owned, beside, beyond, mine, 0), started, kept, inner, inner_rest, outer, outer_rest, initial,
         coeff, guess, begin, earlier),
        [slab, slab, (4, 64, 128), slab, (5,) + coarse, (48, 128), (16, 128), (15,) + coarse],
        work + [(576, 128)],
        name="finish_first",
    )
    beyond, beside = links.together(links.swap_block(owned, False), links.swap_block(owned, True))
    fine, coarse_end = links.call(
        finish_second,
        (*windows(owned, beside, beyond, mine, 1), started, kept, ends, coeff, begin, middle, end, begin_next, coefs),
        [(2, 2, 64, 128), (32, 64)],
        work + [(448, 128)],
        name="finish_second",
        last=True,
    )
    return fine, coarse_end


def on_device(initial, coeff, guess):
    fine, coarse_end = iterate(Links, initial, coeff, guess[0])
    return fine[None], coarse_end[None, None]


def solution(mesh):
    split = Mesh(
        mesh.devices.reshape(mesh.shape["tm"], mesh.shape["space"] // BLOCK, CHIPS, 2), ("tm", "block", "chip", "core")
    )
    space = ("block", "chip", "core")
    return jax.shard_map(
        on_device,
        mesh=split,
        in_specs=(P(space, None, None), P(space, None, None), P("tm", space, None, None)),
        out_specs=(P("tm", None, space, None, None), P("tm", space, None, None)),
        check_vma=False,
    )
```

```python
import jax
import jax.numpy as jnp
from jax import lax
from jax.experimental import pallas as pl
from jax.experimental.pallas import tpu as pltpu
from jax.sharding import Mesh, PartitionSpec as P

STEP = 0.06
QUAD = ((0.0, 0.0, 0.0), (5.0 / 24.0, 1.0 / 3.0, -1.0 / 24.0), (1.0 / 6.0, 2.0 / 3.0, 1.0 / 6.0))
ROWSUM = tuple(sum(row) for row in QUAD)
START = tuple(STEP * (row[1] * QUAD[1][0] + row[2] * QUAD[2][0]) for row in QUAD)
SECTIONS = 8
BLOCK = 8
CHIPS = BLOCK // 2
F32 = jnp.float32

COEF, NEAR1, NEAR2, BEGIN, INITIAL, EDGE = 10, 11, 12, 13, 14, 15
ITEMS = (
    ((0, 8), (1, 7), (COEF, 7), (2, 6), (3, 5), (4, 4), (5, 3), (6, 2), (BEGIN, 2), (INITIAL, 2), (7, 1),
     (NEAR1, 1))
    + tuple((EDGE + i, 1) for i in range(4)),
    ((0, 8), (1, 7), (2, 6), (3, 5), (4, 4), (5, 3), (6, 2), (NEAR1, 1), (NEAR2, 1)),
)
ROWS = ({NEAR1: 16, COEF: 32, BEGIN: 48, INITIAL: 64, **{EDGE + i: 80 + 16 * i for i in range(4)}}, {NEAR1: 16, NEAR2: 32})


def count(items, distance):
    return sum(1 for _, reach in items if reach >= distance)


def shares(core, ahead):
    if ahead == 0:
        return (0, 1), (2 - core, BLOCK - 1)
    if ahead > 0:
        return (0, 2 * ahead - core), (2, BLOCK - 1 - 2 * ahead + core)
    return (0, -2 * ahead + core - 1), (1, BLOCK + 2 * ahead - core)


def slots(items):
    return max(sum(count(items, least) for _, least in shares(core, a)) for core in (0, 1) for a in range(-3, 4))


def turn(x, by, axis):
    return pltpu.roll(x, by % x.shape[axis], axis)


def around(x):
    return turn(x, 1, 0) + turn(x, -1, 0) + turn(x, 1, 1) + turn(x, -1, 1)


def cubic(u):
    return u - u * u * u


def dot(a, b):
    b = b.astype(jnp.bfloat16)
    total, rest = None, a
    for _ in range(3):
        part = rest.astype(jnp.bfloat16)
        rest = rest - part.astype(F32)
        product = jnp.dot(part, b, preferred_element_type=F32)
        total = product if total is None else total + product
    return total


def pair_lanes():
    z = lax.broadcasted_iota(jnp.int32, (128, 128), 0)
    c = lax.broadcasted_iota(jnp.int32, (128, 128), 1)
    return jnp.where((z >> 1) == (c & 63), 1.0, 0.0).astype(F32)


def spread_lanes():
    c = lax.broadcasted_iota(jnp.int32, (128, 128), 0)
    z = lax.broadcasted_iota(jnp.int32, (128, 128), 1)
    return jnp.where((z >> 1) == c, 1.0, 0.0).astype(F32)


def squash(planes, scratch):
    for i, plane in enumerate(planes):
        scratch[64 * i : 64 * i + 64, :] = plane
    both = scratch[pl.ds(0, 32 * len(planes), 2), :] + scratch[pl.ds(1, 32 * len(planes), 2), :]
    sums = dot(both, pair_lanes())
    return [sums[32 * i : 32 * i + 32] for i in range(len(planes))]


def spread(planes, scratch):
    wide = dot(jnp.concatenate(planes, axis=0), spread_lanes())
    scratch[pl.ds(0, 32 * len(planes), 2), :] = wide
    scratch[pl.ds(1, 32 * len(planes), 2), :] = wide
    return [scratch[64 * i : 64 * i + 64, :] for i in range(len(planes))]


def left(shape):
    return lax.broadcasted_iota(jnp.int32, shape, 1) < 64


def pack(x):
    return jnp.where(left((16, 128)), x[:16], x[16:])


def unpack(t):
    other = turn(t, 64, 1)
    here = left((16, 128))
    return jnp.concatenate([jnp.where(here, t, other), jnp.where(here, other, t)], axis=0)


def coarse_slope(below, centre, above, coef):
    return 0.25 * (around(centre) + below + above - 6.0 * centre) + coef * cubic(centre)


def mix(row, nodes):
    return QUAD[row][0] * nodes[0] + QUAD[row][1] * nodes[1] + QUAD[row][2] * nodes[2]


def packets(spot, up, down, inners, outers):
    def put(to_inner, to_outer):
        for parts, outs in ((to_inner, inners), (to_outer, outers)):
            whole = jnp.concatenate(parts, axis=0)
            half = whole.shape[0] // 2
            outs[0][...] = whole[:half]
            outs[1][...] = whole[half:]

    @pl.when(spot[2] == 0)
    def _():
        put(up, down)

    @pl.when(spot[2] != 0)
    def _():
        put(down, up)


def sides(spot, inner, inner_rest, outer, outer_rest):
    a = jnp.concatenate([inner[...], inner_rest[...]], axis=0)
    b = jnp.concatenate([outer[...], outer_rest[...]], axis=0)
    low = jnp.full(a.shape, spot[2], jnp.int32) == 0
    return jnp.where(low, b, a), jnp.where(low, a, b)


def first_kernel(
    spot, initial, coeff, guess, inner, inner_rest, outer, outer_rest, keep, initial_out, coeff_out, guess_out, scratch
):
    for out, given in ((initial_out, initial), (coeff_out, coeff), (guess_out, guess)):
        out[...] = given[...]
    u = [guess[0], guess[1]]
    c = [coeff[0], coeff[1]]
    both = u[0] + u[1]
    total = around(both) - 5.0 * both + c[0] * cubic(u[0]) + c[1] * cubic(u[1])
    own, value, coef, start = squash([total, both, c[0] + c[1], initial[0] + initial[1]], scratch)
    value, coef, start = 0.125 * value, 0.125 * coef, 0.125 * start
    packets(spot, u + [c[1], pack(start)], u + [c[0], pack(start)], [inner, inner_rest], [outer, outer_rest])
    keep[0] = own
    keep[1] = value
    keep[2] = coef
    keep[3] = start


def own_k(own, value0, value0_sides, coef):
    slope = coarse_slope(value0_sides[0], value0, value0_sides[1], coef)
    return [(STEP / 8.0) * own[m] - (STEP * QUAD[m + 1][0]) * slope for m in (0, 1)]


def complete_first(
    spot, inner, inner_rest, outer, outer_rest, kept, initial, received, owned, beside, beyond, mine, keep, begin_out,
    scratch,
):
    below, above = sides(spot, inner, inner_rest, outer, outer_rest)
    begin = starting(spot, initial, received)
    own, value, coef, start = (kept[i] for i in range(4))
    low, high, value_low, value_high, value_begin = squash(
        [below[64:128, :], above[0:64, :], below[0:64, :] + below[64:128, :], above[0:64, :] + above[64:128, :],
         begin[0] + begin[1]],
        scratch,
    )
    value_low, value_high = 0.125 * value_low, 0.125 * value_high
    start_low, start_high = unpack(below[192:208, :]), unpack(above[192:208, :])
    start_slope = coarse_slope(start_low, start, start_high, coef)
    whole = own + low + high
    k = own_k([ROWSUM[1] * whole, ROWSUM[2] * whole], value, [value_low, value_high], coef)
    first = jnp.full((32, 128), spot[0], jnp.int32) == 0
    given = [pack(k[m - 1] + jnp.where(first, start + (STEP * QUAD[m][0]) * start_slope, 0.0)) for m in (2, 1)]
    given += [pack(coef), pack(0.125 * value_begin), pack(start)]
    mine[...] = given[0]
    odd = jnp.full((64, 128), spot[3], jnp.int32) == 1
    for i, part in enumerate(given):
        for out in (owned, beside, beyond):
            out[16 * i : 16 * i + 16, :] = part
    beside[80:144, :] = jnp.where(odd, begin[0], begin[1])
    beyond[80:144, :] = jnp.where(odd, begin[1], begin[0])
    for x in (0, 1):
        owned[80 + 64 * x : 144 + 64 * x, :] = begin[x]
        begin_out[x] = begin[x]
    for i, part in enumerate([k[0], k[1], start, start_slope, start_low, start_high, value_low, value_high]):
        keep[i] = part


def plane(spot, rows, owned, beside, beyond, sections, side, item, up=False):
    odd = spot[3]
    if item < SECTIONS:
        if side == 0:
            return sections[item, 0:16, :]
        at = jnp.where(odd == 1, side, 3 - side)
        return sections[item, pl.ds(pl.multiple_of(16 * at, 16), 16), :]
    row = rows[item]
    if side == 0:
        row += 64 if item >= EDGE and up else 0
        return owned[row : row + 16, :]
    near, far = beside[row : row + 16, :], beyond[row : row + 16, :]
    picked = jnp.full((16, 128), odd, jnp.int32) == (1 if side == 1 else 0)
    return jnp.where(picked, near, far)


def pack_kernel(items, rows):
    total = slots(items)

    def body(spot, owned, beside, beyond, sections, out):
        chip, core = spot[1], spot[2]

        def fill(own_core, away):
            slot = 0
            up = away > 0 or (away == 0 and own_core == 0)
            for side, least in shares(own_core, away):
                for item, reach in items:
                    if reach >= least:
                        part = plane(spot, rows, owned, beside, beyond, sections, side, item, up)
                        out[chip + away, 16 * slot : 16 * slot + 16, :] = part
                        slot += 1

        for own_core in (0, 1):
            for away in range(1 - CHIPS, CHIPS):
                there = jnp.logical_and(chip + away >= 0, chip + away < CHIPS)

                @pl.when(jnp.logical_and(core == own_core, there))
                def _():
                    fill(own_core, away)

    return body, total


def sweep(spot, items, rows, owned, beside, beyond, sections, windows, swapped, coefs, started, line, history):
    core = spot[2]
    place = 2 * spot[1] + core
    rank = {item: i for i, (item, _) in enumerate(items)}
    reach_of = dict(items)

    def fetch(item, w, whole=False):
        if w in (0, -BLOCK, BLOCK):
            side = {0: 0, -BLOCK: 1, BLOCK: 2}[w]
            return unpack(plane(spot, rows, owned, beside, beyond, sections, side, item))
        at = place + w
        if w > 0:
            outside, least = at >= BLOCK, [max(1, BLOCK - w - i) for i in (0, 1)]
        else:
            outside, least = at < 0, [max(1, BLOCK - 1 + w + i) for i in (0, 1)]
        before = jnp.where(core == 0, count(items, least[0]), count(items, least[1]))
        slot = rank[item] + jnp.where(outside, before, 0)
        source = windows if w % 2 == 0 else swapped
        found = source[(at & (BLOCK - 1)) >> 1, pl.ds(pl.multiple_of(16 * slot, 16), 16), :]
        return found if whole else unpack(found)

    if COEF in rank:
        for w in range(-7, 8):
            coefs[w + 7] = fetch(COEF, w)
    outermost = [fetch(INITIAL, w) if INITIAL in rank else jnp.zeros((32, 128), F32) for w in (-2, 2)]
    history[0] = outermost[0]
    history[1] = started[4]
    history[2] = started[2]
    history[3] = started[5]
    history[4] = outermost[1]
    for w in range(-8, 9):
        value = fetch(0, w)
        line[0, w + 8] = value
        if abs(w) <= 2:
            history[5 + w + 2] = value
    for k in range(1, SECTIONS):
        if k not in rank:
            continue
        old, new = (k - 1) % 2, k % 2
        for w in range(-reach_of[k], reach_of[k] + 1):
            centre = line[old, w + 8]
            slope = coarse_slope(line[old, w + 7], centre, line[old, w + 9], coefs[w + 7])
            value = centre + (STEP * QUAD[2][0]) * slope + fetch(k, w)
            line[new, w + 8] = value
            if abs(w) <= 2:
                history[5 * (k + 1) + w + 2] = value
    return fetch


def correct(spot, fetch, coefs, started, history, kept, values, nodes, below, above, coeff, begin, scratch):
    section = spot[0]
    s = [history[5 * section + i] for i in range(5)]
    slope = [coarse_slope(s[i], s[i + 1], s[i + 2], coefs[6 + i]) for i in range(3)]
    later = jnp.full((32, 128), section, jnp.int32) > 0
    edges = []
    for w, i in ((-1, 0), (1, 2)):
        for m, near in ((1, NEAR1), (2, NEAR2)):
            edges.append(fetch(near, w) + jnp.where(later, ROWSUM[m] * s[i + 1] + START[m] * slope[i], 0.0))
    coarse = [s[2]] + [s[2] + (STEP * QUAD[m][0]) * slope[1] + kept[m - 1] for m in (1, 2)]
    wide = spread([coarse[j] - values[j] for j in range(3)] + edges, scratch)
    fixed = [[nodes[j][x] + wide[j] for x in (0, 1)] for j in range(3)]
    rates = [[cubic(fixed[j][x]) for x in (0, 1)] for j in range(3)]
    fresh = []
    for m in (1, 2):
        sums = [mix(m, [fixed[j][x] for j in range(3)]) for x in (0, 1)]
        ends = [below[m - 1] + wide[2 + m], above[m - 1] + wide[4 + m]]
        fresh.append([])
        for x in (0, 1):
            change = around(sums[x]) - 6.0 * sums[x] + sums[1 - x] + ends[x]
            change = change + coeff[x] * mix(m, [rates[j][x] for j in range(3)])
            fresh[-1].append(begin[x] + STEP * change)
    return coarse[2], fresh


def starting(spot, initial, received):
    first = jnp.full((64, 128), spot[0], jnp.int32) == 0
    return [jnp.where(first, initial[x], received[x]) for x in (0, 1)]


def previous_end(section, fetch, coefs, history, starts, coeff, initial, earlier, scratch):
    before = jnp.maximum(section - 1, 0)
    s = [history[5 * before + i] for i in range(5)]
    value = [fetch(BEGIN, w) for w in range(-2, 3)]
    shift = []
    for i in range(3):
        two = history[5 * section + 1 + i]
        slope = coarse_slope(s[i], s[i + 1], s[i + 2], coefs[6 + i])
        slope = slope - coarse_slope(value[i], value[i + 1], value[i + 2], coefs[6 + i])
        one = 0.5 * (s[i + 1] + two) + (STEP * (QUAD[1][0] - 0.5 * QUAD[2][0])) * slope
        shift.append([s[i + 1] - value[i + 1], one - value[i + 1], two - value[i + 1]])
    wide = spread([mix(2, shift[0])] + shift[1] + [mix(2, shift[2])], scratch)
    fixed = [[starts[x] + wide[1 + j] for j in range(3)] for x in (1, 2)]
    sums = [ROWSUM[2] * starts[0] + wide[0], mix(2, fixed[0]), mix(2, fixed[1]), ROWSUM[2] * starts[3] + wide[4]]
    number = jnp.full((64, 128), section, jnp.int32)
    out = []
    for x in (0, 1):
        change = around(sums[x + 1]) - 6.0 * sums[x + 1] + sums[x] + sums[x + 2]
        change = change + coeff[x] * mix(2, [cubic(part) for part in fixed[x]])
        end = jnp.where(number == 1, initial[x], earlier[x]) + STEP * change
        out.append(jnp.where(number == 0, initial[x], end))
    return out


def finish_first(
    spot, owned, beside, beyond, sections, windows, swapped, started, kept, inner, inner_rest, outer, outer_rest,
    initial, coeff, guess, begin, earlier, middle_out, end_out, ends, begin_out, keep, owned_out, mine, coefs, line, history, scratch,
):
    fetch = sweep(
        spot, ITEMS[0], ROWS[0], owned, beside, beyond, sections, windows, swapped, coefs, started, line, history
    )
    below, above = sides(spot, inner, inner_rest, outer, outer_rest)
    section = spot[0]
    later = jnp.full((32, 128), section, jnp.int32) > 0
    s = [history[5 * section + i] for i in range(5)]
    slope = [coarse_slope(s[i], s[i + 1], s[i + 2], coefs[6 + i]) for i in range(3)]
    step = [s[i + 1] + (STEP * QUAD[1][0]) * slope[i] for i in range(3)]
    value = [started[6], kept[1], started[7]]
    coarse = []
    for i in range(3):
        if i == 1:
            one, two = step[1] + started[0], s[2] + (STEP * QUAD[2][0]) * slope[1] + started[1]
        else:
            one = fetch(NEAR1, i - 1) + jnp.where(later, step[i], 0.0)
            two = history[5 * section + 6 + i]
        coarse += [s[i + 1] - value[i], one - value[i], two - value[i]]
    wide = spread(coarse, scratch)
    u = [below[0:64, :], below[64:128, :], guess[0], guess[1], above[0:64, :], above[64:128, :]]
    c = [None, below[128:192, :], coeff[0], coeff[1], above[128:192, :], None]
    b = [None] + [None] * 4 + [None]
    b[2], b[3] = begin[0], begin[1]
    for x, w in ((1, -1), (4, 1)):
        b[x] = jnp.concatenate([fetch(EDGE + i, w, whole=True) for i in range(4)], axis=0)
    begin_next = previous_end(section, fetch, coefs, history, b[1:5], coeff, initial, earlier, scratch)
    for x in (0, 1):
        begin_out[x] = begin_next[x]
    fixed = [[u[x] + wide[3 * (x // 2) + j] for j in range(3)] for x in range(6)]
    nodes = [None] + [[b[x]] for x in range(1, 5)] + [None]
    rates = [None] + [[cubic(fixed[x][j]) for j in range(3)] for x in range(1, 5)] + [None]
    for m in (1, 2):
        sums = [mix(m, fixed[x]) for x in range(6)]
        for x in range(1, 5):
            change = around(sums[x]) - 6.0 * sums[x] + sums[x - 1] + sums[x + 1] + c[x] * mix(m, rates[x])
            nodes[x].append(b[x] + STEP * change)
    for x in (0, 1):
        middle_out[x] = nodes[x + 2][1]
        end_out[x] = nodes[x + 2][2]
    rates = [[cubic(nodes[x][j]) for j in range(3)] for x in (2, 3)]
    planes = []
    for m in (1, 2):
        sums = [mix(m, nodes[x]) for x in range(1, 5)]
        ends[m - 1] = sums[0]
        ends[m + 1] = sums[3]
        both = sums[1] + sums[2]
        planes.append(
            around(both) - 5.0 * both + sums[0] + sums[3] + c[2] * mix(m, rates[0]) + c[3] * mix(m, rates[1])
        )
    for j in range(3):
        planes.append(nodes[2][j] + nodes[3][j])
    small = squash(planes, scratch)
    values = [0.125 * small[2 + j] for j in range(3)]
    k = own_k(small[:2], values[0], [fetch(BEGIN, -1), fetch(BEGIN, 1)], kept[2])
    first = jnp.logical_not(later)
    ours = pack(k[1] + jnp.where(first, started[2] + (STEP * QUAD[2][0]) * started[3], 0.0))
    owned_out[0:16, :] = ours
    mine[...] = ours
    for m in (1, 2):
        near = QUAD[m][1] * k[0] + QUAD[m][2] * k[1] - mix(m, values)
        near = near + jnp.where(first, ROWSUM[m] * started[2] + START[m] * started[3], 0.0)
        owned_out[16 * m : 16 * m + 16, :] = pack(near)
    for i, part in enumerate(values + k):
        keep[i] = part


def finish_second(
    spot, owned, beside, beyond, sections, windows, swapped, started, kept, ends, coeff, begin_in, middle_in, end_in,
    begin, coefs, fresh_out, coarse_out, line, history, scratch,
):
    fetch = sweep(
        spot, ITEMS[1], ROWS[1], owned, beside, beyond, sections, windows, swapped, coefs, started, line, history
    )
    nodes = [[part[0], part[1]] for part in (begin_in, middle_in, end_in)]
    end, fresh = correct(
        spot, fetch, coefs, started, history, (kept[3], kept[4]), [kept[0], kept[1], kept[2]], nodes,
        [ends[0], ends[1]], [ends[2], ends[3]], [coeff[0], coeff[1]], [begin[0], begin[1]], scratch,
    )
    for m in (0, 1):
        for x in (0, 1):
            fresh_out[m, x] = fresh[m][x]
    coarse_out[...] = end[:, :64]


def run(body, args, outs, scratch=(), name=None, first=False, last=False):
    def placed(*refs):
        spot = [lax.axis_index(a) for a in ("tm", "chip", "core", "block")]
        body(spot[:3] + [spot[3] & 1], *refs)

    return pl.pallas_call(
        placed,
        out_shape=[jax.ShapeDtypeStruct(shape, F32) if last else pltpu.VMEM(shape, F32) for shape in outs],
        in_specs=[pl.BlockSpec(memory_space=pltpu.VMEM)] * len(args),
        out_specs=[pl.BlockSpec(memory_space=pltpu.VMEM)] * len(outs),
        scratch_shapes=[pltpu.VMEM(shape, F32) for shape in scratch],
        compiler_params=None if first else pltpu.CompilerParams(vmem_limit_bytes=16 << 20),
        name=name,
    )(*(a if first else pltpu.with_memory_space_constraint(a, pltpu.VMEM) for a in args))


class Links:
    call = staticmethod(run)

    @staticmethod
    def swap_block(x, row):
        n = lax.axis_size("block")
        pairs = [(i, i ^ 1 if row else (i + 2 * (i % 2) - 1) % n) for i in range(n)]
        return lax.ppermute(x, "block", pairs)

    @staticmethod
    def swap_inner(x):
        return lax.ppermute(x, "core", [(0, 1), (1, 0)])

    @staticmethod
    def swap_outer(x):
        n = lax.axis_size("block") * BLOCK
        return lax.ppermute(x, ("block", "chip", "core"), [(i, (i + 2 * (i % 2) - 1) % n) for i in range(n)])

    @staticmethod
    def onward(x, by):
        n = lax.axis_size("tm")
        return lax.ppermute(x, "tm", [(i, i + by) for i in range(n - by)])

    @staticmethod
    def sections(x):
        return lax.all_to_all(jnp.broadcast_to(x, (SECTIONS,) + x.shape), "tm", 0, 0)

    @staticmethod
    def block(x):
        return lax.all_to_all(x, "chip", 0, 0)

    @staticmethod
    def together(*values):
        return lax.optimization_barrier(values)

    @staticmethod
    def stack(*planes):
        return jnp.concatenate([p[:16] for p in planes], axis=0)


def iterate(links, initial, coeff, guess):
    coarse, slab = (32, 128), (2, 64, 128)
    work = [(2, 17) + coarse, (45,) + coarse]

    def windows(owned, beside, beyond, mine, iteration):
        sections = links.sections(links.stack(mine, beside, beyond))
        body, total = pack_kernel(ITEMS[iteration], ROWS[iteration])
        (parcels,) = links.call(
            body, (owned, beside, beyond, sections), [(CHIPS, 16 * total, 128)], name="hand_out"
        )
        parcels = links.block(parcels)
        return owned, beside, beyond, sections, parcels, links.swap_inner(parcels)

    sent = guess
    inner, inner_rest, outer, outer_rest, kept, initial, coeff, guess = links.call(
        first_kernel, (initial, coeff, guess),
        [(104, 128)] * 4 + [(4,) + coarse, slab, slab, slab], [(256, 128)], name="first", first=True,
    )
    outer, inner, outer_rest, inner_rest, received = links.together(
        links.swap_outer(outer), links.swap_inner(inner), links.swap_outer(outer_rest), links.swap_inner(inner_rest),
        links.onward(sent, 1),
    )
    owned, beside, beyond, mine, started, begin = links.call(
        complete_first, (inner, inner_rest, outer, outer_rest, kept, initial, received),
        [(208, 128), (144, 128), (144, 128), (16, 128), (8,) + coarse, slab], [(320, 128)], name="complete_first",
    )
    beside, beyond, earlier = links.together(
        links.swap_block(beside, True), links.swap_block(beyond, False), links.onward(sent, 2)
    )
    middle, end, ends, begin_next, kept, owned, mine, coefs = links.call(
        finish_first,
        (*windows(owned, beside, beyond, mine, 0), started, kept, inner, inner_rest, outer, outer_rest, initial,
         coeff, guess, begin, earlier),
        [slab, slab, (4, 64, 128), slab, (5,) + coarse, (48, 128), (16, 128), (15,) + coarse],
        work + [(576, 128)],
        name="finish_first",
    )
    beyond, beside = links.together(links.swap_block(owned, False), links.swap_block(owned, True))
    fine, coarse_end = links.call(
        finish_second,
        (*windows(owned, beside, beyond, mine, 1), started, kept, ends, coeff, begin, middle, end, begin_next, coefs),
        [(2, 2, 64, 128), (32, 64)],
        work + [(448, 128)],
        name="finish_second",
        last=True,
    )
    return fine, coarse_end


def on_device(initial, coeff, guess):
    fine, coarse_end = iterate(Links, initial, coeff, guess[0])
    return fine[None], coarse_end[None, None]


def solution(mesh):
    split = Mesh(
        mesh.devices.reshape(mesh.shape["tm"], mesh.shape["space"] // BLOCK, CHIPS, 2), ("tm", "block", "chip", "core")
    )
    space = ("block", "chip", "core")
    return jax.shard_map(
        on_device,
        mesh=split,
        in_specs=(P(space, None, None), P(space, None, None), P("tm", space, None, None)),
        out_specs=(P("tm", None, space, None, None), P("tm", space, None, None)),
        check_vma=False,
    )
```
